32 devices in a mesh: dp: 8 (over y, x, core), tensor: 4 (over z).
Axes of the slice: x: 2, y: 2, z: 4, core: 2. Of those that a mesh axis runs over, the one named last changes fastest.
Arguments:
- tokens: bfloat16 [2, 8192, 1024], P(None, ('dp', 'tensor')), may hold values from -6 to 6
- attn_gain: float32 [1024], replicated, may hold values from 0.25 to 1.75
- ffn_gain: float32 [1024], replicated, may hold values from 0.25 to 1.75
- query_weight: bfloat16 [1024, 1024], P(None, 'tensor'), may hold values from -0.1875 to 0.1875
- key_weight: bfloat16 [1024, 1024], P(None, 'tensor'), may hold values from -0.1875 to 0.1875
- value_weight: bfloat16 [1024, 1024], P(None, 'tensor'), may hold values from -0.1875 to 0.1875
- out_weight: bfloat16 [1024, 1024], P('tensor'), may hold values from -1 to 1
- gate_weight: bfloat16 [1024, 2816], P(None, 'tensor'), may hold values from -0.1875 to 0.1875
- up_weight: bfloat16 [1024, 2816], P(None, 'tensor'), may hold values from -0.1875 to 0.1875
- down_weight: bfloat16 [2816, 1024], P('tensor'), may hold values from -0.109375 to 0.109375
- cache_keys: bfloat16 [2, 2048, 1024], P(None, 'dp', 'tensor'), may hold values from -6 to 6
- cache_values: bfloat16 [2, 2048, 1024], P(None, 'dp', 'tensor'), may hold values from -6 to 6
- knn_index: int32 [2, 32, 8, 128], P(None, 'dp', 'tensor'), may hold values from 0 to 511, all different within a row
- cotangent: bfloat16 [2, 8192, 1024], P(None, ('dp', 'tensor')), may hold values from -6 to 6
Outputs:
- output: bfloat16 [2, 8192, 1024], P(None, ('dp', 'tensor'))
- grad_tokens: bfloat16 [2, 8192, 1024], P(None, ('dp', 'tensor'))
- grad_query: float32 [1024, 1024], P(None, 'tensor')
- grad_key: float32 [1024, 1024], P(None, 'tensor')
- grad_value: float32 [1024, 1024], P(None, 'tensor')
- grad_outproj: float32 [1024, 1024], P('tensor')
- grad_gate: float32 [1024, 2816], P(None, 'tensor')
- grad_up: float32 [1024, 2816], P(None, 'tensor')
- grad_down: float32 [2816, 1024], P('tensor')
- grad_attn_gain: float32 [1024], replicated
- grad_ffn_gain: float32 [1024], replicated
The draws below stay inside these ranges and needn't reach their ends.
Inputs may be any that keep to these rules, and one draw needn't show every extreme that they name: knn_index[m, s * 4 + b, h] lists 128 distinct candidate rows read in head h by the queries of block b of sequence s of micro-batch m; an entry e < 256 is row e of the sequence's own cache, an entry e >= 256 is row e - 256 of the cache of sequence s - 1 of the same micro-batch, sequence 0 taking sequence 8 - 1.
All inputs are finite; a program needn't handle non-finite values.
Results may differ from the reference program's by a relative error of at most 0.02.
Values may be sent and summed in bfloat16 or wider, within the bound.
A program may use at most 192 MiB of HBM per device.

```python
import jax
import jax.numpy as jnp
from jax import lax

D = 1024
HEADS = 8
HD = 128
FF = 2816
LEN = 1024
MICRO = 2
BLK = 256
TOPK = 128
CACHE = 256
QB = 512
NBLK = 4
ROWS = 8192
N_DP = 8


def shard_levels(key, extent, split, low, high):
    level, own = 1.0, jax.random.fold_in(key, 6)
    for dim, shards_of in split:
        heights = jnp.exp(jax.random.uniform(jax.random.fold_in(own, dim), (shards_of,), jnp.float32, low / len(split), high / len(split)))
        level = level * jnp.repeat(heights, extent[dim] // shards_of).reshape([-1 if axis == dim else 1 for axis in range(len(extent))])
    return level


def picks_of(own_key, rows, number_of, top, lift):
    sequence = jax.random.permutation(jax.random.fold_in(own_key, 1), number_of)
    boost = sequence
    for power in range(3):
        boost = boost * boost // number_of
    boost = boost * lift // number_of
    chance = jax.random.randint(jax.random.fold_in(own_key, 2), (rows, number_of), 0, 4096) + boost
    sure = jax.random.permutation(jax.random.fold_in(own_key, 3), rows)[jnp.arange(number_of) % rows]
    chance = jnp.where(jnp.arange(rows)[:, None] == sure[None, :], 1 << 14, chance)
    priority = chance * number_of + jnp.arange(number_of)
    return lax.top_k(priority.astype(jnp.int32), top)[1].astype(jnp.int32)


def noise(key, shape, deviation, reach, cuts=(), held_as=jnp.bfloat16):
    values = deviation * jax.random.normal(key, shape, jnp.float32)
    if cuts:
        values = values * shard_levels(key, shape, cuts, -0.22, 0.18)
    return jnp.clip(values, -reach, reach).astype(held_as)


def setup_inputs(seed: int = 0) -> dict:
    key_of = jax.random.split(jax.random.key(seed), 15)
    tokens = noise(key_of[0], (MICRO, ROWS, D), 1.0, 6.0, ((1, 32),))
    attn_gain = jnp.clip(1.0 + 0.15 * jax.random.normal(key_of[1], (D,), jnp.float32), 0.25, 1.75)
    ffn_gain = jnp.clip(1.0 + 0.15 * jax.random.normal(key_of[2], (D,), jnp.float32), 0.25, 1.75)
    query_weight = noise(key_of[3], (D, HEADS * HD), D ** -0.5, 0.1875, ((1, 4),))
    key_weight = noise(key_of[4], (D, HEADS * HD), D ** -0.5, 0.1875, ((1, 4),))
    value_weight = noise(key_of[5], (D, HEADS * HD), D ** -0.5, 0.1875, ((1, 4),))
    out_weight = noise(key_of[6], (HEADS * HD, D), (HEADS * HD // 32) ** -0.5, 1.0, ((0, 4),))
    gate_weight = noise(key_of[7], (D, FF), D ** -0.5, 0.1875, ((1, 4),))
    up_weight = noise(key_of[8], (D, FF), D ** -0.5, 0.1875, ((1, 4),))
    down_weight = noise(key_of[9], (FF, D), FF ** -0.5, 0.109375, ((0, 4),))
    cache_keys = noise(key_of[10], (MICRO, N_DP * CACHE, HEADS * HD), 1.0, 6.0, ((1, 8), (2, 4)))
    cache_values = noise(key_of[11], (MICRO, N_DP * CACHE, HEADS * HD), 1.0, 6.0, ((1, 8), (2, 4)))
    knn_index = picks_of(key_of[12], MICRO * (N_DP * NBLK) * HEADS, 2 * CACHE, TOPK, 0).reshape((MICRO, N_DP * NBLK, HEADS, TOPK))
    cotangent = noise(key_of[13], (MICRO, ROWS, D), 1.0, 6.0, ((1, 32),))
    return dict(tokens=tokens, attn_gain=attn_gain, ffn_gain=ffn_gain, query_weight=query_weight, key_weight=key_weight, value_weight=value_weight, out_weight=out_weight, gate_weight=gate_weight, up_weight=up_weight, down_weight=down_weight, cache_keys=cache_keys, cache_values=cache_values, knn_index=knn_index, cotangent=cotangent)


EPS = 1e-06
NEG = -1e+30
HIGH = lax.Precision.HIGHEST

@jax.custom_vjp
def low(v):
    return lax.optimization_barrier(v.astype(jnp.bfloat16)).astype(jnp.float32)

@jax.custom_vjp
def low_back(v):
    return v

def low_keep(v):
    return (low(v), None)

def low_pass(kept, grad):
    return (grad,)

def back_keep(v):
    return (v, None)

def back_low(kept, grad):
    return (low(grad),)
low.defvjp(low_keep, low_pass)
low_back.defvjp(back_keep, back_low)

def product(first_arg, second_arg):
    return jnp.dot(first_arg, second_arg, precision=HIGH, preferred_element_type=jnp.float32)

def row_scale(values):
    return lax.rsqrt(lax.optimization_barrier(jnp.mean(values * values, axis=-1, keepdims=True)) + EPS)

def attend_block(query_block, key_heads, value_heads, mem_keys, mem_values, first_row):
    sub_blocks = QB // BLK
    near_scores = jnp.einsum('qhd,khd->hqk', query_block, key_heads, precision=HIGH)
    near_scores = low_back(near_scores)
    row_ids = first_row + jnp.arange(QB)
    col_ids = jnp.arange(LEN)
    near_scores = jnp.where(col_ids[None, None, :] <= row_ids[None, :, None], near_scores, NEG)
    query_sub = query_block.reshape(sub_blocks, BLK, HEADS, HD)
    memory = jnp.einsum('sbhd,shtd->hsbt', query_sub, mem_keys, precision=HIGH).reshape(HEADS, QB, TOPK)
    memory = low_back(memory)
    top_score = jnp.maximum(lax.optimization_barrier(jnp.max(near_scores, axis=2, keepdims=True)), lax.optimization_barrier(jnp.max(memory, axis=2, keepdims=True)))
    near_exp = jnp.exp(near_scores - top_score)
    memory_exp = jnp.exp(memory - top_score)
    totals = lax.optimization_barrier(jnp.sum(near_exp, axis=2, keepdims=True)) + lax.optimization_barrier(jnp.sum(memory_exp, axis=2, keepdims=True))
    near_prob = low(near_exp / totals)
    memory_prob = low(memory_exp / totals)
    result = jnp.einsum('hqk,khd->qhd', near_prob, value_heads, precision=HIGH)
    memory_part = jnp.einsum('hsbt,shtd->sbhd', memory_prob.reshape(HEADS, sub_blocks, BLK, TOPK), mem_values, precision=HIGH)
    return result + memory_part.reshape(QB, HEADS, HD)

def sequence_block(inputs, cand_keys, cand_values, knn_rows, params):
    query_weight, key_weight, value_weight, out_weight, gate_weight, up_weight, down_weight, attn_gain, ffn_gain = params
    normed = low(inputs * row_scale(inputs) * attn_gain)
    queries = low(low_back(product(normed, query_weight)) * HD ** (-0.5))
    keys_all = low(low_back(product(normed, key_weight)))
    values_all = low(low_back(product(normed, value_weight)))
    head_pick = jnp.arange(HEADS)[None, :, None]
    key_table = jnp.transpose(cand_keys.reshape(2 * CACHE, HEADS, HD), (1, 0, 2))
    value_table = jnp.transpose(cand_values.reshape(2 * CACHE, HEADS, HD), (1, 0, 2))
    mem_keys = key_table[head_pick, knn_rows]
    mem_values = value_table[head_pick, knn_rows]
    blocks_count = LEN // QB
    sub_blocks = QB // BLK
    key_heads = keys_all.reshape(LEN, HEADS, HD)
    value_heads = values_all.reshape(LEN, HEADS, HD)

    def per_block(members):
        return attend_block(members[0], key_heads, value_heads, members[1], members[2], members[3])
    attended = lax.map(jax.checkpoint(per_block), (queries.reshape(blocks_count, QB, HEADS, HD), mem_keys.reshape(blocks_count, sub_blocks, HEADS, TOPK, HD), mem_values.reshape(blocks_count, sub_blocks, HEADS, TOPK, HD), jnp.arange(blocks_count) * QB))
    mixed = low(low_back(attended.reshape(LEN, HEADS * HD)))
    hidden = inputs + low_back(product(mixed, out_weight))
    normed_two = low(hidden * row_scale(hidden) * ffn_gain)
    gate_value = low_back(product(normed_two, gate_weight))
    up_value = low_back(product(normed_two, up_weight))
    activated = low(jax.nn.silu(gate_value) * up_value)
    return hidden + low_back(product(activated, down_weight))

def reference(tokens, attn_gain, ffn_gain, query_weight, key_weight, value_weight, out_weight, gate_weight, up_weight, down_weight, cache_keys, cache_values, knn_index, cotangent):
    seq_count = MICRO * N_DP
    params = tuple((member.astype(jnp.float32) for member in (query_weight, key_weight, value_weight, out_weight, gate_weight, up_weight, down_weight, attn_gain, ffn_gain)))
    inputs = tokens.astype(jnp.float32).reshape(seq_count, LEN, D)

    def candidates(cache):
        own_rows = cache.astype(jnp.float32).reshape(MICRO, N_DP, CACHE, HEADS * HD)
        joined = jnp.concatenate([own_rows, jnp.roll(own_rows, 1, axis=1)], axis=2)
        return joined.reshape(seq_count, 2 * CACHE, HEADS * HD)
    cand_keys = candidates(cache_keys)
    cand_values = candidates(cache_values)
    knn_rows = knn_index.reshape(seq_count, NBLK, HEADS, TOPK)

    def forward(sequences, weights):

        def per_sequence(members):
            return sequence_block(members[0], members[1], members[2], members[3], weights)
        return lax.map(jax.checkpoint(per_sequence), (sequences, cand_keys, cand_values, knn_rows))
    results, pullback = jax.vjp(forward, inputs, params)
    grad_inputs, grad_params = pullback(cotangent.astype(jnp.float32).reshape(seq_count, LEN, D))
    full_shape = (MICRO, N_DP * LEN, D)
    return (results.reshape(full_shape).astype(jnp.bfloat16), grad_inputs.reshape(full_shape).astype(jnp.bfloat16), grad_params[0], grad_params[1], grad_params[2], grad_params[3], grad_params[4], grad_params[5], grad_params[6], grad_params[7], grad_params[8])
```

```python
import functools

import jax
import jax.numpy as jnp
from jax import lax
from jax.experimental import pallas as pl
from jax.experimental.pallas import tpu as pltpu
from jax.sharding import Mesh
from jax.sharding import PartitionSpec as P

HEADS = 8
HD = 128
MICRO = 2
BLK = 256
TOPK = 128
CACHE = 256
D = 1024
NQ = 4
DP = D // NQ
HALF = 512
LEN = 1024
HID = 352
RA = 4 * HD
RB = 3 * HID

EPS = 1e-06
NEG = -1e30
BF = jnp.bfloat16
F32 = jnp.float32


def nn(a, b):
    return lax.dot_general(a, b, (((1,), (0,)), ((), ())), preferred_element_type=F32)


def nt(a, b):
    return lax.dot_general(a, b, (((1,), (1,)), ((), ())), preferred_element_type=F32)


def tn(a, b):
    return lax.dot_general(a, b, (((0,), (0,)), ((), ())), preferred_element_type=F32)


VM = pl.BlockSpec(memory_space=pltpu.VMEM)
SM = pl.BlockSpec(memory_space=pltpu.SMEM)


def call(body, outs, args, flops=0, trans=0, scratch=(), name=None, vmem=None):
    nbytes = sum(a.size * a.dtype.itemsize for a in args) + sum(
        jnp.dtype(t).itemsize * functools.reduce(lambda x, y: x * y, s, 1) for s, t in outs
    )
    return pl.pallas_call(
        body,
        out_shape=[jax.ShapeDtypeStruct(s, t) for s, t in outs],
        in_specs=[SM if i == 0 else VM for i in range(len(args))],
        out_specs=[VM for _ in outs],
        scratch_shapes=list(scratch),
        name=name,
        compiler_params=pltpu.CompilerParams(vmem_limit_bytes=vmem),
        cost_estimate=pl.CostEstimate(flops=int(flops), bytes_accessed=int(nbytes), transcendentals=int(trans)),
    )(*args)


def block(index, size):
    return pl.ds(pl.multiple_of(index * size, size), size)


def lanes(k):
    return slice(k * DP, (k + 1) * DP)


def prep_rows_body(ids, x, gains, s0, s1, rel_gains):
    q, t = ids[0], ids[2]
    for k in range(NQ):
        cols = block(q ^ k, DP)
        rel_gains[:, lanes(k)] = gains[:, cols]
        for r, out in ((0, s0), (1, s1)):
            out[:, lanes(k)] = x[(r + t) & 1, :, cols]


def unprep_rows_body(ids, b0, b1, out):
    q, t = ids[0], ids[2]
    for k in range(NQ):
        cols = block(q ^ k, DP)
        for r, src in ((0, b0), (1, b1)):
            out[(r + t) & 1, :, cols] = src[:, lanes(k)]


def prep_a_body(ids, wq, wk, wv, wo, out):
    q, c = ids[0], ids[1]
    for k in range(NQ):
        rows = block(q ^ k, DP)
        for i, w in enumerate((wq, wk, wv)):
            out[k, i * HD : (i + 1) * HD, :] = w[rows, block(c, HD)].T
        out[k, 3 * HD : 4 * HD, :] = wo[block(c, HD), rows]


def prep_b_body(ids, wg, wu, wd, out, turned):
    q, c = ids[0], ids[1]
    for k in range(NQ):
        rows = block(q ^ k, DP)
        for i, w in enumerate((wg, wu)):
            turned[...] = w[rows, :].T
            out[k, i * HID : (i + 1) * HID, :] = turned[pl.ds(pl.multiple_of(c * HID, 32), HID), :]
        out[k, 2 * HID : 3 * HID, :] = wd[pl.ds(pl.multiple_of(c * HID, 32), HID), rows]


def memory_body(ids, own, prev, knn, out):
    for m in range(MICRO):
        for h in range(2):
            cols = slice(h * HD, (h + 1) * HD)
            for b in range(LEN // BLK):
                picks = knn[m, b, h : h + 1, :]
                rows = lax.broadcasted_iota(jnp.int32, (CACHE, TOPK), 0)
                hot_own = jnp.where(rows == picks, 1.0, 0.0).astype(BF)
                hot_prev = jnp.where(rows + CACHE == picks, 1.0, 0.0).astype(BF)
                for kv in range(2):
                    got = tn(hot_own, own[kv, m, :, cols]) + tn(hot_prev, prev[kv, m, :, cols])
                    out[m, h, kv * 512 + b * TOPK : kv * 512 + (b + 1) * TOPK, :] = got.astype(BF)


def scale_of(x):
    return lax.rsqrt(jnp.mean(x * x, axis=-1, keepdims=True) + EPS)


def norm_one_body(ids, r0, r1, gains, x_own, n_own):
    t = ids[2]
    for r, src in ((0, r0), (1, r1)):
        rows = block((t & 1) ^ r, 256)
        raw = src[...]
        x = raw.astype(F32)
        x_own[rows, :] = raw
        n_own[rows, :] = (x * scale_of(x) * gains[0:1, :]).astype(BF)


def arrange_body(ids, r0, r1, own):
    t = ids[2]
    for r, src in ((0, r0), (1, r1)):
        own[block((t & 1) ^ r, 256), :] = src[...]


def norm_two_body(ids, x, o_own, o_got, gains, hidden, n_own):
    for i in range(2):
        rows = slice(i * 256, (i + 1) * 256)
        h = x[rows, :].astype(F32) + (o_own[rows, :] + o_got[rows, :].astype(F32))
        hidden[rows, :] = h
        n_own[rows, :] = (h * scale_of(h) * gains[1:2, :]).astype(BF)


def output_body(ids, hidden, y_own, y_got, s0, s1):
    t = ids[2]
    for r, out in ((0, s0), (1, s1)):
        rows = block((t & 1) ^ r, 256)
        out[...] = (hidden[rows, :] + (y_own[rows, :] + y_got[rows, :].astype(F32))).astype(BF)


def norm_back(grad, x, gain):
    scale = scale_of(x)
    scaled = grad * gain
    gain_part = jnp.sum(grad * x * scale, axis=0, keepdims=True)
    back = scale * scaled - x * (scale * scale * scale) * jnp.mean(scaled * x, axis=-1, keepdims=True)
    return back, gain_part


def put_gain(ids, out, total):
    q = ids[0]
    for k in range(NQ):
        out[:, block(q ^ k, DP)] = total[:, lanes(k)]


def norm_two_back_body(ids, d_own, d_got, cot, hidden, gains, grad_hidden, low, gain_out):
    total = jnp.zeros((1, D), F32)
    for i in range(2):
        rows = slice(i * 256, (i + 1) * 256)
        grad = d_own[rows, :] + d_got[rows, :].astype(F32)
        back, part = norm_back(grad, hidden[rows, :], gains[1:2, :])
        total = total + part
        g = cot[rows, :].astype(F32) + back
        grad_hidden[rows, :] = g
        low[rows, :] = g.astype(BF)
    put_gain(ids, gain_out, total)


def norm_one_back_body(ids, d_own, d_got, grad_hidden, x, gains, s0, s1, gain_out):
    t = ids[2]
    total = jnp.zeros((1, D), F32)
    for r, out in ((0, s0), (1, s1)):
        rows = block((t & 1) ^ r, 256)
        grad = d_own[rows, :] + d_got[rows, :].astype(F32)
        back, part = norm_back(grad, x[rows, :].astype(F32), gains[0:1, :])
        total = total + part
        out[...] = (grad_hidden[rows, :] + back).astype(BF)
    put_gain(ids, gain_out, total)


def causal():
    return lax.broadcasted_iota(jnp.int32, (BLK, BLK), 1) <= lax.broadcasted_iota(jnp.int32, (BLK, BLK), 0)


def attention_body(ids, n_own, n_oth, w0, w1, w2, w3, mem, qkv, att, lse):
    c = ids[1]
    w = jnp.concatenate([p[0 : 3 * HD, :] for p in (w0, w1, w2, w3)], axis=1)
    for who, n in ((c, n_own), (1 - c, n_oth)):
        acc = nt(n[...], w)
        rows = block(who, HALF)
        qkv[rows, 0:HD] = (acc[:, 0:HD] * (HD**-0.5)).astype(BF)
        qkv[rows, HD : 3 * HD] = acc[:, HD : 3 * HD].astype(BF)
    keep = causal()
    for b in range(LEN // BLK):
        rows = slice(b * BLK, (b + 1) * BLK)
        query = qkv[rows, 0:HD]
        diag = jnp.where(keep, nt(query, qkv[rows, HD : 2 * HD]), NEG)
        far = nt(query, mem[b * TOPK : (b + 1) * TOPK, :])
        top = jnp.maximum(jnp.max(diag, axis=1, keepdims=True), jnp.max(far, axis=1, keepdims=True))
        if b:
            past = nt(query, qkv[0 : b * BLK, HD : 2 * HD])
            top = jnp.maximum(top, jnp.max(past, axis=1, keepdims=True))
        diag = jnp.exp(diag - top)
        far = jnp.exp(far - top)
        total = jnp.sum(diag, axis=1, keepdims=True) + jnp.sum(far, axis=1, keepdims=True)
        if b:
            past = jnp.exp(past - top)
            total = total + jnp.sum(past, axis=1, keepdims=True)
        inverse = 1.0 / total
        out = nn((diag * inverse).astype(BF), qkv[rows, 2 * HD : 3 * HD])
        out = out + nn((far * inverse).astype(BF), mem[512 + b * TOPK : 512 + (b + 1) * TOPK, :])
        if b:
            out = out + nn((past * inverse).astype(BF), qkv[0 : b * BLK, 2 * HD : 3 * HD])
        att[rows, :] = out.astype(BF)
        lse[rows, :] = jnp.broadcast_to(top + jnp.log(total), (BLK, HD))


def out_proj_body(ids, a0, a1, a2, a3, *refs):
    c = ids[1]
    w, (o_own, o_oth) = refs[:16], refs[16:]
    weights = jnp.concatenate(
        [jnp.concatenate([w[4 * j + k][3 * HD : 4 * HD, :] for k in range(NQ)], axis=1) for j in range(4)], axis=0
    )
    for who, out in ((1 - c, o_oth), (c, o_own)):
        rows = block(who, HALF)
        a = jnp.concatenate([a[rows, :] for a in (a0, a1, a2, a3)], axis=1)
        out[...] = nn(a, weights).astype(out.dtype)


def attention_back_body(pieces, ids, g_own, g_oth, n_own, n_oth, w0, w1, w2, w3, qkv, att, lse, mem,
                        keep_out, send_out, dq_own, dq_oth, da, dk, dv, dall):
    c = ids[1]
    wo = jnp.concatenate([p[3 * HD : 4 * HD, :] for p in (w0, w1, w2, w3)], axis=1)
    grad_o = jnp.zeros((HD, D), F32)
    for who, g in ((c, g_own), (1 - c, g_oth)):
        rows = block(who, HALF)
        grads = g[...]
        da[rows, :] = nt(grads, wo).astype(BF)
        grad_o = grad_o + tn(att[rows, :], grads)
    keep = causal()
    for b in range(LEN // BLK):
        rows = slice(b * BLK, (b + 1) * BLK)
        query = qkv[rows, 0:HD]
        grad = da[rows, :]
        level = lse[rows, 0:1]
        mem_k = mem[b * TOPK : (b + 1) * TOPK, :]
        mem_v = mem[512 + b * TOPK : 512 + (b + 1) * TOPK, :]
        p_d = jnp.exp(jnp.where(keep, nt(query, qkv[rows, HD : 2 * HD]), NEG) - level)
        p_f = jnp.exp(nt(query, mem_k) - level)
        g_d = nt(grad, qkv[rows, 2 * HD : 3 * HD])
        g_f = nt(grad, mem_v)
        delta = jnp.sum(p_d * g_d, axis=1, keepdims=True) + jnp.sum(p_f * g_f, axis=1, keepdims=True)
        if b:
            past = slice(0, b * BLK)
            p_p = jnp.exp(nt(query, qkv[past, HD : 2 * HD]) - level)
            g_p = nt(grad, qkv[past, 2 * HD : 3 * HD])
            delta = delta + jnp.sum(p_p * g_p, axis=1, keepdims=True)
        s_d = (p_d * (g_d - delta)).astype(BF)
        s_f = (p_f * (g_f - delta)).astype(BF)
        dq = nn(s_d, qkv[rows, HD : 2 * HD]) + nn(s_f, mem_k)
        if b:
            s_p = (p_p * (g_p - delta)).astype(BF)
            dq = dq + nn(s_p, qkv[past, HD : 2 * HD])
            dk[past, :] = dk[past, :] + tn(s_p, query)
            dv[past, :] = dv[past, :] + tn(p_p.astype(BF), grad)
        dk[rows, :] = tn(s_d, query)
        dv[rows, :] = tn(p_d.astype(BF), grad)
        dall[rows, 0:HD] = (dq * (HD**-0.5)).astype(BF)
    dall[:, HD : 2 * HD] = dk[...].astype(BF)
    dall[:, 2 * HD : 3 * HD] = dv[...].astype(BF)
    grad_w = jnp.zeros((3 * HD, D), F32)
    for who, n, out in ((c, n_own, dq_own), (1 - c, n_oth, dq_oth)):
        part = dall[block(who, HALF), :]
        out[...] = part
        grad_w = grad_w + tn(part, n[...])
    for out, which in ((keep_out, pieces[:2]), (send_out, pieces[2:])):
        for slot, k in enumerate(which):
            out[slot, 0 : 3 * HD, :] = grad_w[:, lanes(k)].astype(BF)
            out[slot, 3 * HD : 4 * HD, :] = grad_o[:, lanes(k)].astype(BF)


def in_proj_back_body(ids, *refs):
    parts, w, (d_own, d_oth) = refs[:8], refs[8:24], refs[24:]
    weights = jnp.concatenate(
        [jnp.concatenate([w[4 * j + k][0 : 3 * HD, :] for k in range(NQ)], axis=1) for j in range(4)], axis=0
    )
    for side, out in ((1, d_oth), (0, d_own)):
        d = jnp.concatenate([parts[2 * j + side][...] for j in range(4)], axis=1)
        out[...] = nn(d, weights).astype(out.dtype)


def ffn_body(pieces, ids, n_own, n_oth, c_own, c_oth, w0, w1, w2, w3, keep_out, send_out, act, dgu, w):
    for k, p in enumerate((w0, w1, w2, w3)):
        w[:, lanes(k)] = p[...]
    for side, n, cot in ((0, n_own, c_own), (1, n_oth, c_oth)):
        for i in range(2):
            rows = slice(i * 256, (i + 1) * 256)
            cols = slice(side * HALF + i * 256, side * HALF + (i + 1) * 256)
            normed = n[rows, :]
            gate = nt(w[0:HID, :], normed)
            up = nt(w[HID : 2 * HID, :], normed)
            grad = nt(w[2 * HID : 3 * HID, :], cot[rows, :])
            sig = 1.0 / (1.0 + jnp.exp(-gate))
            silu = gate * sig
            act[:, cols] = (silu * up).astype(BF)
            dgu[0:HID, cols] = (grad * up * sig * (1.0 + gate * (1.0 - sig))).astype(BF)
            dgu[HID : 2 * HID, cols] = (grad * silu).astype(BF)
    for out, which in ((keep_out, pieces[:2]), (send_out, pieces[2:])):
        for slot, k in enumerate(which):
            g = nn(dgu[:, 0:HALF], n_own[:, lanes(k)]) + nn(dgu[:, HALF:LEN], n_oth[:, lanes(k)])
            out[slot, 0 : 2 * HID, :] = g.astype(BF)
            g = nn(act[:, 0:HALF], c_own[:, lanes(k)]) + nn(act[:, HALF:LEN], c_oth[:, lanes(k)])
            out[slot, 2 * HID : 3 * HID, :] = g.astype(BF)


def ffn_sum_body(lo, hi, ids, *refs):
    parts, w, (own, oth, acc) = refs[:4], refs[4:20], refs[20:]
    for side, out in ((1, oth), (0, own)):
        cols = slice(side * HALF, (side + 1) * HALF)
        for j in range(4):
            weights = jnp.concatenate([w[4 * j + k][lo:hi, :] for k in range(NQ)], axis=1)
            got = tn(parts[j][:, cols], weights)
            if j == 0:
                acc[...] = got
            elif j < 3:
                acc[...] = acc[...] + got
            else:
                out[...] = (acc[...] + got).astype(out.dtype)


def place_a_body(ids, *refs):
    q, c = ids[0], ids[1]
    own, oth, (gq, gk, gv, go) = refs[:4], refs[4:8], refs[8:]
    for k in range(NQ):
        rows = block(q ^ k, DP)
        for half, src in ((c, own[k]), (1 - c, oth[k])):
            for i, out in enumerate((gq, gk, gv)):
                out[rows, block(half, HD)] = src[i * HD : (i + 1) * HD, :].astype(F32).T
            go[block(half, HD), rows] = src[3 * HD : 4 * HD, :].astype(F32)


def place_b_body(ids, *refs):
    q, c = ids[0], ids[1]
    own, oth, (gg, gu, gd, joined) = refs[:4], refs[4:8], refs[8:]
    for k in range(NQ):
        rows = block(q ^ k, DP)
        for i, out in enumerate((gg, gu)):
            for half, src in ((c, own[k]), (1 - c, oth[k])):
                joined[pl.ds(pl.multiple_of(half * HID, 32), HID), :] = src[i * HID : (i + 1) * HID, :].astype(F32)
            out[rows, :] = joined[...].T
        for half, src in ((c, own[k]), (1 - c, oth[k])):
            gd[pl.ds(pl.multiple_of(half * HID, 32), HID), rows] = src[2 * HID : 3 * HID, :].astype(F32)


def send(value, axis, pairs):
    return lax.ppermute(value, axis, pairs)


def flip(value, axis, bits):
    count = lax.axis_size(axis)
    return send(value, axis, [(i, i ^ bits) for i in range(count)])


def row_pairs(r):
    return [
        (c * 4 + t, (t // 2) * 4 + 2 * c + (r + t) % 2)
        for c in range(2)
        for t in range(4)
    ]


def rows_to_sequences(s0, s1):
    return [send(s, ("c", "t"), row_pairs(r)) for r, s in ((0, s0), (1, s1))]


def rows_back(s0, s1):
    return [send(s, ("c", "t"), [(b, a) for a, b in row_pairs(r)]) for r, s in ((0, s0), (1, s1))]


def memory_pairs(k, i):
    pairs = []
    for c in range(2):
        for t in range(4):
            kind = k + 2 * (c ^ (t >> 1))
            pairs.append((c * 4 + t, (i ^ (kind >> 1)) * 4 + (t ^ kind)))
    return pairs


def gather_weights(own):
    table = [[own[k] for k in range(NQ)]]
    for j in range(1, 4):
        mine = flip(own[0], "t", j)
        by_x = flip(mine, "q", 1)
        by_y = flip(mine, "q", 2)
        if j == 1:
            far = flip(by_x, "q", 2)
        elif j == 2:
            far = flip(by_y, "q", 1)
        else:
            far = flip(mine, "q", 3)
        table.append([mine, by_x, by_y, far])
    return table


PIECES = ((0, 2, 1, 3), (0, 1, 2, 3), (0, 2, 1, 3), (0, 1, 2, 3))


def plane_sum(j, keep, out):
    first, second = (1, 2) if j % 2 == 0 else (2, 1)
    kept = (keep.astype(F32) + flip(out, "q", first).astype(F32)).astype(BF)
    return (kept[0].astype(F32) + flip(kept[1], "q", second).astype(F32)).astype(BF)


def column_sum(sums):
    total = sums[0].astype(F32)
    for j in range(1, 4):
        total = total + flip(sums[j], "t", j).astype(F32)
    if lax.axis_size("r") > 1:
        total = lax.psum(total, "r")
    return total.astype(BF)


def spread(total, odd):
    by_x = flip(total, "q", 1)
    by_y = flip(total, "q", 2)
    far = flip(by_x, "q", 2) if odd else flip(by_y, "q", 1)
    own = [total, by_x, by_y, far]
    return own, [flip(p, "c", 1) for p in own]


def per_device(tokens, attn_gain, ffn_gain, query_weight, key_weight, value_weight, out_weight, gate_weight,
               up_weight, down_weight, cache_keys, cache_values, knn_index, cotangent):
    q, c, t = lax.axis_index("q"), lax.axis_index("c"), lax.axis_index("t")
    ids = jnp.stack([q, c, t]).astype(jnp.int32)
    gains = jnp.stack([attn_gain, ffn_gain])
    rows16 = ((256, D), BF)
    half16, half32 = ((HALF, D), BF), ((HALF, D), F32)

    s0, s1, rel_gains = call(prep_rows_body, [rows16, rows16, ((2, D), F32)], (ids, tokens, gains), name="prep_tokens")
    x0, x1 = rows_to_sequences(s0, s1)
    (own_a,) = call(
        prep_a_body, [((NQ, RA, DP), BF)], (ids, query_weight, key_weight, value_weight, out_weight), name="prep_a"
    )
    wa = gather_weights(own_a)
    own_cache = jnp.stack((cache_keys, cache_values))
    count = lax.axis_size(("r", "q", "c"))
    prev_cache = send(own_cache, ("r", "q", "c"), [(i, (i + 1) % count) for i in range(count)])
    (picked,) = call(
        memory_body, [((MICRO, 2, 1024, HD), BF)], (ids, own_cache, prev_cache, knn_index),
        flops=2 * 32 * 2 * 256 * 128 * 128, name="memory",
    )
    got = {}
    for k in range(2):
        for i in range(2):
            mine = picked[(t & 1) ^ k, i ^ c ^ (t >> 1)]
            got[k, i] = send(mine, ("c", "t"), memory_pairs(k, i))
    mem = [jnp.where(c == 0, got[k & 1, k >> 1], got[k & 1, (k >> 1) ^ 1]) for k in range(4)]
    cs0, cs1, _ = call(prep_rows_body, [rows16, rows16, ((2, D), F32)], (ids, cotangent, gains), name="prep_cotangent")
    cx0, cx1 = rows_to_sequences(cs0, cs1)
    (own_b,) = call(
        prep_b_body, [((NQ, RB, DP), BF)], (ids, gate_weight, up_weight, down_weight),
        scratch=[pltpu.VMEM((2 * HID, DP), BF)], name="prep_b",
    )
    wb = gather_weights(own_b)

    x_own, n1_own = call(norm_one_body, [half16, half16], (ids, x0, x1, rel_gains), name="norm_one")
    n1_oth = flip(n1_own, "c", 1)
    (cot_own,) = call(arrange_body, [half16], (ids, cx0, cx1), name="arrange")
    cot_oth = flip(cot_own, "c", 1)

    heads = [
        call(
            attention_body, [((LEN, 3 * HD), BF), ((LEN, HD), BF), ((LEN, HD), F32)],
            (ids, n1_own, n1_oth, *wa[j], mem[j]),
            flops=2 * 1024 * 1024 * 384 + 4 * 128 * 786432, trans=786432, name="attention",
        )
        for j in range(4)
    ]
    flat_a = [p for row in wa for p in row]
    flat_b = [p for row in wb for p in row]
    o_own, o_oth = call(
        out_proj_body, [half32, half16], (ids, *[h[1] for h in heads], *flat_a), flops=2 * 1024 * 512 * 1024,
        name="out_proj",
    )
    o_got = flip(o_oth, "c", 1)
    hidden, n2_own = call(norm_two_body, [half32, half16], (ids, x_own, o_own, o_got, rel_gains), name="norm_two")
    n2_oth = flip(n2_own, "c", 1)

    chunks = [
        call(
            functools.partial(ffn_body, PIECES[j]),
            [((2, RB, DP), BF), ((2, RB, DP), BF), ((HID, LEN), BF), ((2 * HID, LEN), BF)],
            (ids, n2_own, n2_oth, cot_own, cot_oth, *wb[j]),
            flops=6 * 2 * 1024 * 1024 * HID, trans=1024 * HID,
            scratch=[pltpu.VMEM((RB, D), BF)], name="ffn",
        )
        for j in range(4)
    ]
    d2_own, d2_oth = call(
        functools.partial(ffn_sum_body, 0, 2 * HID), [half32, half16], (ids, *[ch[3] for ch in chunks], *flat_b),
        flops=2 * 1024 * 1024 * 8 * HID, scratch=[pltpu.VMEM((HALF, D), F32)], name="ffn_back",
    )
    d2_got = flip(d2_oth, "c", 1)
    y_own, y_oth = call(
        functools.partial(ffn_sum_body, 2 * HID, 3 * HID), [half32, half16], (ids, *[ch[2] for ch in chunks], *flat_b),
        flops=2 * 1024 * 1024 * 4 * HID, scratch=[pltpu.VMEM((HALF, D), F32)], name="ffn_out",
    )
    y_got = flip(y_oth, "c", 1)
    grad_hidden, low_own, gain_two = call(
        norm_two_back_body, [half32, half16, ((1, D), F32)], (ids, d2_own, d2_got, cot_own, hidden, rel_gains),
        name="norm_two_back",
    )
    low_oth = flip(low_own, "c", 1)
    os0, os1 = call(output_body, [rows16, rows16], (ids, hidden, y_own, y_got), name="output")
    ob0, ob1 = rows_back(os0, os1)
    (output,) = call(unprep_rows_body, [((MICRO, 256, D), BF)], (ids, ob0, ob1), name="unprep_output")

    sums_b = [plane_sum(j, ch[0], ch[1]) for j, ch in enumerate(chunks)]
    backs = [
        call(
            functools.partial(attention_back_body, PIECES[j]),
            [((2, RA, DP), BF), ((2, RA, DP), BF), ((HALF, 3 * HD), BF), ((HALF, 3 * HD), BF)],
            (ids, low_own, low_oth, n1_own, n1_oth, *wa[j], *heads[j], mem[j]),
            flops=2 * 1024 * 1024 * 640 + 10 * 128 * 786432, trans=786432,
            scratch=[
                pltpu.VMEM((LEN, HD), BF), pltpu.VMEM((LEN, HD), F32), pltpu.VMEM((LEN, HD), F32),
                pltpu.VMEM((LEN, 3 * HD), BF),
            ],
            name="attention_back",
        )
        for j in range(4)
    ]
    total_b = column_sum(sums_b)
    b_own, b_oth = spread(total_b, True)
    sums_a = [plane_sum(j, bk[0], bk[1]) for j, bk in enumerate(backs)]
    d1_own, d1_oth = call(
        in_proj_back_body, [half32, half16], (ids, *[p for bk in backs for p in bk[2:]], *flat_a),
        flops=2 * 1024 * 1024 * 1536, name="in_proj_back",
    )
    d1_got = flip(d1_oth, "c", 1)
    gs0, gs1, gain_one = call(
        norm_one_back_body, [rows16, rows16, ((1, D), F32)], (ids, d1_own, d1_got, grad_hidden, x_own, rel_gains),
        name="norm_one_back",
    )
    gb0, gb1 = rows_back(gs0, gs1)
    (grad_tokens,) = call(unprep_rows_body, [((MICRO, 256, D), BF)], (ids, gb0, gb1), name="unprep_grad")
    total_a = column_sum(sums_a)
    a_own, a_oth = spread(total_a, False)

    wide, tall = ((D, 2 * HID), F32), ((2 * HID, D), F32)
    gg, gu, gd = call(
        place_b_body, [wide, wide, tall], (ids, *b_own, *b_oth), scratch=[pltpu.VMEM((2 * HID, DP), F32)], name="place_b"
    )
    col, row = ((D, 2 * HD), F32), ((2 * HD, D), F32)
    gq, gk, gv, go = call(place_a_body, [col, col, col, row], (ids, *a_own, *a_oth), name="place_a")
    gain_sums = lax.psum(jnp.concatenate((gain_one, gain_two)), ("r", "q", "c", "t"))
    return output, grad_tokens, gq, gk, gv, go, gg, gu, gd, gain_sums[0], gain_sums[1]


def solution(mesh):
    n_dp, n_t = mesh.shape["dp"], mesh.shape["tensor"]
    fine = Mesh(mesh.devices.reshape(n_dp // 8, NQ, 2, n_t), ("r", "q", "c", "t"))
    dp = ("r", "q", "c")
    rows = P(None, dp + ("t",), None)
    placed = (
        rows, P(), P(), P(None, "t"), P(None, "t"), P(None, "t"), P("t", None), P(None, "t"), P(None, "t"),
        P("t", None), P(None, dp, "t"), P(None, dp, "t"), P(None, dp, "t", None), rows,
    )
    return jax.shard_map(
        per_device,
        mesh=fine,
        in_specs=placed,
        out_specs=(
            rows, rows, P(None, "t"), P(None, "t"), P(None, "t"), P("t", None), P(None, "t"), P(None, "t"),
            P("t", None), P(), P(),
        ),
        check_vma=False,
    )
```

```python
import functools

import jax
import jax.numpy as jnp
from jax import lax
from jax.experimental import pallas as pl
from jax.experimental.pallas import tpu as pltpu
from jax.sharding import Mesh
from jax.sharding import PartitionSpec as P

HEADS = 8
HD = 128
MICRO = 2
BLK = 256
TOPK = 128
CACHE = 256
D = 1024
NQ = 4
DP = D // NQ
HALF = 512
LEN = 1024
HID = 352
RA = 4 * HD
RB = 3 * HID

EPS = 1e-06
NEG = -1e30
BF = jnp.bfloat16
F32 = jnp.float32


def nn(a, b):
    return lax.dot_general(a, b, (((1,), (0,)), ((), ())), preferred_element_type=F32)


def nt(a, b):
    return lax.dot_general(a, b, (((1,), (1,)), ((), ())), preferred_element_type=F32)


def tn(a, b):
    return lax.dot_general(a, b, (((0,), (0,)), ((), ())), preferred_element_type=F32)


VM = pl.BlockSpec(memory_space=pltpu.VMEM)
SM = pl.BlockSpec(memory_space=pltpu.SMEM)


def call(body, outs, args, flops=0, trans=0, scratch=(), name=None, vmem=None):
    nbytes = sum(a.size * a.dtype.itemsize for a in args) + sum(
        jnp.dtype(t).itemsize * functools.reduce(lambda x, y: x * y, s, 1) for s, t in outs
    )
    return pl.pallas_call(
        body,
        out_shape=[jax.ShapeDtypeStruct(s, t) for s, t in outs],
        in_specs=[SM if i == 0 else VM for i in range(len(args))],
        out_specs=[VM for _ in outs],
        scratch_shapes=list(scratch),
        name=name,
        compiler_params=pltpu.CompilerParams(vmem_limit_bytes=vmem),
        cost_estimate=pl.CostEstimate(flops=int(flops), bytes_accessed=int(nbytes), transcendentals=int(trans)),
    )(*args)


def block(index, size):
    return pl.ds(pl.multiple_of(index * size, size), size)


def lanes(k):
    return slice(k * DP, (k + 1) * DP)


def unprep_rows_body(ids, b0, b1, out):
    q, t = ids[0], ids[2]
    for k in range(NQ):
        cols = block(q ^ k, DP)
        for r, src in ((0, b0), (1, b1)):
            out[(r + t) & 1, :, cols] = src[:, lanes(k)]


def scale_of(x):
    return lax.rsqrt(jnp.mean(x * x, axis=-1, keepdims=True) + EPS)


def own_b_body(ids, gate_t, up_t, down, out):
    q, c = ids[0], ids[1]
    for k in range(NQ):
        for i, w in enumerate((gate_t, up_t, down)):
            out[i * HID : (i + 1) * HID, lanes(k)] = w[pl.ds(pl.multiple_of(c * HID, 32), HID), block(q ^ k, DP)]


def rel_gain(ids, gain):
    return jnp.concatenate([gain[:, block(ids[0] ^ k, DP)] for k in range(NQ)], axis=1)


def output_body(ids, hidden, y_own, y_got, s0, s1):
    t = ids[2]
    for r, out in ((0, s0), (1, s1)):
        rows = block((t & 1) ^ r, 256)
        out[...] = (hidden[rows, :] + (y_own[rows, :] + y_got[rows, :].astype(F32))).astype(BF)


def norm_back(grad, x, gain):
    scale = scale_of(x)
    scaled = grad * gain
    gain_part = jnp.sum(grad * x * scale, axis=0, keepdims=True)
    back = scale * scaled - x * (scale * scale * scale) * jnp.mean(scaled * x, axis=-1, keepdims=True)
    return back, gain_part


def put_gain(ids, out, total):
    q = ids[0]
    for k in range(NQ):
        out[:, block(q ^ k, DP)] = total[:, lanes(k)]


def norm_two_back_body(ids, d_own, d_got, cot, hidden, gain, grad_hidden, low, gain_out):
    gain = rel_gain(ids, gain)
    total = jnp.zeros((1, D), F32)
    for i in range(2):
        rows = slice(i * 256, (i + 1) * 256)
        grad = d_own[rows, :] + d_got[rows, :].astype(F32)
        back, part = norm_back(grad, hidden[rows, :], gain)
        total = total + part
        g = cot[rows, :].astype(F32) + back
        grad_hidden[rows, :] = g
        low[rows, :] = g.astype(BF)
    put_gain(ids, gain_out, total)


def norm_one_back_body(ids, d_own, d_got, grad_hidden, x, gain, s0, s1, gain_out):
    gain = rel_gain(ids, gain)
    t = ids[2]
    total = jnp.zeros((1, D), F32)
    for r, out in ((0, s0), (1, s1)):
        rows = block((t & 1) ^ r, 256)
        grad = d_own[rows, :] + d_got[rows, :].astype(F32)
        back, part = norm_back(grad, x[rows, :].astype(F32), gain)
        total = total + part
        out[...] = (grad_hidden[rows, :] + back).astype(BF)
    put_gain(ids, gain_out, total)


def causal():
    return lax.broadcasted_iota(jnp.int32, (BLK, BLK), 1) <= lax.broadcasted_iota(jnp.int32, (BLK, BLK), 0)


def attention_back_body(j, pieces, ids, g_own, g_oth, n_own, n_oth, wa, qkv_all, att_all, lse_all, mem_all,
                        keep_out, send_out, dq_own, dq_oth, da, dk, dv, dall):
    c = ids[1]
    wo = wa[j, 3 * HD : 4 * HD, :]
    qkv, att, lse, mem = qkv_all.at[j], att_all.at[:, j * HD : (j + 1) * HD], lse_all.at[j], mem_all.at[j]
    grad_o = jnp.zeros((HD, D), F32)
    for who, g in ((c, g_own), (1 - c, g_oth)):
        rows = block(who, HALF)
        grads = g[...]
        da[rows, :] = nt(grads, wo).astype(BF)
        grad_o = grad_o + tn(att[rows, :], grads)
    keep = causal()
    for b in range(LEN // BLK):
        rows = slice(b * BLK, (b + 1) * BLK)
        query = qkv[rows, 0:HD]
        grad = da[rows, :]
        level = lse[rows, 0:1]
        mem_k = mem[b * TOPK : (b + 1) * TOPK, :]
        mem_v = mem[512 + b * TOPK : 512 + (b + 1) * TOPK, :]
        p_d = jnp.exp(jnp.where(keep, nt(query, qkv[rows, HD : 2 * HD]), NEG) - level)
        p_f = jnp.exp(nt(query, mem_k) - level)
        g_d = nt(grad, qkv[rows, 2 * HD : 3 * HD])
        g_f = nt(grad, mem_v)
        delta = jnp.sum(p_d * g_d, axis=1, keepdims=True) + jnp.sum(p_f * g_f, axis=1, keepdims=True)
        if b:
            past = slice(0, b * BLK)
            p_p = jnp.exp(nt(query, qkv[past, HD : 2 * HD]) - level)
            g_p = nt(grad, qkv[past, 2 * HD : 3 * HD])
            delta = delta + jnp.sum(p_p * g_p, axis=1, keepdims=True)
        s_d = (p_d * (g_d - delta)).astype(BF)
        s_f = (p_f * (g_f - delta)).astype(BF)
        dq = nn(s_d, qkv[rows, HD : 2 * HD]) + nn(s_f, mem_k)
        if b:
            s_p = (p_p * (g_p - delta)).astype(BF)
            dq = dq + nn(s_p, qkv[past, HD : 2 * HD])
            dk[past, :] = dk[past, :] + tn(s_p, query)
            dv[past, :] = dv[past, :] + tn(p_p.astype(BF), grad)
        dk[rows, :] = tn(s_d, query)
        dv[rows, :] = tn(p_d.astype(BF), grad)
        dall[rows, 0:HD] = (dq * (HD**-0.5)).astype(BF)
    dall[:, HD : 2 * HD] = dk[...].astype(BF)
    dall[:, 2 * HD : 3 * HD] = dv[...].astype(BF)
    grad_w = jnp.zeros((3 * HD, D), F32)
    for who, n, out in ((c, n_own, dq_own), (1 - c, n_oth, dq_oth)):
        part = dall[block(who, HALF), :]
        out[...] = part
        grad_w = grad_w + tn(part, n[...])
    for out, which in ((keep_out, pieces[:2]), (send_out, pieces[2:])):
        for slot, k in enumerate(which):
            out[slot, 0 : 3 * HD, :] = grad_w[:, lanes(k)].astype(BF)
            out[slot, 3 * HD : 4 * HD, :] = grad_o[:, lanes(k)].astype(BF)


def in_proj_back_body(ids, *refs):
    parts, (wa, d_own, d_oth) = refs[:8], refs[8:]
    weights = jnp.concatenate([wa[j, 0 : 3 * HD, :] for j in range(4)], axis=0)
    for side, out in ((1, d_oth), (0, d_own)):
        d = jnp.concatenate([parts[2 * j + side][...] for j in range(4)], axis=1)
        out[...] = nn(d, weights).astype(out.dtype)


def ffn_body(pieces, ids, n_own, n_oth, c_own, c_oth, w, keep_out, send_out, act, dgu):
    for side, n, cot in ((0, n_own, c_own), (1, n_oth, c_oth)):
        for i in range(2):
            rows = slice(i * 256, (i + 1) * 256)
            cols = slice(side * HALF + i * 256, side * HALF + (i + 1) * 256)
            normed = n[rows, :]
            gate = nt(w[0:HID, :], normed)
            up = nt(w[HID : 2 * HID, :], normed)
            grad = nt(w[2 * HID : 3 * HID, :], cot[rows, :])
            sig = 1.0 / (1.0 + jnp.exp(-gate))
            silu = gate * sig
            act[:, cols] = (silu * up).astype(BF)
            dgu[0:HID, cols] = (grad * up * sig * (1.0 + gate * (1.0 - sig))).astype(BF)
            dgu[HID : 2 * HID, cols] = (grad * silu).astype(BF)
    for out, which in ((keep_out, pieces[:2]), (send_out, pieces[2:])):
        for slot, k in enumerate(which):
            g = nn(dgu[:, 0:HALF], n_own[:, lanes(k)]) + nn(dgu[:, HALF:LEN], n_oth[:, lanes(k)])
            out[slot, 0 : 2 * HID, :] = g.astype(BF)
            g = nn(act[:, 0:HALF], c_own[:, lanes(k)]) + nn(act[:, HALF:LEN], c_oth[:, lanes(k)])
            out[slot, 2 * HID : 3 * HID, :] = g.astype(BF)


def ffn_sum_body(lo, hi, ids, *refs):
    parts, w, (own, oth, acc) = refs[:4], refs[4:6], refs[6:]
    for side, out in ((1, oth), (0, own)):
        cols = slice(side * HALF, (side + 1) * HALF)
        for j in range(4):
            weights = w[1][j - 1, lo:hi, :] if j else w[0][lo:hi, :]
            got = tn(parts[j][:, cols], weights)
            if j == 0:
                acc[...] = got
            elif j < 3:
                acc[...] = acc[...] + got
            else:
                out[...] = (acc[...] + got).astype(out.dtype)


def place_a_body(ids, *refs):
    q, c = ids[0], ids[1]
    own, oth, (gq, gk, gv, go) = refs[:4], refs[4:8], refs[8:]
    for k in range(NQ):
        rows = block(q ^ k, DP)
        for half, src in ((c, own[k]), (1 - c, oth[k])):
            for i, out in enumerate((gq, gk, gv)):
                out[rows, block(half, HD)] = src[i * HD : (i + 1) * HD, :].astype(F32).T
            go[block(half, HD), rows] = src[3 * HD : 4 * HD, :].astype(F32)


def place_b_body(ids, *refs):
    q, c = ids[0], ids[1]
    own, oth, outs = refs[:4], refs[4:8], refs[8:]
    for k in range(NQ):
        cols = block(q ^ k, DP)
        for half, src in ((c, own[k]), (1 - c, oth[k])):
            rows = pl.ds(pl.multiple_of(half * HID, 32), HID)
            for i, out in enumerate(outs):
                out[rows, cols] = src[i * HID : (i + 1) * HID, :].astype(F32)


def where_am_i():
    return lax.axis_index("r"), lax.axis_index("q"), lax.axis_index("c"), lax.axis_index("t")


def at(q, c, t):
    return {"q": q, "c": c, "t": t}


def dp_at(index):
    return {"r": index // (2 * NQ), "q": lax.rem(index // 2, NQ), "c": lax.rem(index, 2)}


def remote(src, dst, send_sem, recv_sem, device):
    return pltpu.make_async_remote_copy(
        src_ref=src, dst_ref=dst, send_sem=send_sem, recv_sem=recv_sem, device_id=device,
        device_id_type=pl.DeviceIdType.MESH,
    )


def arrived(dst, recv_sem, spare):
    pltpu.make_async_copy(dst, dst, recv_sem).wait()


def greet(devices):
    barrier = pltpu.get_barrier_semaphore()
    for device in devices:
        pl.semaphore_signal(barrier, inc=1, device_id=device, device_id_type=pl.DeviceIdType.MESH)
    pl.semaphore_wait(barrier, len(devices))


class Sends:
    def __init__(self):
        self.open = []

    def go(self, src, dst, send_sem, recv_sem, device, when=None):
        copy = remote(src, dst, send_sem, recv_sem, device)
        self.open.append((copy, when))
        if when is None:
            copy.start()
        else:
            pl.when(when)(copy.start)

    def drain(self):
        for copy, when in self.open:
            if when is None:
                copy.wait_send()
            else:
                pl.when(when)(copy.wait_send)
        self.open = []


def front_body(tok, cot, gain_a, gain_f, ck, cv, knn, wq, wk, wv, wo, gate_t, up_t, down,
               wa, wb, x_own, n_own, n_oth, cot_own, cot_oth, mem, qkv, att, lse, hidden, n2_own, n2_oth,
               prev_k, prev_v, picked, o_send, o_got,
               row_send, row_recv, cot_send, cot_recv, cache_send, cache_recv, mem_send, mem_recv,
               za_send, za_recv, xa_send, xa_recv, zb_send, zb_recv, xb_send, xb_recv, pair_send, pair_recv):
    r, q, c, t = where_am_i()
    count = lax.axis_size("r") * 2 * NQ
    me = (r * NQ + q) * 2 + c
    after = dp_at(lax.rem(me + 1, count))
    across = dp_at(lax.rem(me + jnp.where(c == 0, count - 1, 1), count))
    mid = (t == 1) | (t == 2)
    second, third = jnp.where(mid, 3, 2), jnp.where(mid, 2, 3)
    partner = at(q, 1 - c, t)
    sends = Sends()
    greet(
        [at(q, c, t ^ j) for j in range(1, 4)] + [at(q, 1 - c, t ^ j) for j in range(4)]
        + [at(q ^ 1, c, t), at(q ^ 2, c, t), at(q ^ 3, c, t), across]
    )

    def rows_out(src, dst, send_sem, recv_sem):
        slot = t & 1
        for m in range(MICRO):
            here = (c == (t >> 1)) & (m == slot)
            for k in range(NQ):
                one = src.at[m, :, block(q ^ k, DP)]
                two = dst.at[block(slot, 256), lanes(k)]
                sends.go(one, two, send_sem.at[m, k], recv_sem.at[slot, k], at(q, t >> 1, 2 * c + m),
                         when=jnp.logical_not(here))
                pl.when(here)(pltpu.make_async_copy(one, two, recv_sem.at[slot, k]).start)

    def rows_in(dst, recv_sem):
        for slot in range(2):
            for k in range(NQ):
                arrived(dst.at[slot * 256 : (slot + 1) * 256, lanes(k)], recv_sem.at[slot, k], None)

    rows_out(tok, x_own, row_send, row_recv)
    for i, (one, two) in enumerate(((ck, prev_k), (cv, prev_v))):
        sends.go(one, two, cache_send.at[i], cache_recv.at[i], after)

    for k in range(NQ):
        rows = block(q ^ k, DP)
        for i, w in enumerate((wq, wk, wv)):
            wa[0, i * HD : (i + 1) * HD, lanes(k)] = w[rows, block(c, HD)].T
        wa[0, 3 * HD : 4 * HD, lanes(k)] = wo[block(c, HD), rows]

    for i, two in enumerate((prev_k, prev_v)):
        arrived(two, cache_recv.at[i], None)
    for m in range(MICRO):
        for h in range(2):
            cols = slice(h * HD, (h + 1) * HD)
            for b in range(LEN // BLK):
                picks = knn[m, b, h : h + 1, :]
                rows = lax.broadcasted_iota(jnp.int32, (CACHE, TOPK), 0)
                hot_own = jnp.where(rows == picks, 1.0, 0.0).astype(BF)
                hot_prev = jnp.where(rows + CACHE == picks, 1.0, 0.0).astype(BF)
                for kv, own, prev in ((0, ck, prev_k), (1, cv, prev_v)):
                    got = tn(hot_own, own[m, :, cols]) + tn(hot_prev, prev[m, :, cols])
                    picked[m, h, kv * 512 + b * TOPK : kv * 512 + (b + 1) * TOPK, :] = got.astype(BF)
    for m in range(MICRO):
        for h in range(2):
            kind = t ^ (2 * c + m)
            here = (c == h) & (kind == 0)
            sends.go(picked.at[m, h], mem.at[kind], mem_send.at[m, h], mem_recv.at[kind], at(q, h, 2 * c + m),
                     when=jnp.logical_not(here))
            pl.when(here)(pltpu.make_async_copy(picked.at[m, h], mem.at[kind], mem_recv.at[kind]).start)

    near, far_mid = at(q, c, t ^ 1), at(q, c, t ^ 3)
    a_piece = [wa.at[0, :, lanes(0)]]
    b_piece = [w.at[pl.ds(pl.multiple_of(c * HID, 32), HID), block(q, DP)] for w in (gate_t, up_t, down)]

    def a_slot(s):
        return [wa.at[s, :, lanes(0)]]

    def b_slot(s):
        return [wb.at[s - 1, i * HID : (i + 1) * HID, lanes(0)] for i in range(3)]

    def z_first(piece, slot, send_sem, recv_sem):
        for i, (one, two) in enumerate(zip(piece, slot(1))):
            sends.go(one, two, send_sem.at[0, i], recv_sem.at[1, i], near)
        for i, (one, two) in enumerate(zip(piece, slot(3))):
            sends.go(one, two, send_sem.at[1, i], recv_sem.at[3, i], far_mid, when=mid)

    def relay(order, slot, whole, z_send, z_recv, x_send, x_recv):
        s = (None, 1, second, third)[order]
        for i, two in enumerate(slot(s)):
            arrived(two, z_recv.at[s, i], None)
        if order == 1:
            for i, (one, two) in enumerate(zip(slot(1), slot(2))):
                sends.go(one, two, z_send.at[2, i], z_recv.at[2, i], far_mid, when=mid)
        elif order == 2:
            for i, (one, two) in enumerate(zip(slot(3), slot(2))):
                sends.go(one, two, z_send.at[3, i], z_recv.at[2, i], near, when=mid)
        else:
            for i, (one, two) in enumerate(zip(slot(2), slot(3))):
                sends.go(one, two, z_send.at[4, i], z_recv.at[3, i], near, when=mid)
        sends.go(whole(s, 0), whole(s, 1), x_send.at[s, 1], x_recv.at[s, 1], at(q ^ 1, c, t))
        sends.go(whole(s, 0), whole(s, 2), x_send.at[s, 2], x_recv.at[s, 2], at(q ^ 2, c, t))
        if order == 3:
            sends.go(whole(s, 0), whole(s, 3), x_send.at[s, 3], x_recv.at[s, 3], at(q ^ 3, c, t))

    def relay_far(order, whole, x_send, x_recv):
        s = (None, 1, second)[order]
        arrived(whole(s, order), x_recv.at[s, order], None)
        sends.go(whole(s, order), whole(s, 3), x_send.at[s, 3], x_recv.at[s, 3], at(q ^ (3 - order), c, t))

    def in_place(order, whole, x_recv):
        s = (None, 1, second, third)[order]
        for k in range(1, NQ):
            if k != order or order == 3:
                arrived(whole(s, k), x_recv.at[s, k], None)

    def a_whole(s, k):
        return wa.at[s, :, lanes(k)]

    def b_whole(s, k):
        return wb.at[s - 1, :, lanes(k)]

    relay_a = functools.partial(relay, slot=a_slot, whole=a_whole, z_send=za_send, z_recv=za_recv, x_send=xa_send, x_recv=xa_recv)
    relay_b = functools.partial(relay, slot=b_slot, whole=b_whole, z_send=zb_send, z_recv=zb_recv, x_send=xb_send, x_recv=xb_recv)

    z_first(a_piece, a_slot, za_send, za_recv)
    rows_out(cot, cot_own, cot_send, cot_recv)
    z_first(b_piece, b_slot, zb_send, zb_recv)

    rows_in(x_own, row_recv)
    gain = jnp.concatenate([gain_a[:, block(q ^ k, DP)] for k in range(NQ)], axis=1)
    for i in range(2):
        rows = slice(i * 256, (i + 1) * 256)
        x = x_own[rows, :].astype(F32)
        n_own[rows, :] = (x * scale_of(x) * gain).astype(BF)
    sends.go(n_own, n_oth, pair_send.at[0], pair_recv.at[0], partner)

    def project(j, who, n):
        acc = nt(n[...], wa[j, 0 : 3 * HD, :])
        rows = block(who, HALF)
        qkv[j, rows, 0:HD] = (acc[:, 0:HD] * (HD**-0.5)).astype(BF)
        qkv[j, rows, HD : 3 * HD] = acc[:, HD : 3 * HD].astype(BF)

    def attend(j):
        keep = causal()
        for b in range(LEN // BLK):
            rows = slice(b * BLK, (b + 1) * BLK)
            query = qkv[j, rows, 0:HD]
            diag = jnp.where(keep, nt(query, qkv[j, rows, HD : 2 * HD]), NEG)
            far = nt(query, mem[j, b * TOPK : (b + 1) * TOPK, :])
            top = jnp.maximum(jnp.max(diag, axis=1, keepdims=True), jnp.max(far, axis=1, keepdims=True))
            if b:
                past = nt(query, qkv[j, 0 : b * BLK, HD : 2 * HD])
                top = jnp.maximum(top, jnp.max(past, axis=1, keepdims=True))
            diag = jnp.exp(diag - top)
            far = jnp.exp(far - top)
            total = jnp.sum(diag, axis=1, keepdims=True) + jnp.sum(far, axis=1, keepdims=True)
            if b:
                past = jnp.exp(past - top)
                total = total + jnp.sum(past, axis=1, keepdims=True)
            inverse = 1.0 / total
            out = nn((diag * inverse).astype(BF), qkv[j, rows, 2 * HD : 3 * HD])
            out = out + nn((far * inverse).astype(BF), mem[j, 512 + b * TOPK : 512 + (b + 1) * TOPK, :])
            if b:
                out = out + nn((past * inverse).astype(BF), qkv[j, 0 : b * BLK, 2 * HD : 3 * HD])
            att[rows, j * HD : (j + 1) * HD] = out.astype(BF)
            lse[j, rows, :] = jnp.broadcast_to(top + jnp.log(total), (BLK, HD))

    def got_mem(j):
        arrived(mem.at[j], mem_recv.at[j], None)

    project(0, c, n_own)
    arrived(n_oth, pair_recv.at[0], None)
    project(0, 1 - c, n_oth)
    got_mem(0)
    relay_a(1)
    attend(0)
    relay_a(2)
    relay_far(1, a_whole, xa_send, xa_recv)
    relay_a(3)
    relay_far(2, a_whole, xa_send, xa_recv)
    in_place(1, a_whole, xa_recv)
    got_mem(1)
    project(1, c, n_own)
    project(1, 1 - c, n_oth)
    attend(1)
    in_place(2, a_whole, xa_recv)
    in_place(3, a_whole, xa_recv)
    relay_b(1)
    for j in (2, 3):
        got_mem(j)
        project(j, c, n_own)
        project(j, 1 - c, n_oth)
        attend(j)
        if j == 2:
            relay_b(2)
            relay_far(1, b_whole, xb_send, xb_recv)

    weights = jnp.concatenate([wa[j, 3 * HD : 4 * HD, :] for j in range(4)], axis=0)
    o_send[...] = nn(att[block(1 - c, HALF), :], weights).astype(BF)
    sends.go(o_send, o_got, pair_send.at[1], pair_recv.at[1], partner)
    hidden[...] = nn(att[block(c, HALF), :], weights)
    rows_in(cot_own, cot_recv)
    sends.go(cot_own, cot_oth, pair_send.at[2], pair_recv.at[2], partner)
    arrived(o_got, pair_recv.at[1], None)
    gain = jnp.concatenate([gain_f[:, block(q ^ k, DP)] for k in range(NQ)], axis=1)
    for i in range(2):
        rows = slice(i * 256, (i + 1) * 256)
        h = x_own[rows, :].astype(F32) + (hidden[rows, :] + o_got[rows, :].astype(F32))
        hidden[rows, :] = h
        n2_own[rows, :] = (h * scale_of(h) * gain).astype(BF)
    sends.go(n2_own, n2_oth, pair_send.at[3], pair_recv.at[3], partner)
    relay_b(3)
    relay_far(2, b_whole, xb_send, xb_recv)
    for order in range(1, 4):
        in_place(order, b_whole, xb_recv)
    arrived(n2_oth, pair_recv.at[3], None)
    arrived(cot_oth, pair_recv.at[2], None)
    sends.drain()


def front(*args):
    hbm = pl.BlockSpec(memory_space=pl.ANY)
    outs = [
        ((4, RA, D), BF, VM), ((3, RB, D), BF, hbm), ((HALF, D), BF, VM), ((HALF, D), BF, VM), ((HALF, D), BF, VM),
        ((HALF, D), BF, hbm), ((HALF, D), BF, hbm), ((4, 1024, HD), BF, VM), ((4, LEN, 3 * HD), BF, VM),
        ((LEN, 4 * HD), BF, VM), ((4, LEN, HD), F32, VM), ((HALF, D), F32, VM), ((HALF, D), BF, VM), ((HALF, D), BF, VM),
    ]
    dma = pltpu.SemaphoreType.DMA
    return pl.pallas_call(
        front_body,
        out_shape=[jax.ShapeDtypeStruct(s, d) for s, d, _ in outs],
        in_specs=[hbm, hbm] + [VM] * 9 + [hbm] * 3,
        out_specs=[m for _, _, m in outs],
        scratch_shapes=[
            pltpu.VMEM((MICRO, CACHE, 256), BF), pltpu.VMEM((MICRO, CACHE, 256), BF),
            pltpu.VMEM((MICRO, 2, 1024, HD), BF), pltpu.VMEM((HALF, D), BF), pltpu.VMEM((HALF, D), BF),
            dma((2, 4)), dma((2, 4)), dma((2, 4)), dma((2, 4)), dma((2,)), dma((2,)), dma((2, 2)), dma((4,)),
            dma((5, 1)), dma((4, 1)), dma((4, 4)), dma((4, 4)), dma((5, 3)), dma((4, 3)), dma((4, 4)), dma((4, 4)),
            dma((4,)), dma((4,)),
        ],
        compiler_params=pltpu.CompilerParams(collective_id=0, has_side_effects=True, vmem_limit_bytes=60 << 20),
        name="front",
        cost_estimate=pl.CostEstimate(flops=int(2e10), bytes_accessed=int(5e7), transcendentals=0),
    )(*args)


def send(value, axis, pairs):
    return lax.ppermute(value, axis, pairs)


def flip(value, axis, bits):
    count = lax.axis_size(axis)
    return send(value, axis, [(i, i ^ bits) for i in range(count)])


def row_pairs(r):
    return [
        (c * 4 + t, (t // 2) * 4 + 2 * c + (r + t) % 2)
        for c in range(2)
        for t in range(4)
    ]


def rows_to_sequences(s0, s1):
    return [send(s, ("c", "t"), row_pairs(r)) for r, s in ((0, s0), (1, s1))]


def rows_back(s0, s1):
    return [send(s, ("c", "t"), [(b, a) for a, b in row_pairs(r)]) for r, s in ((0, s0), (1, s1))]


PIECES = ((0, 2, 1, 3), (0, 1, 2, 3), (0, 2, 1, 3), (0, 1, 2, 3))


def plane_sum(j, keep, out):
    first, second = (1, 2) if j % 2 == 0 else (2, 1)
    kept = (keep.astype(F32) + flip(out, "q", first).astype(F32)).astype(BF)
    return (kept[0].astype(F32) + flip(kept[1], "q", second).astype(F32)).astype(BF)


def column_sum(sums):
    total = sums[0].astype(F32)
    for j in range(1, 4):
        total = total + flip(sums[j], "t", j).astype(F32)
    if lax.axis_size("r") > 1:
        total = lax.psum(total, "r")
    return total.astype(BF)


def spread(total, odd):
    by_x = flip(total, "q", 1)
    by_y = flip(total, "q", 2)
    far = flip(by_x, "q", 2) if odd else flip(by_y, "q", 1)
    own = [total, by_x, by_y, far]
    return own, [flip(p, "c", 1) for p in own]


def per_device(tokens, attn_gain, ffn_gain, query_weight, key_weight, value_weight, out_weight, gate_weight,
               up_weight, down_weight, cache_keys, cache_values, knn_index, cotangent):
    q, c, t = lax.axis_index("q"), lax.axis_index("c"), lax.axis_index("t")
    ids = jnp.stack([q, c, t]).astype(jnp.int32)
    gain_a, gain_f = attn_gain.reshape(1, D), ffn_gain.reshape(1, D)
    gate_t, up_t = gate_weight.T, up_weight.T
    rows16 = ((256, D), BF)
    half16, half32 = ((HALF, D), BF), ((HALF, D), F32)

    wa, wb, x_own, n1_own, n1_oth, cot_own, cot_oth, mem, qkv, att, lse, hidden, n2_own, n2_oth = front(
        tokens, cotangent, gain_a, gain_f, cache_keys, cache_values, knn_index, query_weight, key_weight, value_weight,
        out_weight, gate_t, up_t, down_weight,
    )
    (wb0,) = call(own_b_body, [((RB, D), BF)], (ids, gate_t, up_t, down_weight), name="own_b")
    chunks = [
        call(
            functools.partial(ffn_body, PIECES[j]),
            [((2, RB, DP), BF), ((2, RB, DP), BF), ((HID, LEN), BF), ((2 * HID, LEN), BF)],
            (ids, n2_own, n2_oth, cot_own, cot_oth, wb[j - 1] if j else wb0),
            flops=6 * 2 * 1024 * 1024 * HID, trans=1024 * HID, name="ffn",
        )
        for j in range(4)
    ]
    d2_own, d2_oth = call(
        functools.partial(ffn_sum_body, 0, 2 * HID), [half32, half16], (ids, *[ch[3] for ch in chunks], wb0, wb),
        flops=2 * 1024 * 1024 * 8 * HID, scratch=[pltpu.VMEM((HALF, D), F32)], name="ffn_back",
    )
    d2_got = flip(d2_oth, "c", 1)
    y_own, y_oth = call(
        functools.partial(ffn_sum_body, 2 * HID, 3 * HID), [half32, half16], (ids, *[ch[2] for ch in chunks], wb0, wb),
        flops=2 * 1024 * 1024 * 4 * HID, scratch=[pltpu.VMEM((HALF, D), F32)], name="ffn_out",
    )
    y_got = flip(y_oth, "c", 1)
    grad_hidden, low_own, gain_two = call(
        norm_two_back_body, [half32, half16, ((1, D), F32)], (ids, d2_own, d2_got, cot_own, hidden, gain_f),
        name="norm_two_back",
    )
    low_oth = flip(low_own, "c", 1)
    os0, os1 = call(output_body, [rows16, rows16], (ids, hidden, y_own, y_got), name="output")
    ob0, ob1 = rows_back(os0, os1)
    (output,) = call(unprep_rows_body, [((MICRO, 256, D), BF)], (ids, ob0, ob1), name="unprep_output")

    sums_b = [plane_sum(j, ch[0], ch[1]) for j, ch in enumerate(chunks)]
    backs = [
        call(
            functools.partial(attention_back_body, j, PIECES[j]),
            [((2, RA, DP), BF), ((2, RA, DP), BF), ((HALF, 3 * HD), BF), ((HALF, 3 * HD), BF)],
            (ids, low_own, low_oth, n1_own, n1_oth, wa, qkv, att, lse, mem),
            flops=2 * 1024 * 1024 * 640 + 10 * 128 * 786432, trans=786432,
            scratch=[
                pltpu.VMEM((LEN, HD), BF), pltpu.VMEM((LEN, HD), F32), pltpu.VMEM((LEN, HD), F32),
                pltpu.VMEM((LEN, 3 * HD), BF),
            ],
            name="attention_back",
        )
        for j in range(4)
    ]
    total_b = column_sum(sums_b)
    b_own, b_oth = spread(total_b, True)
    sums_a = [plane_sum(j, bk[0], bk[1]) for j, bk in enumerate(backs)]
    d1_own, d1_oth = call(
        in_proj_back_body, [half32, half16], (ids, *[p for bk in backs for p in bk[2:]], wa),
        flops=2 * 1024 * 1024 * 1536, name="in_proj_back",
    )
    d1_got = flip(d1_oth, "c", 1)
    gs0, gs1, gain_one = call(
        norm_one_back_body, [rows16, rows16, ((1, D), F32)], (ids, d1_own, d1_got, grad_hidden, x_own, gain_a),
        name="norm_one_back",
    )
    gb0, gb1 = rows_back(gs0, gs1)
    (grad_tokens,) = call(unprep_rows_body, [((MICRO, 256, D), BF)], (ids, gb0, gb1), name="unprep_grad")
    total_a = column_sum(sums_a)
    a_own, a_oth = spread(total_a, False)

    tall = ((2 * HID, D), F32)
    gg, gu, gd = call(place_b_body, [tall, tall, tall], (ids, *b_own, *b_oth), name="place_b")
    col, row = ((D, 2 * HD), F32), ((2 * HD, D), F32)
    gq, gk, gv, go = call(place_a_body, [col, col, col, row], (ids, *a_own, *a_oth), name="place_a")
    gain_sums = lax.psum(jnp.concatenate((gain_one, gain_two)), ("r", "q", "c", "t"))
    return output, grad_tokens, gq, gk, gv, go, gg.T, gu.T, gd, gain_sums[0], gain_sums[1]


def solution(mesh):
    n_dp, n_t = mesh.shape["dp"], mesh.shape["tensor"]
    fine = Mesh(mesh.devices.reshape(n_dp // 8, NQ, 2, n_t), ("r", "q", "c", "t"))
    dp = ("r", "q", "c")
    rows = P(None, dp + ("t",), None)
    placed = (
        rows, P(), P(), P(None, "t"), P(None, "t"), P(None, "t"), P("t", None), P(None, "t"), P(None, "t"),
        P("t", None), P(None, dp, "t"), P(None, dp, "t"), P(None, dp, "t", None), rows,
    )
    return jax.shard_map(
        per_device,
        mesh=fine,
        in_specs=placed,
        out_specs=(
            rows, rows, P(None, "t"), P(None, "t"), P(None, "t"), P("t", None), P(None, "t"), P(None, "t"),
            P("t", None), P(), P(),
        ),
        check_vma=False,
    )
```

```python
import functools

import jax
import jax.numpy as jnp
from jax import lax
from jax.experimental import pallas as pl
from jax.experimental.pallas import tpu as pltpu
from jax.sharding import Mesh
from jax.sharding import PartitionSpec as P

HEADS = 8
HD = 128
MICRO = 2
BLK = 256
TOPK = 128
CACHE = 256
D = 1024
NQ = 4
DP = D // NQ
HALF = 512
LEN = 1024
HID = 352
RA = 4 * HD
RB = 3 * HID

EPS = 1e-06
NEG = -1e30
BF = jnp.bfloat16
F32 = jnp.float32


def nn(a, b):
    return lax.dot_general(a, b, (((1,), (0,)), ((), ())), preferred_element_type=F32)


def nt(a, b):
    return lax.dot_general(a, b, (((1,), (1,)), ((), ())), preferred_element_type=F32)


def tn(a, b):
    return lax.dot_general(a, b, (((0,), (0,)), ((), ())), preferred_element_type=F32)


VM = pl.BlockSpec(memory_space=pltpu.VMEM)


def call(body, outs, args, flops=0, trans=0, scratch=(), name=None, vmem=None):
    nbytes = sum(a.size * a.dtype.itemsize for a in args) + sum(
        jnp.dtype(t).itemsize * functools.reduce(lambda x, y: x * y, s, 1) for s, t in outs
    )
    return pl.pallas_call(
        body,
        out_shape=[jax.ShapeDtypeStruct(s, t) for s, t in outs],
        in_specs=[VM for _ in args],
        out_specs=[VM for _ in outs],
        scratch_shapes=list(scratch),
        name=name,
        compiler_params=pltpu.CompilerParams(vmem_limit_bytes=vmem),
        cost_estimate=pl.CostEstimate(flops=int(flops), bytes_accessed=int(nbytes), transcendentals=int(trans)),
    )(*args)


def block(index, size):
    return pl.ds(pl.multiple_of(index * size, size), size)


def lanes(k):
    return slice(k * DP, (k + 1) * DP)


def scale_of(x):
    return lax.rsqrt(jnp.mean(x * x, axis=-1, keepdims=True) + EPS)


def norm_back(grad, x, gain):
    scale = scale_of(x)
    scaled = grad * gain
    gain_part = jnp.sum(grad * x * scale, axis=0, keepdims=True)
    back = scale * scaled - x * (scale * scale * scale) * jnp.mean(scaled * x, axis=-1, keepdims=True)
    return back, gain_part


def causal():
    return lax.broadcasted_iota(jnp.int32, (BLK, BLK), 1) <= lax.broadcasted_iota(jnp.int32, (BLK, BLK), 0)


def place_a_body(got, gq, gk, gv, go):
    for half in range(2):
        rows = slice(half * HD, (half + 1) * HD)
        for i, out in enumerate((gq, gk, gv)):
            out[:, rows] = got[half, i * HD : (i + 1) * HD, :].astype(F32).T
        go[rows, :] = got[half, 3 * HD : 4 * HD, :].astype(F32)


def place_b_body(got, *outs):
    for half in range(2):
        for i, out in enumerate(outs):
            out[half * HID : (half + 1) * HID, :] = got[half, i * HID : (i + 1) * HID, :].astype(F32)


def where_am_i():
    return lax.axis_index("r"), lax.axis_index("q"), lax.axis_index("c"), lax.axis_index("t")


def at(q, c, t):
    return {"q": q, "c": c, "t": t}


def dp_at(index):
    return {"r": index // (2 * NQ), "q": lax.rem(index // 2, NQ), "c": lax.rem(index, 2)}


def remote(src, dst, send_sem, recv_sem, device):
    return pltpu.make_async_remote_copy(
        src_ref=src, dst_ref=dst, send_sem=send_sem, recv_sem=recv_sem, device_id=device,
        device_id_type=pl.DeviceIdType.MESH,
    )


def arrived(dst, recv_sem, spare):
    pltpu.make_async_copy(dst, dst, recv_sem).wait()


def greet(devices):
    barrier = pltpu.get_barrier_semaphore()
    for device in devices:
        pl.semaphore_signal(barrier, inc=1, device_id=device, device_id_type=pl.DeviceIdType.MESH)
    pl.semaphore_wait(barrier, len(devices))


class Sends:
    def __init__(self):
        self.open = []

    def go(self, src, dst, send_sem, recv_sem, device, when=None):
        copy = remote(src, dst, send_sem, recv_sem, device)
        self.open.append((copy, when))
        if when is None:
            copy.start()
        else:
            pl.when(when)(copy.start)

    def drain(self):
        for copy, when in self.open:
            if when is None:
                copy.wait_send()
            else:
                pl.when(when)(copy.wait_send)
        self.open = []


def front_body(tok, cot, gain_a, gain_f, ck, cv, knn, wq, wk, wv, wo, gate_t, up_t, down,
               wa, wb, x_own, n_own, n_oth, cot_own, cot_oth, mem, qkv, att, lse, hidden, n2_own, n2_oth,
               prev_k, prev_v, picked, o_send, o_got,
               row_send, row_recv, cot_send, cot_recv, cache_send, cache_recv, mem_send, mem_recv,
               za_send, za_recv, xa_send, xa_recv, zb_send, zb_recv, xb_send, xb_recv, pair_send, pair_recv):
    r, q, c, t = where_am_i()
    count = lax.axis_size("r") * 2 * NQ
    me = (r * NQ + q) * 2 + c
    after = dp_at(lax.rem(me + 1, count))
    across = dp_at(lax.rem(me + jnp.where(c == 0, count - 1, 1), count))
    mid = (t == 1) | (t == 2)
    second, third = jnp.where(mid, 3, 2), jnp.where(mid, 2, 3)
    partner = at(q, 1 - c, t)
    sends = Sends()
    greet(
        [at(q, c, t ^ j) for j in range(1, 4)] + [at(q, 1 - c, t ^ j) for j in range(4)]
        + [at(q ^ 1, c, t), at(q ^ 2, c, t), at(q ^ 3, c, t), across]
    )

    def rows_out(src, dst, send_sem, recv_sem):
        slot = t & 1
        for m in range(MICRO):
            here = (c == (t >> 1)) & (m == slot)
            for k in range(NQ):
                one = src.at[m, :, block(q ^ k, DP)]
                two = dst.at[block(slot, 256), lanes(k)]
                sends.go(one, two, send_sem.at[m, k], recv_sem.at[slot, k], at(q, t >> 1, 2 * c + m),
                         when=jnp.logical_not(here))
                pl.when(here)(pltpu.make_async_copy(one, two, recv_sem.at[slot, k]).start)

    def rows_in(dst, recv_sem):
        for slot in range(2):
            for k in range(NQ):
                arrived(dst.at[slot * 256 : (slot + 1) * 256, lanes(k)], recv_sem.at[slot, k], None)

    rows_out(tok, x_own, row_send, row_recv)
    for i, (one, two) in enumerate(((ck, prev_k), (cv, prev_v))):
        sends.go(one, two, cache_send.at[i], cache_recv.at[i], after)

    for k in range(NQ):
        rows = block(q ^ k, DP)
        for i, w in enumerate((wq, wk, wv)):
            wa[0, i * HD : (i + 1) * HD, lanes(k)] = w[rows, block(c, HD)].T
        wa[0, 3 * HD : 4 * HD, lanes(k)] = wo[block(c, HD), rows]

    for i, two in enumerate((prev_k, prev_v)):
        arrived(two, cache_recv.at[i], None)
    for m in range(MICRO):
        for h in range(2):
            cols = slice(h * HD, (h + 1) * HD)
            for b in range(LEN // BLK):
                picks = knn[m, b, h : h + 1, :]
                rows = lax.broadcasted_iota(jnp.int32, (CACHE, TOPK), 0)
                hot_own = jnp.where(rows == picks, 1.0, 0.0).astype(BF)
                hot_prev = jnp.where(rows + CACHE == picks, 1.0, 0.0).astype(BF)
                for kv, own, prev in ((0, ck, prev_k), (1, cv, prev_v)):
                    got = tn(hot_own, own[m, :, cols]) + tn(hot_prev, prev[m, :, cols])
                    picked[m, h, kv * 512 + b * TOPK : kv * 512 + (b + 1) * TOPK, :] = got.astype(BF)
    for m in range(MICRO):
        for h in range(2):
            kind = t ^ (2 * c + m)
            here = (c == h) & (kind == 0)
            sends.go(picked.at[m, h], mem.at[kind], mem_send.at[m, h], mem_recv.at[kind], at(q, h, 2 * c + m),
                     when=jnp.logical_not(here))
            pl.when(here)(pltpu.make_async_copy(picked.at[m, h], mem.at[kind], mem_recv.at[kind]).start)

    near, far_mid = at(q, c, t ^ 1), at(q, c, t ^ 3)
    a_piece = [wa.at[0, :, lanes(0)]]
    b_piece = [w.at[pl.ds(pl.multiple_of(c * HID, 32), HID), block(q, DP)] for w in (gate_t, up_t, down)]

    def a_slot(s):
        return [wa.at[s, :, lanes(0)]]

    def b_slot(s):
        return [wb.at[s - 1, i * HID : (i + 1) * HID, lanes(0)] for i in range(3)]

    def z_first(piece, slot, send_sem, recv_sem):
        for i, (one, two) in enumerate(zip(piece, slot(1))):
            sends.go(one, two, send_sem.at[0, i], recv_sem.at[1, i], near)
        for i, (one, two) in enumerate(zip(piece, slot(3))):
            sends.go(one, two, send_sem.at[1, i], recv_sem.at[3, i], far_mid, when=mid)

    def relay(order, slot, whole, z_send, z_recv, x_send, x_recv):
        s = (None, 1, second, third)[order]
        for i, two in enumerate(slot(s)):
            arrived(two, z_recv.at[s, i], None)
        if order == 1:
            for i, (one, two) in enumerate(zip(slot(1), slot(2))):
                sends.go(one, two, z_send.at[2, i], z_recv.at[2, i], far_mid, when=mid)
        elif order == 2:
            for i, (one, two) in enumerate(zip(slot(3), slot(2))):
                sends.go(one, two, z_send.at[3, i], z_recv.at[2, i], near, when=mid)
        else:
            for i, (one, two) in enumerate(zip(slot(2), slot(3))):
                sends.go(one, two, z_send.at[4, i], z_recv.at[3, i], near, when=mid)
        sends.go(whole(s, 0), whole(s, 1), x_send.at[s, 1], x_recv.at[s, 1], at(q ^ 1, c, t))
        sends.go(whole(s, 0), whole(s, 2), x_send.at[s, 2], x_recv.at[s, 2], at(q ^ 2, c, t))
        if order == 3:
            sends.go(whole(s, 0), whole(s, 3), x_send.at[s, 3], x_recv.at[s, 3], at(q ^ 3, c, t))

    def relay_far(order, whole, x_send, x_recv):
        s = (None, 1, second)[order]
        arrived(whole(s, order), x_recv.at[s, order], None)
        sends.go(whole(s, order), whole(s, 3), x_send.at[s, 3], x_recv.at[s, 3], at(q ^ (3 - order), c, t))

    def in_place(order, whole, x_recv):
        s = (None, 1, second, third)[order]
        for k in range(1, NQ):
            if k != order or order == 3:
                arrived(whole(s, k), x_recv.at[s, k], None)

    def a_whole(s, k):
        return wa.at[s, :, lanes(k)]

    def b_whole(s, k):
        return wb.at[s - 1, :, lanes(k)]

    relay_a = functools.partial(relay, slot=a_slot, whole=a_whole, z_send=za_send, z_recv=za_recv, x_send=xa_send, x_recv=xa_recv)
    relay_b = functools.partial(relay, slot=b_slot, whole=b_whole, z_send=zb_send, z_recv=zb_recv, x_send=xb_send, x_recv=xb_recv)

    z_first(a_piece, a_slot, za_send, za_recv)
    rows_out(cot, cot_own, cot_send, cot_recv)
    z_first(b_piece, b_slot, zb_send, zb_recv)

    rows_in(x_own, row_recv)
    gain = jnp.concatenate([gain_a[:, block(q ^ k, DP)] for k in range(NQ)], axis=1)
    for i in range(2):
        rows = slice(i * 256, (i + 1) * 256)
        x = x_own[rows, :].astype(F32)
        n_own[rows, :] = (x * scale_of(x) * gain).astype(BF)
    sends.go(n_own, n_oth, pair_send.at[0], pair_recv.at[0], partner)

    def project(j, who, n):
        acc = nt(n[...], wa[j, 0 : 3 * HD, :])
        rows = block(who, HALF)
        qkv[j, rows, 0:HD] = (acc[:, 0:HD] * (HD**-0.5)).astype(BF)
        qkv[j, rows, HD : 3 * HD] = acc[:, HD : 3 * HD].astype(BF)

    def attend(j):
        keep = causal()
        for b in range(LEN // BLK):
            rows = slice(b * BLK, (b + 1) * BLK)
            query = qkv[j, rows, 0:HD]
            diag = jnp.where(keep, nt(query, qkv[j, rows, HD : 2 * HD]), NEG)
            far = nt(query, mem[j, b * TOPK : (b + 1) * TOPK, :])
            top = jnp.maximum(jnp.max(diag, axis=1, keepdims=True), jnp.max(far, axis=1, keepdims=True))
            if b:
                past = nt(query, qkv[j, 0 : b * BLK, HD : 2 * HD])
                top = jnp.maximum(top, jnp.max(past, axis=1, keepdims=True))
            diag = jnp.exp(diag - top)
            far = jnp.exp(far - top)
            total = jnp.sum(diag, axis=1, keepdims=True) + jnp.sum(far, axis=1, keepdims=True)
            if b:
                past = jnp.exp(past - top)
                total = total + jnp.sum(past, axis=1, keepdims=True)
            inverse = 1.0 / total
            out = nn((diag * inverse).astype(BF), qkv[j, rows, 2 * HD : 3 * HD])
            out = out + nn((far * inverse).astype(BF), mem[j, 512 + b * TOPK : 512 + (b + 1) * TOPK, :])
            if b:
                out = out + nn((past * inverse).astype(BF), qkv[j, 0 : b * BLK, 2 * HD : 3 * HD])
            att[rows, j * HD : (j + 1) * HD] = out.astype(BF)
            lse[j, rows, :] = jnp.broadcast_to(top + jnp.log(total), (BLK, HD))

    def got_mem(j):
        arrived(mem.at[j], mem_recv.at[j], None)

    project(0, c, n_own)
    arrived(n_oth, pair_recv.at[0], None)
    project(0, 1 - c, n_oth)
    got_mem(0)
    relay_a(1)
    attend(0)
    relay_a(2)
    relay_far(1, a_whole, xa_send, xa_recv)
    relay_a(3)
    relay_far(2, a_whole, xa_send, xa_recv)
    in_place(1, a_whole, xa_recv)
    got_mem(1)
    project(1, c, n_own)
    project(1, 1 - c, n_oth)
    attend(1)
    in_place(2, a_whole, xa_recv)
    in_place(3, a_whole, xa_recv)
    relay_b(1)
    for j in (2, 3):
        got_mem(j)
        project(j, c, n_own)
        project(j, 1 - c, n_oth)
        attend(j)
        if j == 2:
            relay_b(2)
            relay_far(1, b_whole, xb_send, xb_recv)

    weights = jnp.concatenate([wa[j, 3 * HD : 4 * HD, :] for j in range(4)], axis=0)
    o_send[...] = nn(att[block(1 - c, HALF), :], weights).astype(BF)
    sends.go(o_send, o_got, pair_send.at[1], pair_recv.at[1], partner)
    hidden[...] = nn(att[block(c, HALF), :], weights)
    rows_in(cot_own, cot_recv)
    sends.go(cot_own, cot_oth, pair_send.at[2], pair_recv.at[2], partner)
    arrived(o_got, pair_recv.at[1], None)
    gain = jnp.concatenate([gain_f[:, block(q ^ k, DP)] for k in range(NQ)], axis=1)
    for i in range(2):
        rows = slice(i * 256, (i + 1) * 256)
        h = x_own[rows, :].astype(F32) + (hidden[rows, :] + o_got[rows, :].astype(F32))
        hidden[rows, :] = h
        n2_own[rows, :] = (h * scale_of(h) * gain).astype(BF)
    sends.go(n2_own, n2_oth, pair_send.at[3], pair_recv.at[3], partner)
    relay_b(3)
    relay_far(2, b_whole, xb_send, xb_recv)
    for order in range(1, 4):
        in_place(order, b_whole, xb_recv)
    arrived(n2_oth, pair_recv.at[3], None)
    arrived(cot_oth, pair_recv.at[2], None)
    sends.drain()


def front(*args):
    hbm = pl.BlockSpec(memory_space=pl.ANY)
    outs = [
        ((4, RA, D), BF, VM), ((3, RB, D), BF, hbm), ((HALF, D), BF, VM), ((HALF, D), BF, VM), ((HALF, D), BF, VM),
        ((HALF, D), BF, hbm), ((HALF, D), BF, hbm), ((4, 1024, HD), BF, VM), ((4, LEN, 3 * HD), BF, VM),
        ((LEN, 4 * HD), BF, VM), ((4, LEN, HD), F32, VM), ((HALF, D), F32, VM), ((HALF, D), BF, VM), ((HALF, D), BF, VM),
    ]
    dma = pltpu.SemaphoreType.DMA
    return pl.pallas_call(
        front_body,
        out_shape=[jax.ShapeDtypeStruct(s, d) for s, d, _ in outs],
        in_specs=[hbm, hbm] + [VM] * 9 + [hbm] * 3,
        out_specs=[m for _, _, m in outs],
        scratch_shapes=[
            pltpu.VMEM((MICRO, CACHE, 256), BF), pltpu.VMEM((MICRO, CACHE, 256), BF),
            pltpu.VMEM((MICRO, 2, 1024, HD), BF), pltpu.VMEM((HALF, D), BF), pltpu.VMEM((HALF, D), BF),
            dma((2, 4)), dma((2, 4)), dma((2, 4)), dma((2, 4)), dma((2,)), dma((2,)), dma((2, 2)), dma((4,)),
            dma((5, 1)), dma((4, 1)), dma((4, 4)), dma((4, 4)), dma((5, 3)), dma((4, 3)), dma((4, 4)), dma((4, 4)),
            dma((4,)), dma((4,)),
        ],
        compiler_params=pltpu.CompilerParams(collective_id=0, has_side_effects=True, vmem_limit_bytes=60 << 20),
        name="front",
        cost_estimate=pl.CostEstimate(flops=int(2e10), bytes_accessed=int(5e7), transcendentals=0),
    )(*args)


def everyone(q, c, t):
    return (
        [at(q, c, t ^ j) for j in range(1, 4)] + [at(q, 1 - c, t ^ j) for j in range(4)]
        + [at(q ^ 1, c, t), at(q ^ 2, c, t)]
    )


def add_low(a, b):
    return (a.astype(F32) + b.astype(F32)).astype(BF)


class Plane:
    def __init__(self, chunk, recv1, recv2, sems):
        self.chunk, self.recv1, self.recv2 = chunk, recv1, recv2
        self.s1, self.r1, self.s2, self.r2 = sems
        _, self.q, self.c, self.t = where_am_i()

    def order(self, j):
        odd = j & 1
        return 1 + odd, 2 - odd

    def copy1(self, j):
        first, _ = self.order(j)
        return remote(self.chunk.at[j, pl.ds(2, 2)], self.recv1.at[j], self.s1.at[j], self.r1.at[j],
                      at(self.q ^ first, self.c, self.t))

    def copy2(self, j):
        _, second = self.order(j)
        return remote(self.chunk.at[j, 1], self.recv2.at[j], self.s2.at[j], self.r2.at[j],
                      at(self.q ^ second, self.c, self.t))

    def stage2(self, j):
        arrived(self.recv1.at[j], self.r1.at[j], None)
        self.chunk[j, 1] = add_low(self.chunk[j, 1], self.recv1[j, 1])
        self.chunk[j, 0] = add_low(self.chunk[j, 0], self.recv1[j, 0])
        self.copy2(j).start()

    def stage3(self, j, out):
        arrived(self.recv2.at[j], self.r2.at[j], None)
        out[j] = add_low(self.chunk[j, 0], self.recv2[j])

    def drain(self):
        for j in range(4):
            self.copy1(j).wait_send()
            self.copy2(j).wait_send()


def rows_back(sends, src, dst, send_sem, recv_sem):
    _, q, c, t = where_am_i()
    m = t & 1
    for s in range(2):
        here = (c == (t >> 1)) & (s == m)
        for k in range(NQ):
            one = src.at[s * 256 : (s + 1) * 256, lanes(k)]
            two = dst.at[m, :, block(q ^ k, DP)]
            sends.go(one, two, send_sem.at[s, k], recv_sem.at[m, k], at(q, t >> 1, 2 * c + s),
                     when=jnp.logical_not(here))
            pl.when(here)(pltpu.make_async_copy(one, two, recv_sem.at[m, k]).start)


def rows_back_in(dst, recv_sem):
    _, q, _, _ = where_am_i()
    for m in range(2):
        for k in range(NQ):
            arrived(dst.at[m, :, block(q ^ k, DP)], recv_sem.at[m, k], None)


def put_gain(out, row, total):
    _, q, _, _ = where_am_i()
    for k in range(NQ):
        out[row : row + 1, block(q ^ k, DP)] = total[:, lanes(k)]


def local_gain(gain):
    _, q, _, _ = where_am_i()
    return jnp.concatenate([gain[:, block(q ^ k, DP)] for k in range(NQ)], axis=1)


DMA = pltpu.SemaphoreType.DMA
HBM = pl.BlockSpec(memory_space=pl.ANY)


def remote_call(body, name, number, args, places, outs, scratch, flops):
    return pl.pallas_call(
        body,
        out_shape=[jax.ShapeDtypeStruct(s, d) for s, d, _ in outs],
        in_specs=list(places),
        out_specs=[m for _, _, m in outs],
        scratch_shapes=list(scratch),
        compiler_params=pltpu.CompilerParams(collective_id=number, has_side_effects=True, vmem_limit_bytes=62 << 20),
        name=name,
        cost_estimate=pl.CostEstimate(flops=int(flops), bytes_accessed=int(5e7), transcendentals=0),
    )(*args)


def middle_body(n_own, n_oth, cot_own, cot_oth, hidden, gain_f, gate_t, up_t, down, wb,
                sums, grad_hidden, low_own, low_oth, out_rows, gain_two,
                wgu, wd, act, dgu, chunk, recv1, recv2, d_send, d_got, y_send, y_got, rows_buf,
                own_sem, got_sem, s1, r1, s2, r2, pair_send, pair_recv, row_send, row_recv):
    _, q, c, t = where_am_i()
    partner = at(q, 1 - c, t)
    sends = Sends()

    def own_copies():
        rows = pl.ds(pl.multiple_of(c * HID, 32), HID)
        for k in range(NQ):
            for i, (w, two) in enumerate(((gate_t, wgu.at[0:HID, lanes(k)]), (up_t, wgu.at[HID : 2 * HID, lanes(k)]),
                                          (down, wd.at[0:HID, lanes(k)]))):
                yield pltpu.make_async_copy(w.at[rows, block(q ^ k, DP)], two, own_sem.at[i, k])

    def got_copies(j):
        gu = wgu.at[pl.ds(pl.multiple_of(j * (2 * HID), 32), 2 * HID)]
        d = wd.at[pl.ds(pl.multiple_of(j * HID, 32), HID)]
        yield pltpu.make_async_copy(wb.at[j - 1, pl.ds(0, 2 * HID)], gu, got_sem.at[j - 1, 0])
        yield pltpu.make_async_copy(wb.at[j - 1, pl.ds(2 * HID, HID)], d, got_sem.at[j - 1, 1])

    for j in range(1, 4):
        for copy in got_copies(j):
            copy.start()
    for copy in own_copies():
        copy.start()
    greet(everyone(q, c, t))
    plane = Plane(chunk, recv1, recv2, (s1, r1, s2, r2))

    def feed(i, carry):
        j = (i + 1) & 3

        @pl.when(j > 0)
        def _():
            for copy in got_copies(j):
                copy.wait()

        @pl.when(j == 0)
        def _():
            for copy in own_copies():
                copy.wait()

        gate_rows = pl.ds(pl.multiple_of(j * (2 * HID), 32), HID)
        up_rows = pl.ds(pl.multiple_of(j * (2 * HID) + HID, 32), HID)
        down_rows = pl.ds(pl.multiple_of(j * HID, 32), HID)
        for side, n, cot in ((0, n_own, cot_own), (1, n_oth, cot_oth)):
            for b in range(2):
                rows = slice(b * 256, (b + 1) * 256)
                cols = slice(side * HALF + b * 256, side * HALF + (b + 1) * 256)
                normed = n[rows, :]
                gate = nt(wgu[gate_rows, :], normed)
                up = nt(wgu[up_rows, :], normed)
                grad = nt(wd[down_rows, :], cot[rows, :])
                sig = 1.0 / (1.0 + jnp.exp(-gate))
                silu = gate * sig
                act[down_rows, cols] = (silu * up).astype(BF)
                dgu[gate_rows, cols] = (grad * up * sig * (1.0 + gate * (1.0 - sig))).astype(BF)
                dgu[up_rows, cols] = (grad * silu).astype(BF)
        first, second = plane.order(j)
        both = pl.ds(pl.multiple_of(j * (2 * HID), 32), 2 * HID)
        for slot, k in ((2, first), (3, 3), (0, 0), (1, second)):
            cols = block(k, DP)
            g = nn(dgu[both, 0:HALF], n_own[:, cols]) + nn(dgu[both, HALF:LEN], n_oth[:, cols])
            chunk[j, slot, 0 : 2 * HID, :] = g.astype(BF)
            g = nn(act[down_rows, 0:HALF], cot_own[:, cols]) + nn(act[down_rows, HALF:LEN], cot_oth[:, cols])
            chunk[j, slot, 2 * HID : 3 * HID, :] = g.astype(BF)
            if slot == 0:
                plane.copy1(j).start()

        @pl.when(i == 3)
        def _():
            plane.stage2(1)

        return carry

    lax.fori_loop(0, 4, feed, 0)
    own, oth = slice(0, HALF), slice(HALF, LEN)
    d_send[...] = tn(dgu[:, oth], wgu[...]).astype(BF)
    sends.go(d_send, d_got, pair_send.at[0], pair_recv.at[0], partner)
    plane.stage2(2)
    y_send[...] = tn(act[:, oth], wd[...]).astype(BF)
    sends.go(y_send, y_got, pair_send.at[1], pair_recv.at[1], partner)
    arrived(d_got, pair_recv.at[0], None)
    gain = local_gain(gain_f)
    total = jnp.zeros((1, D), F32)
    for b in range(2):
        rows = slice(b * 256, (b + 1) * 256)
        grad = tn(dgu[:, rows], wgu[...]) + d_got[rows, :].astype(F32)
        back, part = norm_back(grad, hidden[rows, :], gain)
        total = total + part
        g = cot_own[rows, :].astype(F32) + back
        grad_hidden[rows, :] = g
        low_own[rows, :] = g.astype(BF)
    put_gain(gain_two, 0, total)
    plane.stage2(3)
    plane.stage3(1, sums)
    sends.go(low_own, low_oth, pair_send.at[2], pair_recv.at[2], partner)
    arrived(y_got, pair_recv.at[1], None)
    for b in range(2):
        rows = slice(b * 256, (b + 1) * 256)
        rows_buf[rows, :] = (hidden[rows, :] + (tn(act[:, rows], wd[...]) + y_got[rows, :].astype(F32))).astype(BF)
    rows_back(sends, rows_buf, out_rows, row_send, row_recv)
    plane.stage2(0)
    for j in (2, 3, 0):
        plane.stage3(j, sums)
    arrived(low_oth, pair_recv.at[2], None)
    rows_back_in(out_rows, row_recv)
    plane.drain()
    sends.drain()


def middle(*args):
    half16 = ((HALF, D), BF, VM)
    outs = [((4, RB, DP), BF, VM), ((HALF, D), F32, VM), half16, half16, ((MICRO, 256, D), BF, VM), ((1, D), F32, VM)]
    buf = pltpu.VMEM((HALF, D), BF)
    scratch = [
        pltpu.VMEM((4 * 2 * HID, D), BF), pltpu.VMEM((4 * HID, D), BF), pltpu.VMEM((4 * HID, LEN), BF),
        pltpu.VMEM((4 * 2 * HID, LEN), BF), pltpu.VMEM((4, NQ, RB, DP), BF), pltpu.VMEM((4, 2, RB, DP), BF),
        pltpu.VMEM((4, RB, DP), BF), buf, buf, buf, buf, buf,
        DMA((3, 4)), DMA((3, 2)), DMA((4,)), DMA((4,)), DMA((4,)), DMA((4,)), DMA((3,)), DMA((3,)), DMA((2, 4)), DMA((2, 4)),
    ]
    return remote_call(middle_body, "middle", 1, args, [VM] * 6 + [HBM] * 4, outs, scratch, 2.6e10)


class Spread:
    def __init__(self, piece, got, sends, send_sem, recv_sem, odd):
        self.piece, self.got, self.sends, self.ss, self.rs, self.odd = piece, got, sends, send_sem, recv_sem, odd
        _, self.q, self.c, self.t = where_am_i()

    def place(self, k, half):
        return self.got.at[half, :, block(self.q ^ k, DP)]

    def go(self, src, k, number, device, slot):
        self.sends.go(src, self.place(k, self.c), self.ss.at[number], self.rs.at[slot], device)

    def start(self):
        q, c, t = self.q, self.c, self.t
        self.go(self.piece, 0, 1, at(q ^ 1, c, t), 1)
        self.go(self.piece, 0, 2, at(q ^ 2, c, t), 2)
        self.go(self.piece, 0, 4, at(q, 1 - c, t), 4)
        pltpu.make_async_copy(self.piece, self.place(0, c), self.rs.at[0]).start()

    def relay(self):
        q, c, t = self.q, self.c, self.t
        one, two = (1, 2) if self.odd else (2, 1)
        arrived(self.place(one, c), self.rs.at[one], None)
        self.go(self.place(one, c), one, 3, at(q ^ two, c, t), 3)
        self.go(self.place(one, c), one, 4 + one, at(q, 1 - c, t), 4 + one)
        arrived(self.place(two, c), self.rs.at[two], None)
        self.go(self.place(two, c), two, 4 + two, at(q, 1 - c, t), 4 + two)

    def last(self):
        arrived(self.place(3, self.c), self.rs.at[3], None)
        self.go(self.place(3, self.c), 3, 7, at(self.q, 1 - self.c, self.t), 7)

    def finish(self):
        arrived(self.place(0, self.c), self.rs.at[0], None)
        for k in range(NQ):
            arrived(self.place(k, 1 - self.c), self.rs.at[4 + k], None)


def tail_body(low_own, low_oth, n_own, n_oth, x_own, wa, qkv_all, att_all, lse_all, mem_all, grad_hidden, gain_a, gain_two,
              sums_b, grad_rows, got_b, got_a, gains,
              da, dk, dv, dall, chunk, recv1, recv2, sums_a, zb, za, piece_b, piece_a, d_send, d_got, rows_buf, g_send, g_got,
              s1, r1, s2, r2, zb_send, zb_recv, za_send, za_recv, pair_send, pair_recv, row_send, row_recv,
              bs, br, as_, ar, gs, gr):
    _, q, c, t = where_am_i()
    sends = Sends()
    greet(everyone(q, c, t))
    plane = Plane(chunk, recv1, recv2, (s1, r1, s2, r2))
    for j in range(1, 4):
        sends.go(sums_b.at[j], zb.at[j - 1], zb_send.at[j - 1], zb_recv.at[j - 1], at(q, c, t ^ j))

    def z_copy(j):
        return remote(sums_a.at[j], za.at[j - 1], za_send.at[j - 1], za_recv.at[j - 1], at(q, c, t ^ j))

    def attend_back(i, carry):
        j = (i + 1) & 3
        first, second = plane.order(j)
        wo = wa[j, 3 * HD : 4 * HD, :]
        qkv, lse, mem, head = qkv_all.at[j], lse_all.at[j], mem_all.at[j], block(j, HD)
        grad_o = jnp.zeros((HD, D), F32)
        for who, g in ((c, low_own), (1 - c, low_oth)):
            rows = block(who, HALF)
            grads = g[...]
            da[rows, :] = nt(grads, wo).astype(BF)
            grad_o = grad_o + tn(att_all[rows, head], grads)
        keep = causal()
        for b in range(LEN // BLK):
            rows = slice(b * BLK, (b + 1) * BLK)
            query = qkv[rows, 0:HD]
            grad = da[rows, :]
            level = lse[rows, 0:1]
            mem_k = mem[b * TOPK : (b + 1) * TOPK, :]
            mem_v = mem[512 + b * TOPK : 512 + (b + 1) * TOPK, :]
            p_d = jnp.exp(jnp.where(keep, nt(query, qkv[rows, HD : 2 * HD]), NEG) - level)
            p_f = jnp.exp(nt(query, mem_k) - level)
            g_d = nt(grad, qkv[rows, 2 * HD : 3 * HD])
            g_f = nt(grad, mem_v)
            delta = jnp.sum(p_d * g_d, axis=1, keepdims=True) + jnp.sum(p_f * g_f, axis=1, keepdims=True)
            if b:
                past = slice(0, b * BLK)
                p_p = jnp.exp(nt(query, qkv[past, HD : 2 * HD]) - level)
                g_p = nt(grad, qkv[past, 2 * HD : 3 * HD])
                delta = delta + jnp.sum(p_p * g_p, axis=1, keepdims=True)
            s_d = (p_d * (g_d - delta)).astype(BF)
            s_f = (p_f * (g_f - delta)).astype(BF)
            dq = nn(s_d, qkv[rows, HD : 2 * HD]) + nn(s_f, mem_k)
            if b:
                s_p = (p_p * (g_p - delta)).astype(BF)
                dq = dq + nn(s_p, qkv[past, HD : 2 * HD])
                dk[past, :] = dk[past, :] + tn(s_p, query)
                dv[past, :] = dv[past, :] + tn(p_p.astype(BF), grad)
            dk[rows, :] = tn(s_d, query)
            dv[rows, :] = tn(p_d.astype(BF), grad)
            dall[j, rows, 0:HD] = (dq * (HD**-0.5)).astype(BF)
        dall[j, :, HD : 2 * HD] = dk[...].astype(BF)
        dall[j, :, 2 * HD : 3 * HD] = dv[...].astype(BF)
        grad_w = tn(dall[j, block(c, HALF), :], n_own[...]) + tn(dall[j, block(1 - c, HALF), :], n_oth[...])
        for k, slot in ((0, 0), (1, first_slot(first, 1)), (2, first_slot(first, 2)), (3, 3)):
            chunk[j, slot, 0 : 3 * HD, :] = grad_w[:, lanes(k)].astype(BF)
            chunk[j, slot, 3 * HD : 4 * HD, :] = grad_o[:, lanes(k)].astype(BF)

        @pl.when(i >= 2)
        def _():
            plane.stage3(i - 1, sums_a)

        @pl.when(i >= 1)
        def _():
            plane.stage2(i)

        plane.copy1(j).start()

        @pl.when(i >= 2)
        def _():
            z_copy(i - 1).start()

        return carry

    def first_slot(first, k):
        return jnp.where(first == k, 2, 1)

    lax.fori_loop(0, 4, attend_back, 0)
    weights = jnp.concatenate([wa[j, 0 : 3 * HD, :] for j in range(4)], axis=0)

    def into_rows(who, b):
        rows = pl.ds(pl.multiple_of(who * HALF + b * 256, 256), 256)
        d = jnp.concatenate([dall[j, rows, :] for j in range(4)], axis=1)
        return nn(d, weights)

    for b in range(2):
        d_send[b * 256 : (b + 1) * 256, :] = into_rows(1 - c, b).astype(BF)
    sends.go(d_send, d_got, pair_send.at[0], pair_recv.at[0], at(q, 1 - c, t))
    plane.stage3(3, sums_a)
    for j in range(3):
        arrived(zb.at[j], zb_recv.at[j], None)
    piece_b[...] = (((sums_b[0].astype(F32) + zb[0].astype(F32)) + zb[1].astype(F32)) + zb[2].astype(F32)).astype(BF)
    z_copy(3).start()
    arrived(d_got, pair_recv.at[0], None)
    to_b = Spread(piece_b, got_b, sends, bs, br, True)
    to_a = Spread(piece_a, got_a, sends, as_, ar, False)
    plane.stage2(0)
    to_b.start()
    gain = local_gain(gain_a)
    total = jnp.zeros((1, D), F32)
    for b in range(2):
        rows = slice(b * 256, (b + 1) * 256)
        grad = into_rows(c, b) + d_got[rows, :].astype(F32)
        back, part = norm_back(grad, x_own[rows, :].astype(F32), gain)
        total = total + part
        rows_buf[rows, :] = (grad_hidden[rows, :] + back).astype(BF)
    put_gain(gains, 0, total)
    gains[1:2, :] = gain_two[...]
    rows_back(sends, rows_buf, grad_rows, row_send, row_recv)
    plane.stage3(0, sums_a)
    to_b.relay()
    for j in range(3):
        arrived(za.at[j], za_recv.at[j], None)
    piece_a[...] = (((sums_a[0].astype(F32) + za[0].astype(F32)) + za[1].astype(F32)) + za[2].astype(F32)).astype(BF)
    to_a.start()
    for i, device in enumerate((at(q, 1 - c, t), at(q ^ 1, c, t), at(q ^ 2, c, t), at(q, c, t ^ 1), at(q, c, t ^ 2))):
        g_send[i] = gains[...]
        sends.go(g_send.at[i], g_got.at[i], gs.at[i], gr.at[i], device)
        arrived(g_got.at[i], gr.at[i], None)
        gains[...] = gains[...] + g_got[i]
    to_b.last()
    to_a.relay()
    to_a.last()
    to_b.finish()
    to_a.finish()
    rows_back_in(grad_rows, row_recv)
    plane.drain()
    for j in range(1, 4):
        z_copy(j).wait_send()
    sends.drain()


def tail(*args):
    outs = [((MICRO, 256, D), BF, VM), ((2, RB, D), BF, HBM), ((2, RA, D), BF, HBM), ((2, D), F32, VM)]
    buf = pltpu.VMEM((HALF, D), BF)
    scratch = [
        pltpu.VMEM((LEN, HD), BF), pltpu.VMEM((LEN, HD), F32), pltpu.VMEM((LEN, HD), F32), pltpu.VMEM((4, LEN, 3 * HD), BF),
        pltpu.VMEM((4, NQ, RA, DP), BF), pltpu.VMEM((4, 2, RA, DP), BF), pltpu.VMEM((4, RA, DP), BF),
        pltpu.VMEM((4, RA, DP), BF), pltpu.VMEM((3, RB, DP), BF), pltpu.VMEM((3, RA, DP), BF),
        pltpu.VMEM((RB, DP), BF), pltpu.VMEM((RA, DP), BF), buf, buf, buf,
        pltpu.VMEM((5, 2, D), F32), pltpu.VMEM((5, 2, D), F32),
        DMA((4,)), DMA((4,)), DMA((4,)), DMA((4,)), DMA((3,)), DMA((3,)), DMA((3,)), DMA((3,)), DMA((1,)), DMA((1,)),
        DMA((2, 4)), DMA((2, 4)), DMA((8,)), DMA((8,)), DMA((8,)), DMA((8,)), DMA((5,)), DMA((5,)),
    ]
    return remote_call(tail_body, "tail", 2, args, [VM] * 14, outs, scratch, 1.5e10)


def per_device(tokens, attn_gain, ffn_gain, query_weight, key_weight, value_weight, out_weight, gate_weight,
               up_weight, down_weight, cache_keys, cache_values, knn_index, cotangent):
    gain_a, gain_f = attn_gain.reshape(1, D), ffn_gain.reshape(1, D)
    gate_t, up_t = gate_weight.T, up_weight.T
    wa, wb, x_own, n1_own, n1_oth, cot_own, cot_oth, mem, qkv, att, lse, hidden, n2_own, n2_oth = front(
        tokens, cotangent, gain_a, gain_f, cache_keys, cache_values, knn_index, query_weight, key_weight, value_weight,
        out_weight, gate_t, up_t, down_weight,
    )
    sums_b, grad_hidden, low_own, low_oth, output, gain_two = middle(
        n2_own, n2_oth, cot_own, cot_oth, hidden, gain_f, gate_t, up_t, down_weight, wb
    )
    grad_tokens, got_b, got_a, gains = tail(
        low_own, low_oth, n1_own, n1_oth, x_own, wa, qkv, att, lse, mem, grad_hidden, gain_a, gain_two, sums_b
    )
    if lax.axis_size("r") > 1:
        got_b = lax.psum(got_b.astype(F32), "r")
        got_a = lax.psum(got_a.astype(F32), "r")
        gains = lax.psum(gains, "r")
    tall = ((2 * HID, D), F32)
    gg, gu, gd = call(place_b_body, [tall, tall, tall], (got_b,), name="place_b")
    col, row = ((D, 2 * HD), F32), ((2 * HD, D), F32)
    gq, gk, gv, go = call(place_a_body, [col, col, col, row], (got_a,), name="place_a")
    return output, grad_tokens, gq, gk, gv, go, gg.T, gu.T, gd, gains[0], gains[1]


def solution(mesh):
    n_dp, n_t = mesh.shape["dp"], mesh.shape["tensor"]
    fine = Mesh(mesh.devices.reshape(n_dp // 8, NQ, 2, n_t), ("r", "q", "c", "t"))
    dp = ("r", "q", "c")
    rows = P(None, dp + ("t",), None)
    placed = (
        rows, P(), P(), P(None, "t"), P(None, "t"), P(None, "t"), P("t", None), P(None, "t"), P(None, "t"),
        P("t", None), P(None, dp, "t"), P(None, dp, "t"), P(None, dp, "t", None), rows,
    )
    return jax.shard_map(
        per_device,
        mesh=fine,
        in_specs=placed,
        out_specs=(
            rows, rows, P(None, "t"), P(None, "t"), P(None, "t"), P("t", None), P(None, "t"), P(None, "t"),
            P("t", None), P(), P(),
        ),
        check_vma=False,
    )
```

```python
import functools

import jax
import jax.numpy as jnp
from jax import lax
from jax.experimental import pallas as pl
from jax.experimental.pallas import tpu as pltpu
from jax.sharding import Mesh
from jax.sharding import PartitionSpec as P

HEADS = 8
HD = 128
MICRO = 2
BLK = 256
TOPK = 128
CACHE = 256
D = 1024
NQ = 4
DP = D // NQ
HALF = 512
LEN = 1024
HID = 352
RA = 4 * HD
RB = 3 * HID

EPS = 1e-06
NEG = -1e30
BF = jnp.bfloat16
F32 = jnp.float32


def nn(a, b):
    return lax.dot_general(a, b, (((1,), (0,)), ((), ())), preferred_element_type=F32)


def nt(a, b):
    return lax.dot_general(a, b, (((1,), (1,)), ((), ())), preferred_element_type=F32)


def tn(a, b):
    return lax.dot_general(a, b, (((0,), (0,)), ((), ())), preferred_element_type=F32)


VM = pl.BlockSpec(memory_space=pltpu.VMEM)


def call(body, outs, args, flops=0, trans=0, scratch=(), name=None, vmem=None):
    nbytes = sum(a.size * a.dtype.itemsize for a in args) + sum(
        jnp.dtype(t).itemsize * functools.reduce(lambda x, y: x * y, s, 1) for s, t in outs
    )
    return pl.pallas_call(
        body,
        out_shape=[jax.ShapeDtypeStruct(s, t) for s, t in outs],
        in_specs=[VM for _ in args],
        out_specs=[VM for _ in outs],
        scratch_shapes=list(scratch),
        name=name,
        compiler_params=pltpu.CompilerParams(vmem_limit_bytes=vmem),
        cost_estimate=pl.CostEstimate(flops=int(flops), bytes_accessed=int(nbytes), transcendentals=int(trans)),
    )(*args)


def block(index, size):
    return pl.ds(pl.multiple_of(index * size, size), size)


def lanes(k):
    return slice(k * DP, (k + 1) * DP)


def scale_of(x):
    return lax.rsqrt(jnp.mean(x * x, axis=-1, keepdims=True) + EPS)


def norm_back(grad, x, gain):
    scale = scale_of(x)
    scaled = grad * gain
    gain_part = jnp.sum(grad * x * scale, axis=0, keepdims=True)
    back = scale * scaled - x * (scale * scale * scale) * jnp.mean(scaled * x, axis=-1, keepdims=True)
    return back, gain_part


def causal():
    return lax.broadcasted_iota(jnp.int32, (BLK, BLK), 1) <= lax.broadcasted_iota(jnp.int32, (BLK, BLK), 0)


def place_a_body(got, gq, gk, gv, go):
    for half in range(2):
        rows = slice(half * HD, (half + 1) * HD)
        for i, out in enumerate((gq, gk, gv)):
            out[:, rows] = got[half, i * HD : (i + 1) * HD, :].astype(F32).T
        go[rows, :] = got[half, 3 * HD : 4 * HD, :].astype(F32)


def place_b_body(got, *outs):
    for half in range(2):
        for i, out in enumerate(outs):
            out[half * HID : (half + 1) * HID, :] = got[half, i * HID : (i + 1) * HID, :].astype(F32)


def where_am_i():
    return lax.axis_index("r"), lax.axis_index("q"), lax.axis_index("c"), lax.axis_index("t")


def at(q, c, t):
    return {"q": q, "c": c, "t": t}


def dp_at(index):
    return {"r": index // (2 * NQ), "q": lax.rem(index // 2, NQ), "c": lax.rem(index, 2)}


def remote(src, dst, send_sem, recv_sem, device):
    return pltpu.make_async_remote_copy(
        src_ref=src, dst_ref=dst, send_sem=send_sem, recv_sem=recv_sem, device_id=device,
        device_id_type=pl.DeviceIdType.MESH,
    )


def arrived(dst, recv_sem, spare):
    pltpu.make_async_copy(dst, dst, recv_sem).wait()


def greet(devices):
    barrier = pltpu.get_barrier_semaphore()
    for device in devices:
        pl.semaphore_signal(barrier, inc=1, device_id=device, device_id_type=pl.DeviceIdType.MESH)
    pl.semaphore_wait(barrier, len(devices))


class Sends:
    def __init__(self):
        self.open = []

    def go(self, src, dst, send_sem, recv_sem, device, when=None):
        copy = remote(src, dst, send_sem, recv_sem, device)
        self.open.append((copy, when))
        if when is None:
            copy.start()
        else:
            pl.when(when)(copy.start)

    def drain(self):
        for copy, when in self.open:
            if when is None:
                copy.wait_send()
            else:
                pl.when(when)(copy.wait_send)
        self.open = []


def front_body(tok, cot, gain_a, gain_f, ck, cv, knn, wq, wk, wv, wo, gate_t, up_t, down,
               wa, wb, x_own, n_own, n_oth, cot_own, cot_oth, mem, qkv, att, lse, hidden, n2_own, n2_oth,
               prev_k, prev_v, picked, o_send, o_got,
               row_send, row_recv, cot_send, cot_recv, cache_send, cache_recv, mem_send, mem_recv,
               za_send, za_recv, xa_send, xa_recv, zb_send, zb_recv, xb_send, xb_recv, pair_send, pair_recv):
    r, q, c, t = where_am_i()
    count = lax.axis_size("r") * 2 * NQ
    me = (r * NQ + q) * 2 + c
    after = dp_at(lax.rem(me + 1, count))
    across = dp_at(lax.rem(me + jnp.where(c == 0, count - 1, 1), count))
    mid = (t == 1) | (t == 2)
    second, third = jnp.where(mid, 3, 2), jnp.where(mid, 2, 3)
    partner = at(q, 1 - c, t)
    sends = Sends()
    greet(
        [at(q, c, t ^ j) for j in range(1, 4)] + [at(q, 1 - c, t ^ j) for j in range(4)]
        + [at(q ^ 1, c, t), at(q ^ 2, c, t), at(q ^ 3, c, t), across]
    )

    def rows_out(src, dst, send_sem, recv_sem):
        slot = t & 1
        for m in range(MICRO):
            here = (c == (t >> 1)) & (m == slot)
            for k in range(NQ):
                one = src.at[m, :, block(q ^ k, DP)]
                two = dst.at[block(slot, 256), lanes(k)]
                sends.go(one, two, send_sem.at[m, k], recv_sem.at[slot, k], at(q, t >> 1, 2 * c + m),
                         when=jnp.logical_not(here))
                pl.when(here)(pltpu.make_async_copy(one, two, recv_sem.at[slot, k]).start)

    def rows_in(dst, recv_sem):
        for slot in range(2):
            for k in range(NQ):
                arrived(dst.at[slot * 256 : (slot + 1) * 256, lanes(k)], recv_sem.at[slot, k], None)

    near, far_mid = at(q, c, t ^ 1), at(q, c, t ^ 3)
    ends = jnp.logical_not(mid)
    a_piece = [wa.at[0, :, lanes(0)]]
    b_piece = [w.at[pl.ds(pl.multiple_of(c * HID, 32), HID), block(q, DP)] for w in (gate_t, up_t, down)]

    def a_slot(s):
        return [wa.at[s, :, lanes(0)]]

    def b_slot(s):
        return [wb.at[s - 1, i * HID : (i + 1) * HID, lanes(0)] for i in range(3)]

    def z_first(piece, slot, send_sem, recv_sem):
        for i, (one, two) in enumerate(zip(piece, slot(1))):
            sends.go(one, two, send_sem.at[0, i], recv_sem.at[1, i], near)
        for i, (one, two) in enumerate(zip(piece, slot(3))):
            sends.go(one, two, send_sem.at[1, i], recv_sem.at[3, i], far_mid, when=mid)

    def relay_some(order, s, when, slot, whole, z_send, z_recv, x_send, x_recv):
        for i, two in enumerate(slot(s)):
            if when is None:
                arrived(two, z_recv.at[s, i], None)
            else:
                pl.when(when)(functools.partial(arrived, two, z_recv.at[s, i], None))
        if order == 1:
            for i, (one, two) in enumerate(zip(slot(1), slot(2))):
                sends.go(one, two, z_send.at[2, i], z_recv.at[2, i], far_mid, when=mid)
        elif when is mid:
            back = 2 if order == 2 else 3
            for i, (one, two) in enumerate(zip(slot(s), slot(back))):
                sends.go(one, two, z_send.at[order + 1, i], z_recv.at[back, i], near, when=mid)
        for k in (1, 2, 3) if order == 3 else (1, 2):
            sends.go(whole(s, 0), whole(s, k), x_send.at[s, k], x_recv.at[s, k], at(q ^ k, c, t), when=when)

    def relay_far(order, whole, x_send, x_recv):
        s = (None, 1, second)[order]
        arrived(whole(s, order), x_recv.at[s, order], None)
        sends.go(whole(s, order), whole(s, 3), x_send.at[s, 3], x_recv.at[s, 3], at(q ^ (3 - order), c, t))

    def in_place(order, whole, x_recv):
        s = (None, 1, second, third)[order]
        for k in range(1, NQ):
            if k != order or order == 3:
                arrived(whole(s, k), x_recv.at[s, k], None)

    def a_whole(s, k):
        return wa.at[s, :, lanes(k)]

    def b_whole(s, k):
        return wb.at[s - 1, :, lanes(k)]

    relay_a = functools.partial(relay_some, slot=a_slot, whole=a_whole, z_send=za_send, z_recv=za_recv, x_send=xa_send, x_recv=xa_recv)
    relay_b = functools.partial(relay_some, slot=b_slot, whole=b_whole, z_send=zb_send, z_recv=zb_recv, x_send=xb_send, x_recv=xb_recv)

    for i, (one, two) in enumerate(((ck, prev_k), (cv, prev_v))):
        sends.go(one, two, cache_send.at[i], cache_recv.at[i], after)
    for k in range(NQ):
        rows = block(q ^ k, DP)
        for i, w in enumerate((wq, wk, wv)):
            wa[0, i * HD : (i + 1) * HD, lanes(k)] = w[rows, block(c, HD)].T
        wa[0, 3 * HD : 4 * HD, lanes(k)] = wo[block(c, HD), rows]
        if k == 1:
            z_first(a_piece, a_slot, za_send, za_recv)
            z_first(b_piece, b_slot, zb_send, zb_recv)
            rows_out(tok, x_own, row_send, row_recv)

    relay_a(1, 1, None)
    relay_a(2, 3, mid)
    for i, two in enumerate((prev_k, prev_v)):
        arrived(two, cache_recv.at[i], None)

    def pick(i, carry):
        m, h, b = i // 8, (i // 4) % 2, i % 4
        cols = block(h, HD)
        picks = knn[m, b, pl.ds(h, 1), :]
        rows = lax.broadcasted_iota(jnp.int32, (CACHE, TOPK), 0)
        hot_own = jnp.where(rows == picks, 1.0, 0.0).astype(BF)
        hot_prev = jnp.where(rows + CACHE == picks, 1.0, 0.0).astype(BF)
        for kv, own, prev in ((0, ck, prev_k), (1, cv, prev_v)):
            got = tn(hot_own, own[m, :, cols]) + tn(hot_prev, prev[m, :, cols])
            picked[m, h, pl.ds(pl.multiple_of(kv * 512 + b * TOPK, TOPK), TOPK), :] = got.astype(BF)
        return carry

    lax.fori_loop(0, 16, pick, 0)
    relay_b(1, 1, None)
    relay_b(2, 3, mid)
    relay_far(1, a_whole, xa_send, xa_recv)

    def send_mem():
        for m in range(MICRO):
            for h in range(2):
                kind = t ^ (2 * c + m)
                here = (c == h) & (kind == 0)
                sends.go(picked.at[m, h], mem.at[kind], mem_send.at[m, h], mem_recv.at[kind], at(q, h, 2 * c + m),
                         when=jnp.logical_not(here))
                pl.when(here)(pltpu.make_async_copy(picked.at[m, h], mem.at[kind], mem_recv.at[kind]).start)

    relay_far(1, b_whole, xb_send, xb_recv)
    rows_in(x_own, row_recv)
    gain = jnp.concatenate([gain_a[:, block(q ^ k, DP)] for k in range(NQ)], axis=1)
    for i in range(2):
        rows = slice(i * 256, (i + 1) * 256)
        x = x_own[rows, :].astype(F32)
        n_own[rows, :] = (x * scale_of(x) * gain).astype(BF)
    sends.go(n_own, n_oth, pair_send.at[0], pair_recv.at[0], partner)

    def project(j, who, n):
        acc = nt(n[...], wa[j, 0 : 3 * HD, :])
        rows = block(who, HALF)
        qkv[j, rows, 0:HD] = (acc[:, 0:HD] * (HD**-0.5)).astype(BF)
        qkv[j, rows, HD : 3 * HD] = acc[:, HD : 3 * HD].astype(BF)

    def attend(j):
        keep = causal()
        for b in range(LEN // BLK):
            rows = slice(b * BLK, (b + 1) * BLK)
            query = qkv[j, rows, 0:HD]
            diag = jnp.where(keep, nt(query, qkv[j, rows, HD : 2 * HD]), NEG)
            far = nt(query, mem[j, b * TOPK : (b + 1) * TOPK, :])
            top = jnp.maximum(jnp.max(diag, axis=1, keepdims=True), jnp.max(far, axis=1, keepdims=True))
            if b:
                past = nt(query, qkv[j, 0 : b * BLK, HD : 2 * HD])
                top = jnp.maximum(top, jnp.max(past, axis=1, keepdims=True))
            diag = jnp.exp(diag - top)
            far = jnp.exp(far - top)
            total = jnp.sum(diag, axis=1, keepdims=True) + jnp.sum(far, axis=1, keepdims=True)
            if b:
                past = jnp.exp(past - top)
                total = total + jnp.sum(past, axis=1, keepdims=True)
            inverse = 1.0 / total
            out = nn((diag * inverse).astype(BF), qkv[j, rows, 2 * HD : 3 * HD])
            out = out + nn((far * inverse).astype(BF), mem[j, 512 + b * TOPK : 512 + (b + 1) * TOPK, :])
            if b:
                out = out + nn((past * inverse).astype(BF), qkv[j, 0 : b * BLK, 2 * HD : 3 * HD])
            att[rows, block(j, HD)] = out.astype(BF)
            lse[j, rows, :] = jnp.broadcast_to(top + jnp.log(total), (BLK, HD))

    def got_mem(j):
        arrived(mem.at[j], mem_recv.at[j], None)

    project(0, c, n_own)
    arrived(n_oth, pair_recv.at[0], None)
    project(0, 1 - c, n_oth)
    relay_a(2, 2, ends)
    relay_a(3, 2, mid)
    relay_b(2, 2, ends)
    relay_b(3, 2, mid)
    send_mem()
    rows_out(cot, cot_own, cot_send, cot_recv)
    relay_far(2, a_whole, xa_send, xa_recv)
    in_place(1, a_whole, xa_recv)
    project(1, c, n_own)
    project(1, 1 - c, n_oth)
    got_mem(0)
    attend(0)
    relay_far(2, b_whole, xb_send, xb_recv)
    relay_a(3, 3, ends)
    relay_b(3, 3, ends)
    in_place(2, a_whole, xa_recv)
    project(second, c, n_own)
    project(second, 1 - c, n_oth)
    got_mem(1)
    attend(1)
    in_place(3, a_whole, xa_recv)
    project(third, c, n_own)
    project(third, 1 - c, n_oth)
    got_mem(second)
    attend(second)
    got_mem(third)
    attend(third)

    weights = jnp.concatenate([wa[j, 3 * HD : 4 * HD, :] for j in range(4)], axis=0)
    o_send[...] = nn(att[block(1 - c, HALF), :], weights).astype(BF)
    sends.go(o_send, o_got, pair_send.at[1], pair_recv.at[1], partner)
    hidden[...] = nn(att[block(c, HALF), :], weights)
    rows_in(cot_own, cot_recv)
    sends.go(cot_own, cot_oth, pair_send.at[2], pair_recv.at[2], partner)
    arrived(o_got, pair_recv.at[1], None)
    gain = jnp.concatenate([gain_f[:, block(q ^ k, DP)] for k in range(NQ)], axis=1)
    for i in range(2):
        rows = slice(i * 256, (i + 1) * 256)
        h = x_own[rows, :].astype(F32) + (hidden[rows, :] + o_got[rows, :].astype(F32))
        hidden[rows, :] = h
        n2_own[rows, :] = (h * scale_of(h) * gain).astype(BF)
    sends.go(n2_own, n2_oth, pair_send.at[3], pair_recv.at[3], partner)
    for order in range(1, 4):
        in_place(order, b_whole, xb_recv)
    arrived(n2_oth, pair_recv.at[3], None)
    arrived(cot_oth, pair_recv.at[2], None)
    sends.drain()


def front(*args):
    hbm = pl.BlockSpec(memory_space=pl.ANY)
    outs = [
        ((4, RA, D), BF, VM), ((3, RB, D), BF, hbm), ((HALF, D), BF, VM), ((HALF, D), BF, VM), ((HALF, D), BF, VM),
        ((HALF, D), BF, hbm), ((HALF, D), BF, hbm), ((4, 1024, HD), BF, VM), ((4, LEN, 3 * HD), BF, VM),
        ((LEN, 4 * HD), BF, VM), ((4, LEN, HD), F32, VM), ((HALF, D), F32, VM), ((HALF, D), BF, VM), ((HALF, D), BF, VM),
    ]
    dma = pltpu.SemaphoreType.DMA
    return pl.pallas_call(
        front_body,
        out_shape=[jax.ShapeDtypeStruct(s, d) for s, d, _ in outs],
        in_specs=[hbm, hbm] + [VM] * 9 + [hbm] * 3,
        out_specs=[m for _, _, m in outs],
        scratch_shapes=[
            pltpu.VMEM((MICRO, CACHE, 256), BF), pltpu.VMEM((MICRO, CACHE, 256), BF),
            pltpu.VMEM((MICRO, 2, 1024, HD), BF), pltpu.VMEM((HALF, D), BF), pltpu.VMEM((HALF, D), BF),
            dma((2, 4)), dma((2, 4)), dma((2, 4)), dma((2, 4)), dma((2,)), dma((2,)), dma((2, 2)), dma((4,)),
            dma((5, 1)), dma((4, 1)), dma((4, 4)), dma((4, 4)), dma((5, 3)), dma((4, 3)), dma((4, 4)), dma((4, 4)),
            dma((4,)), dma((4,)),
        ],
        compiler_params=pltpu.CompilerParams(collective_id=0, has_side_effects=True, vmem_limit_bytes=60 << 20),
        name="front",
        cost_estimate=pl.CostEstimate(flops=int(2e10), bytes_accessed=int(5e7), transcendentals=0),
    )(*args)


def everyone(q, c, t):
    return (
        [at(q, c, t ^ j) for j in range(1, 4)] + [at(q, 1 - c, t ^ j) for j in range(4)]
        + [at(q ^ 1, c, t), at(q ^ 2, c, t)]
    )


def add_low(a, b):
    return (a.astype(F32) + b.astype(F32)).astype(BF)


def turn(i):
    return jnp.where(i < 2, 2 * i + 1, 6 - 2 * i)


def slot_of(p, k):
    return (0, (2, 1)[p], (1, 2)[p], 3)[k]


class Plane:
    def __init__(self, chunk, recv1, recv2, sems):
        self.chunk, self.recv1, self.recv2 = chunk, recv1, recv2
        self.s1, self.r1, self.s2, self.r2 = sems
        _, self.q, self.c, self.t = where_am_i()

    def copy1(self, j, p):
        return remote(self.chunk.at[j, p, pl.ds(2, 2)], self.recv1.at[j, p], self.s1.at[j, p], self.r1.at[j, p],
                      at(self.q ^ (1 + p), self.c, self.t))

    def copy2(self, j, p):
        return remote(self.chunk.at[j, p, 1], self.recv2.at[j, p], self.s2.at[j, p], self.r2.at[j, p],
                      at(self.q ^ (2 - p), self.c, self.t))

    def start(self, j):
        for p in range(2):
            self.copy1(j, p).start()

    def stage2(self, j):
        for p in range(2):
            arrived(self.recv1.at[j, p], self.r1.at[j, p], None)
            self.chunk[j, p, 1] = add_low(self.chunk[j, p, 1], self.recv1[j, p, 1])
        self.chunk[j, 0, 0] = add_low(self.chunk[j, 0, 0], self.recv1[j, 0, 0])
        for p in range(2):
            self.copy2(j, p).start()
        self.chunk[j, 1, 0] = add_low(self.chunk[j, 1, 0], self.recv1[j, 1, 0])

    def stage3(self, j, out):
        half = self.chunk.shape[3]
        for p in range(2):
            arrived(self.recv2.at[j, p], self.r2.at[j, p], None)
            out[p * half : (p + 1) * half, :] = add_low(self.chunk[j, p, 0], self.recv2[j, p])

    def drain(self):
        for j in range(4):
            for p in range(2):
                self.copy1(j, p).wait_send()
                self.copy2(j, p).wait_send()


def rows_back(sends, src, dst, send_sem, recv_sem, slots=(0, 1)):
    _, q, c, t = where_am_i()
    m = t & 1
    for s in slots:
        here = (c == (t >> 1)) & (s == m)
        for k in range(NQ):
            one = src.at[s * 256 : (s + 1) * 256, lanes(k)]
            two = dst.at[m, :, block(q ^ k, DP)]
            sends.go(one, two, send_sem.at[s, k], recv_sem.at[m, k], at(q, t >> 1, 2 * c + s),
                     when=jnp.logical_not(here))
            pl.when(here)(pltpu.make_async_copy(one, two, recv_sem.at[m, k]).start)


def rows_back_in(dst, recv_sem):
    _, q, _, _ = where_am_i()
    for m in range(2):
        for k in range(NQ):
            arrived(dst.at[m, :, block(q ^ k, DP)], recv_sem.at[m, k], None)


def put_gain(out, row, total):
    _, q, _, _ = where_am_i()
    for k in range(NQ):
        out[row : row + 1, block(q ^ k, DP)] = total[:, lanes(k)]


def local_gain(gain):
    _, q, _, _ = where_am_i()
    return jnp.concatenate([gain[:, block(q ^ k, DP)] for k in range(NQ)], axis=1)


DMA = pltpu.SemaphoreType.DMA
HBM = pl.BlockSpec(memory_space=pl.ANY)


def remote_call(body, name, number, args, places, outs, scratch, flops):
    return pl.pallas_call(
        body,
        out_shape=[jax.ShapeDtypeStruct(s, d) for s, d, _ in outs],
        in_specs=list(places),
        out_specs=[m for _, _, m in outs],
        scratch_shapes=list(scratch),
        compiler_params=pltpu.CompilerParams(collective_id=number, has_side_effects=True, vmem_limit_bytes=62 << 20),
        name=name,
        cost_estimate=pl.CostEstimate(flops=int(flops), bytes_accessed=int(5e7), transcendentals=0),
    )(*args)


def middle_body(n_own, n_oth, cot_own, cot_oth, hidden, gain_f, gate_t, up_t, down, wb,
                sums, grad_hidden, low_own, low_oth, out_rows, gain_two,
                wgu, wd, act, dgu, chunk, recv1, recv2, z_out, z_in, d_send, d_got, y_send, y_got, rows_buf,
                own_sem, got_sem, s1, r1, s2, r2, z_send, z_recv, pair_send, pair_recv, row_send, row_recv):
    _, q, c, t = where_am_i()
    partner = at(q, 1 - c, t)
    sends = Sends()

    def own_copies():
        rows = pl.ds(pl.multiple_of(c * HID, 32), HID)
        for k in range(NQ):
            for i, (w, two) in enumerate(((gate_t, wgu.at[0:HID, lanes(k)]), (up_t, wgu.at[HID : 2 * HID, lanes(k)]),
                                          (down, wd.at[0:HID, lanes(k)]))):
                yield pltpu.make_async_copy(w.at[rows, block(q ^ k, DP)], two, own_sem.at[i, k])

    def got_copies(j):
        gu = wgu.at[pl.ds(pl.multiple_of(j * (2 * HID), 32), 2 * HID)]
        d = wd.at[pl.ds(pl.multiple_of(j * HID, 32), HID)]
        yield pltpu.make_async_copy(wb.at[j - 1, pl.ds(0, 2 * HID)], gu, got_sem.at[j - 1, 0])
        yield pltpu.make_async_copy(wb.at[j - 1, pl.ds(2 * HID, HID)], d, got_sem.at[j - 1, 1])

    for j in range(1, 4):
        for copy in got_copies(j):
            copy.start()
    for copy in own_copies():
        copy.start()
    greet(everyone(q, c, t))
    plane = Plane(chunk, recv1, recv2, (s1, r1, s2, r2))

    def feed(i, carry):
        j = turn(i)

        @pl.when(j > 0)
        def _():
            for copy in got_copies(j):
                copy.wait()

        @pl.when(j == 0)
        def _():
            for copy in own_copies():
                copy.wait()

        gate_rows = pl.ds(pl.multiple_of(j * (2 * HID), 32), HID)
        up_rows = pl.ds(pl.multiple_of(j * (2 * HID) + HID, 32), HID)
        down_rows = pl.ds(pl.multiple_of(j * HID, 32), HID)
        for side, n, cot in ((0, n_own, cot_own), (1, n_oth, cot_oth)):
            for b in range(2):
                rows = slice(b * 256, (b + 1) * 256)
                cols = slice(side * HALF + b * 256, side * HALF + (b + 1) * 256)
                normed = n[rows, :]
                gate = nt(wgu[gate_rows, :], normed)
                up = nt(wgu[up_rows, :], normed)
                grad = nt(wd[down_rows, :], cot[rows, :])
                sig = 1.0 / (1.0 + jnp.exp(-gate))
                silu = gate * sig
                act[down_rows, cols] = (silu * up).astype(BF)
                dgu[gate_rows, cols] = (grad * up * sig * (1.0 + gate * (1.0 - sig))).astype(BF)
                dgu[up_rows, cols] = (grad * silu).astype(BF)
        both = pl.ds(pl.multiple_of(j * (2 * HID), 32), 2 * HID)
        half = RB // 2
        rest = 2 * HID - half
        for k in (3, 1, 2, 0):
            one, two = slot_of(0, k), slot_of(1, k)
            g = nn(dgu[both, 0:HALF], n_own[:, lanes(k)]) + nn(dgu[both, HALF:LEN], n_oth[:, lanes(k)])
            chunk[j, 0, one, :, :] = g[0:half].astype(BF)
            chunk[j, 1, two, 0:rest, :] = g[half:].astype(BF)
            if k == 0:
                plane.start(j)
            g = nn(act[down_rows, 0:HALF], cot_own[:, lanes(k)]) + nn(act[down_rows, HALF:LEN], cot_oth[:, lanes(k)])
            chunk[j, 1, two, rest:half, :] = g.astype(BF)

        @pl.when(i == 2)
        def _():
            plane.stage2(1)

        @pl.when(i == 3)
        def _():
            plane.stage2(3)

        return carry

    lax.fori_loop(0, 4, feed, 0)
    own, oth = slice(0, HALF), slice(HALF, LEN)
    d_send[...] = tn(dgu[:, oth], wgu[...]).astype(BF)
    sends.go(d_send, d_got, pair_send.at[0], pair_recv.at[0], partner)
    y_send[...] = tn(act[:, oth], wd[...]).astype(BF)
    sends.go(y_send, y_got, pair_send.at[1], pair_recv.at[1], partner)
    arrived(d_got, pair_recv.at[0], None)
    gain = local_gain(gain_f)
    total = jnp.zeros((1, D), F32)
    for b in range(2):
        rows = slice(b * 256, (b + 1) * 256)
        grad = tn(dgu[:, rows], wgu[...]) + d_got[rows, :].astype(F32)
        back, part = norm_back(grad, hidden[rows, :], gain)
        total = total + part
        g = cot_own[rows, :].astype(F32) + back
        grad_hidden[rows, :] = g
        low_own[rows, :] = g.astype(BF)
    put_gain(gain_two, 0, total)
    sends.go(low_own, low_oth, pair_send.at[2], pair_recv.at[2], partner)
    arrived(y_got, pair_recv.at[1], None)
    for b in range(2):
        rows = slice(b * 256, (b + 1) * 256)
        rows_buf[rows, :] = (hidden[rows, :] + (tn(act[:, rows], wd[...]) + y_got[rows, :].astype(F32))).astype(BF)
    rows_back(sends, rows_buf, out_rows, row_send, row_recv)
    plane.stage2(2)
    plane.stage3(1, z_out.at[0])
    plane.stage2(0)
    sends.go(z_out.at[0], z_in.at[0], z_send.at[0], z_recv.at[0], at(q, c, t ^ 1))
    plane.stage3(3, z_out.at[1])
    plane.stage3(2, sums.at[1])
    sends.go(z_out.at[1], z_in.at[1], z_send.at[1], z_recv.at[1], at(q, c, t ^ 1))
    plane.stage3(0, sums.at[0])
    for i in range(2):
        arrived(z_in.at[i], z_recv.at[i], None)
        sums[i] = add_low(sums[i], z_in[i])
    arrived(low_oth, pair_recv.at[2], None)
    rows_back_in(out_rows, row_recv)
    plane.drain()
    sends.drain()


def middle(*args):
    half16 = ((HALF, D), BF, VM)
    outs = [((2, RB, DP), BF, VM), ((HALF, D), F32, VM), half16, half16, ((MICRO, 256, D), BF, VM), ((1, D), F32, VM)]
    buf = pltpu.VMEM((HALF, D), BF)
    scratch = [
        pltpu.VMEM((4 * 2 * HID, D), BF), pltpu.VMEM((4 * HID, D), BF), pltpu.VMEM((4 * HID, LEN), BF),
        pltpu.VMEM((4 * 2 * HID, LEN), BF), pltpu.VMEM((4, 2, NQ, RB // 2, DP), BF), pltpu.VMEM((4, 2, 2, RB // 2, DP), BF),
        pltpu.VMEM((4, 2, RB // 2, DP), BF), pltpu.VMEM((2, RB, DP), BF), pltpu.VMEM((2, RB, DP), BF), buf, buf, buf, buf, buf,
        DMA((3, 4)), DMA((3, 2)), DMA((4, 2)), DMA((4, 2)), DMA((4, 2)), DMA((4, 2)), DMA((2,)), DMA((2,)), DMA((3,)), DMA((3,)),
        DMA((2, 4)), DMA((2, 4)),
    ]
    return remote_call(middle_body, "middle", 1, args, [VM] * 6 + [HBM] * 4, outs, scratch, 2.6e10)


class Spread:
    def __init__(self, piece, got, sends, send_sem, recv_sem):
        self.piece, self.got, self.sends, self.ss, self.rs = piece, got, sends, send_sem, recv_sem
        _, self.q, self.c, self.t = where_am_i()

    def place(self, k, half, p=None):
        size = self.got.shape[1] // 2
        rows = pl.ds(0, 2 * size) if p is None else pl.ds(p * size, size)
        return self.got.at[half, rows, block(self.q ^ k, DP)]

    def go(self, src, dst, number, device):
        self.sends.go(src, dst, self.ss.at[number], self.rs.at[number], device)

    def start(self):
        q, c, t = self.q, self.c, self.t
        for k in (1, 2):
            self.go(self.piece, self.place(0, c), k, at(q ^ k, c, t))
        self.go(self.piece, self.place(0, c), 4, at(q, 1 - c, t))
        pltpu.make_async_copy(self.piece, self.place(0, c), self.rs.at[0]).start()

    def relay(self):
        q, c, t = self.q, self.c, self.t
        for p, k, number in ((0, 1, 3), (1, 2, 8)):
            arrived(self.place(k, c), self.rs.at[k], None)
            self.go(self.place(k, c, p), self.place(k, c, p), number, at(q ^ (3 - k), c, t))
            self.go(self.place(k, c), self.place(k, c), 4 + k, at(q, 1 - c, t))

    def last(self):
        for p, number in ((0, 3), (1, 8)):
            arrived(self.place(3, self.c, p), self.rs.at[number], None)
        self.go(self.place(3, self.c), self.place(3, self.c), 7, at(self.q, 1 - self.c, self.t))

    def finish(self):
        arrived(self.place(0, self.c), self.rs.at[0], None)
        for k in range(NQ):
            arrived(self.place(k, 1 - self.c), self.rs.at[4 + k], None)


def tail_body(low_own, low_oth, n_own, n_oth, x_own, wa, qkv_all, att_all, lse_all, mem_all, grad_hidden, gain_a, gain_two,
              sums_b, grad_rows, got_b, got_a, gains,
              da, dk, dv, dall, chunk, recv1, recv2, sums_a, zb, z1, z2, piece_b, piece_a, d_send, d_got, rows_buf, g_near, g_far,
              s1, r1, s2, r2, zb_send, zb_recv, z1_send, z1_recv, z2_send, z2_recv, pair_send, pair_recv, row_send, row_recv,
              bs, br, as_, ar, gs, gr, hs, hr):
    _, q, c, t = where_am_i()
    sends = Sends()
    greet(everyone(q, c, t) + [at(q ^ 3, c, t)])
    plane = Plane(chunk, recv1, recv2, (s1, r1, s2, r2))
    sends.go(sums_b.at[1], zb, zb_send.at[0], zb_recv.at[0], at(q, c, t ^ 2))

    def z_first(i):
        sends.go(sums_a.at[2 * i + 1], z1.at[i], z1_send.at[i], z1_recv.at[i], at(q, c, t ^ 1))

    def attend_back(i, carry):
        j = turn(i)
        wo = wa[j, 3 * HD : 4 * HD, :]
        qkv, lse, mem, head = qkv_all.at[j], lse_all.at[j], mem_all.at[j], block(j, HD)
        grad_o = jnp.zeros((HD, D), F32)
        for who, g in ((c, low_own), (1 - c, low_oth)):
            rows = block(who, HALF)
            grads = g[...]
            da[rows, :] = nt(grads, wo).astype(BF)
            grad_o = grad_o + tn(att_all[rows, head], grads)
        keep = causal()
        for b in range(LEN // BLK):
            rows = slice(b * BLK, (b + 1) * BLK)
            query = qkv[rows, 0:HD]
            grad = da[rows, :]
            level = lse[rows, 0:1]
            mem_k = mem[b * TOPK : (b + 1) * TOPK, :]
            mem_v = mem[512 + b * TOPK : 512 + (b + 1) * TOPK, :]
            p_d = jnp.exp(jnp.where(keep, nt(query, qkv[rows, HD : 2 * HD]), NEG) - level)
            p_f = jnp.exp(nt(query, mem_k) - level)
            g_d = nt(grad, qkv[rows, 2 * HD : 3 * HD])
            g_f = nt(grad, mem_v)
            delta = jnp.sum(p_d * g_d, axis=1, keepdims=True) + jnp.sum(p_f * g_f, axis=1, keepdims=True)
            if b:
                past = slice(0, b * BLK)
                p_p = jnp.exp(nt(query, qkv[past, HD : 2 * HD]) - level)
                g_p = nt(grad, qkv[past, 2 * HD : 3 * HD])
                delta = delta + jnp.sum(p_p * g_p, axis=1, keepdims=True)
            s_d = (p_d * (g_d - delta)).astype(BF)
            s_f = (p_f * (g_f - delta)).astype(BF)
            dq = nn(s_d, qkv[rows, HD : 2 * HD]) + nn(s_f, mem_k)
            if b:
                s_p = (p_p * (g_p - delta)).astype(BF)
                dq = dq + nn(s_p, qkv[past, HD : 2 * HD])
                dk[past, :] = dk[past, :] + tn(s_p, query)
                dv[past, :] = dv[past, :] + tn(p_p.astype(BF), grad)
            dk[rows, :] = tn(s_d, query)
            dv[rows, :] = tn(p_d.astype(BF), grad)
            dall[j, rows, 0:HD] = (dq * (HD**-0.5)).astype(BF)
        dall[j, :, HD : 2 * HD] = dk[...].astype(BF)
        dall[j, :, 2 * HD : 3 * HD] = dv[...].astype(BF)
        grad_w = tn(dall[j, block(c, HALF), :], n_own[...]) + tn(dall[j, block(1 - c, HALF), :], n_oth[...])
        for k in range(NQ):
            one, two = slot_of(0, k), slot_of(1, k)
            chunk[j, 0, one, :, :] = grad_w[0 : 2 * HD, lanes(k)].astype(BF)
            chunk[j, 1, two, 0:HD, :] = grad_w[2 * HD : 3 * HD, lanes(k)].astype(BF)
            chunk[j, 1, two, HD : 2 * HD, :] = grad_o[:, lanes(k)].astype(BF)

        @pl.when(i >= 1)
        def _():
            plane.stage2(turn(i - 1))

        plane.start(j)
        return carry

    lax.fori_loop(0, 4, attend_back, 0)
    weights = jnp.concatenate([wa[j, 0 : 3 * HD, :] for j in range(4)], axis=0)

    def into_rows(who, b):
        rows = pl.ds(pl.multiple_of(who * HALF + b * 256, 256), 256)
        d = jnp.concatenate([dall[j, rows, :] for j in range(4)], axis=1)
        return nn(d, weights)

    for b in range(2):
        d_send[b * 256 : (b + 1) * 256, :] = into_rows(1 - c, b).astype(BF)
    sends.go(d_send, d_got, pair_send.at[0], pair_recv.at[0], at(q, 1 - c, t))
    plane.stage3(1, sums_a.at[1])
    plane.stage3(3, sums_a.at[3])
    z_first(0)
    arrived(d_got, pair_recv.at[0], None)
    to_b = Spread(piece_b, got_b, sends, bs, br)
    to_a = Spread(piece_a, got_a, sends, as_, ar)
    gain = local_gain(gain_a)
    total = jnp.zeros((1, D), F32)
    for b in range(2):
        rows = slice(b * 256, (b + 1) * 256)
        grad = into_rows(c, b) + d_got[rows, :].astype(F32)
        back, part = norm_back(grad, x_own[rows, :].astype(F32), gain)
        total = total + part
        rows_buf[rows, :] = (grad_hidden[rows, :] + back).astype(BF)
        if b == 0:
            z_first(1)
            plane.stage2(0)
            arrived(zb, zb_recv.at[0], None)
            piece_b[...] = add_low(sums_b[0], zb[...])
            to_b.start()
    here = c * 4 + t
    put_gain(g_near.at[here], 0, total)
    g_near[here, 1:2, :] = gain_two[...]
    group = [(dc, dt) for dc in range(2) for dt in range(4) if dc + dt]
    for i, (dc, dt) in enumerate(group):
        sends.go(g_near.at[here], g_near.at[here], gs.at[i], gr.at[here], at(q, c ^ dc, t ^ dt))
    rows_back(sends, rows_buf, grad_rows, row_send, row_recv, (0,))
    plane.stage3(2, sums_a.at[2])
    arrived(z1.at[1], z1_recv.at[1], None)
    sums_a[2] = add_low(sums_a[2], z1[1])
    for dc, dt in group:
        there = (c ^ dc) * 4 + (t ^ dt)
        arrived(g_near.at[there], gr.at[there], None)
    sends.go(sums_a.at[2], z2, z2_send.at[0], z2_recv.at[0], at(q, c, t ^ 2))
    rows_back(sends, rows_buf, grad_rows, row_send, row_recv, (1,))
    part = g_near[0]
    for i in range(1, 8):
        part = part + g_near[i]
    g_far[q] = part
    for k in range(1, NQ):
        sends.go(g_far.at[q], g_far.at[q], hs.at[k], hr.at[q], at(q ^ k, c, t))
    plane.stage3(0, sums_a.at[0])
    to_b.relay()
    arrived(z1.at[0], z1_recv.at[0], None)
    arrived(z2, z2_recv.at[0], None)
    piece_a[...] = ((sums_a[0].astype(F32) + z1[0].astype(F32)) + z2[...].astype(F32)).astype(BF)
    to_a.start()
    to_b.last()
    for k in range(1, NQ):
        arrived(g_far.at[q ^ k], hr.at[q ^ k], None)
    gains[...] = ((g_far[0] + g_far[1]) + g_far[2]) + g_far[3]
    to_a.relay()
    to_a.last()
    to_b.finish()
    to_a.finish()
    rows_back_in(grad_rows, row_recv)
    plane.drain()
    sends.drain()


def tail(*args):
    outs = [((MICRO, 256, D), BF, VM), ((2, RB, D), BF, HBM), ((2, RA, D), BF, HBM), ((2, D), F32, VM)]
    buf = pltpu.VMEM((HALF, D), BF)
    scratch = [
        pltpu.VMEM((LEN, HD), BF), pltpu.VMEM((LEN, HD), F32), pltpu.VMEM((LEN, HD), F32), pltpu.VMEM((4, LEN, 3 * HD), BF),
        pltpu.VMEM((4, 2, NQ, RA // 2, DP), BF), pltpu.VMEM((4, 2, 2, RA // 2, DP), BF), pltpu.VMEM((4, 2, RA // 2, DP), BF),
        pltpu.VMEM((4, RA, DP), BF), pltpu.VMEM((RB, DP), BF), pltpu.VMEM((2, RA, DP), BF), pltpu.VMEM((RA, DP), BF),
        pltpu.VMEM((RB, DP), BF), pltpu.VMEM((RA, DP), BF), buf, buf, buf,
        pltpu.VMEM((8, 2, D), F32), pltpu.VMEM((NQ, 2, D), F32),
        DMA((4, 2)), DMA((4, 2)), DMA((4, 2)), DMA((4, 2)), DMA((1,)), DMA((1,)), DMA((2,)), DMA((2,)), DMA((1,)), DMA((1,)),
        DMA((1,)), DMA((1,)), DMA((2, 4)), DMA((2, 4)), DMA((9,)), DMA((9,)), DMA((9,)), DMA((9,)), DMA((7,)), DMA((8,)),
        DMA((4,)), DMA((4,)),
    ]
    return remote_call(tail_body, "tail", 2, args, [VM] * 14, outs, scratch, 1.5e10)


def per_device(tokens, attn_gain, ffn_gain, query_weight, key_weight, value_weight, out_weight, gate_weight,
               up_weight, down_weight, cache_keys, cache_values, knn_index, cotangent):
    gain_a, gain_f = attn_gain.reshape(1, D), ffn_gain.reshape(1, D)
    gate_t, up_t = gate_weight.T, up_weight.T
    wa, wb, x_own, n1_own, n1_oth, cot_own, cot_oth, mem, qkv, att, lse, hidden, n2_own, n2_oth = front(
        tokens, cotangent, gain_a, gain_f, cache_keys, cache_values, knn_index, query_weight, key_weight, value_weight,
        out_weight, gate_t, up_t, down_weight,
    )
    sums_b, grad_hidden, low_own, low_oth, output, gain_two = middle(
        n2_own, n2_oth, cot_own, cot_oth, hidden, gain_f, gate_t, up_t, down_weight, wb
    )
    grad_tokens, got_b, got_a, gains = tail(
        low_own, low_oth, n1_own, n1_oth, x_own, wa, qkv, att, lse, mem, grad_hidden, gain_a, gain_two, sums_b
    )
    if lax.axis_size("r") > 1:
        got_b = lax.psum(got_b.astype(F32), "r")
        got_a = lax.psum(got_a.astype(F32), "r")
        gains = lax.psum(gains, "r")
    tall = ((2 * HID, D), F32)
    gg, gu, gd = call(place_b_body, [tall, tall, tall], (got_b,), name="place_b")
    col, row = ((D, 2 * HD), F32), ((2 * HD, D), F32)
    gq, gk, gv, go = call(place_a_body, [col, col, col, row], (got_a,), name="place_a")
    return output, grad_tokens, gq, gk, gv, go, gg.T, gu.T, gd, gains[0], gains[1]


def solution(mesh):
    n_dp, n_t = mesh.shape["dp"], mesh.shape["tensor"]
    fine = Mesh(mesh.devices.reshape(n_dp // 8, NQ, 2, n_t), ("r", "q", "c", "t"))
    dp = ("r", "q", "c")
    rows = P(None, dp + ("t",), None)
    placed = (
        rows, P(), P(), P(None, "t"), P(None, "t"), P(None, "t"), P("t", None), P(None, "t"), P(None, "t"),
        P("t", None), P(None, dp, "t"), P(None, dp, "t"), P(None, dp, "t", None), rows,
    )
    return jax.shard_map(
        per_device,
        mesh=fine,
        in_specs=placed,
        out_specs=(
            rows, rows, P(None, "t"), P(None, "t"), P(None, "t"), P("t", None), P(None, "t"), P(None, "t"),
            P("t", None), P(), P(),
        ),
        check_vma=False,
    )
```

```python
import functools

import jax
import jax.numpy as jnp
from jax import lax
from jax.experimental import pallas as pl
from jax.experimental.pallas import tpu as pltpu
from jax.sharding import Mesh
from jax.sharding import PartitionSpec as P

HEADS = 8
HD = 128
MICRO = 2
BLK = 256
TOPK = 128
CACHE = 256
D = 1024
NQ = 4
DP = D // NQ
HALF = 512
LEN = 1024
HID = 352
RA = 4 * HD
RB = 3 * HID

EPS = 1e-06
NEG = -1e30
BF = jnp.bfloat16
F32 = jnp.float32


def nn(a, b):
    return lax.dot_general(a, b, (((1,), (0,)), ((), ())), preferred_element_type=F32)


def nt(a, b):
    return lax.dot_general(a, b, (((1,), (1,)), ((), ())), preferred_element_type=F32)


def tn(a, b):
    return lax.dot_general(a, b, (((0,), (0,)), ((), ())), preferred_element_type=F32)


VM = pl.BlockSpec(memory_space=pltpu.VMEM)


def block(index, size):
    return pl.ds(pl.multiple_of(index * size, size), size)


def lanes(k):
    return slice(k * DP, (k + 1) * DP)


def scale_of(x):
    return lax.rsqrt(jnp.mean(x * x, axis=-1, keepdims=True) + EPS)


def norm_back(grad, x, gain):
    scale = scale_of(x)
    scaled = grad * gain
    gain_part = jnp.sum(grad * x * scale, axis=0, keepdims=True)
    back = scale * scaled - x * (scale * scale * scale) * jnp.mean(scaled * x, axis=-1, keepdims=True)
    return back, gain_part


def causal():
    return lax.broadcasted_iota(jnp.int32, (BLK, BLK), 1) <= lax.broadcasted_iota(jnp.int32, (BLK, BLK), 0)


def place_a_body(got, gq, gk, gv, go):
    for half in range(2):
        rows = slice(half * HD, (half + 1) * HD)
        for i, out in enumerate((gq, gk, gv)):
            out[:, rows] = got[half, i * HD : (i + 1) * HD, :].astype(F32).T
        go[rows, :] = got[half, 3 * HD : 4 * HD, :].astype(F32)


def place_b_body(got, *outs):
    for half in range(2):
        for i, out in enumerate(outs):
            out[half * HID : (half + 1) * HID, :] = got[half, i * HID : (i + 1) * HID, :].astype(F32)


def place(body, got, kinds, name):
    shapes = {"tall": (2 * HID, D), "col": (D, 2 * HD), "row": (2 * HD, D)}
    specs = {
        "tall": pl.BlockSpec((2 * HID, DP), lambda i: (0, i)),
        "col": pl.BlockSpec((DP, 2 * HD), lambda i: (i, 0)),
        "row": pl.BlockSpec((2 * HD, DP), lambda i: (0, i)),
    }
    return pl.pallas_call(
        body,
        grid=(NQ,),
        out_shape=[jax.ShapeDtypeStruct(shapes[k], F32) for k in kinds],
        in_specs=[pl.BlockSpec((*got.shape[:2], DP), lambda i: (0, 0, i))],
        out_specs=[specs[k] for k in kinds],
        name=name,
        cost_estimate=pl.CostEstimate(flops=0, bytes_accessed=int(got.size * 6), transcendentals=0),
    )(got)


def where_am_i():
    return lax.axis_index("r"), lax.axis_index("q"), lax.axis_index("c"), lax.axis_index("t")


def at(q, c, t):
    return {"q": q, "c": c, "t": t}


def dp_at(index):
    return {"r": index // (2 * NQ), "q": lax.rem(index // 2, NQ), "c": lax.rem(index, 2)}


def remote(src, dst, send_sem, recv_sem, device):
    return pltpu.make_async_remote_copy(
        src_ref=src, dst_ref=dst, send_sem=send_sem, recv_sem=recv_sem, device_id=device,
        device_id_type=pl.DeviceIdType.MESH,
    )


def arrived(dst, recv_sem, spare):
    pltpu.make_async_copy(dst, dst, recv_sem).wait()


def greet(devices):
    barrier = pltpu.get_barrier_semaphore()
    for device in devices:
        pl.semaphore_signal(barrier, inc=1, device_id=device, device_id_type=pl.DeviceIdType.MESH)
    pl.semaphore_wait(barrier, len(devices))


class Sends:
    def __init__(self):
        self.open = []

    def go(self, src, dst, send_sem, recv_sem, device, when=None):
        copy = remote(src, dst, send_sem, recv_sem, device)
        self.open.append((copy, when))
        if when is None:
            copy.start()
        else:
            pl.when(when)(copy.start)

    def drain(self):
        for copy, when in self.open:
            if when is None:
                copy.wait_send()
            else:
                pl.when(when)(copy.wait_send)
        self.open = []


def front_body(tok, cot, gain_a, gain_f, ck, cv, knn, wq, wk, wv, wo, gate_t, up_t, down,
               wa, wb, x_own, n_own, n_oth, cot_own, cot_oth, mem, qkv, att, lse, hidden, n2_own, n2_oth,
               prev_k, prev_v, picked, o_send, o_got,
               row_send, row_recv, cot_send, cot_recv, cache_send, cache_recv, mem_send, mem_recv,
               za_send, za_recv, xa_send, xa_recv, zb_send, zb_recv, xb_send, xb_recv, pair_send, pair_recv):
    r, q, c, t = where_am_i()
    count = lax.axis_size("r") * 2 * NQ
    me = (r * NQ + q) * 2 + c
    after = dp_at(lax.rem(me + 1, count))
    across = dp_at(lax.rem(me + jnp.where(c == 0, count - 1, 1), count))
    mid = (t == 1) | (t == 2)
    second, third = jnp.where(mid, 3, 2), jnp.where(mid, 2, 3)
    partner = at(q, 1 - c, t)
    sends = Sends()
    greet(
        [at(q, c, t ^ j) for j in range(1, 4)] + [at(q, 1 - c, t ^ j) for j in range(4)]
        + [at(q ^ 1, c, t), at(q ^ 2, c, t), at(q ^ 3, c, t), across]
    )

    def rows_out(src, dst, send_sem, recv_sem):
        slot = t & 1
        for m in range(MICRO):
            here = (c == (t >> 1)) & (m == slot)
            for k in range(NQ):
                one = src.at[m, :, block(q ^ k, DP)]
                two = dst.at[block(slot, 256), lanes(k)]
                sends.go(one, two, send_sem.at[m, k], recv_sem.at[slot, k], at(q, t >> 1, 2 * c + m),
                         when=jnp.logical_not(here))
                pl.when(here)(pltpu.make_async_copy(one, two, recv_sem.at[slot, k]).start)

    def rows_in(dst, recv_sem):
        for slot in range(2):
            for k in range(NQ):
                arrived(dst.at[slot * 256 : (slot + 1) * 256, lanes(k)], recv_sem.at[slot, k], None)

    near, far_mid = at(q, c, t ^ 1), at(q, c, t ^ 3)
    ends = jnp.logical_not(mid)
    a_piece = [wa.at[0, :, lanes(0)]]
    b_piece = [w.at[pl.ds(pl.multiple_of(c * HID, 32), HID), block(q, DP)] for w in (gate_t, up_t, down)]

    def a_slot(s):
        return [wa.at[s, :, lanes(0)]]

    def b_slot(s):
        return [wb.at[s - 1, i * HID : (i + 1) * HID, lanes(0)] for i in range(3)]

    def z_first(piece, slot, send_sem, recv_sem):
        for i, (one, two) in enumerate(zip(piece, slot(1))):
            sends.go(one, two, send_sem.at[0, i], recv_sem.at[1, i], near)
        for i, (one, two) in enumerate(zip(piece, slot(3))):
            sends.go(one, two, send_sem.at[1, i], recv_sem.at[3, i], far_mid, when=mid)

    def relay_some(order, s, when, slot, whole, z_send, z_recv, x_send, x_recv):
        for i, two in enumerate(slot(s)):
            if when is None:
                arrived(two, z_recv.at[s, i], None)
            else:
                pl.when(when)(functools.partial(arrived, two, z_recv.at[s, i], None))
        if order == 1:
            for i, (one, two) in enumerate(zip(slot(1), slot(2))):
                sends.go(one, two, z_send.at[2, i], z_recv.at[2, i], far_mid, when=mid)
        elif when is mid:
            back = 2 if order == 2 else 3
            for i, (one, two) in enumerate(zip(slot(s), slot(back))):
                sends.go(one, two, z_send.at[order + 1, i], z_recv.at[back, i], near, when=mid)
        for k in (1, 2, 3) if order == 3 else (1, 2):
            sends.go(whole(s, 0), whole(s, k), x_send.at[s, k], x_recv.at[s, k], at(q ^ k, c, t), when=when)

    def relay_far(order, whole, x_send, x_recv):
        s = (None, 1, second)[order]
        arrived(whole(s, order), x_recv.at[s, order], None)
        sends.go(whole(s, order), whole(s, 3), x_send.at[s, 3], x_recv.at[s, 3], at(q ^ (3 - order), c, t))

    def in_place(order, whole, x_recv):
        s = (None, 1, second, third)[order]
        for k in range(1, NQ):
            if k != order or order == 3:
                arrived(whole(s, k), x_recv.at[s, k], None)

    def a_whole(s, k):
        return wa.at[s, :, lanes(k)]

    def b_whole(s, k):
        return wb.at[s - 1, :, lanes(k)]

    relay_a = functools.partial(relay_some, slot=a_slot, whole=a_whole, z_send=za_send, z_recv=za_recv, x_send=xa_send, x_recv=xa_recv)
    relay_b = functools.partial(relay_some, slot=b_slot, whole=b_whole, z_send=zb_send, z_recv=zb_recv, x_send=xb_send, x_recv=xb_recv)

    for i, (one, two) in enumerate(((ck, prev_k), (cv, prev_v))):
        sends.go(one, two, cache_send.at[i], cache_recv.at[i], after)
    for k in range(NQ):
        rows = block(q ^ k, DP)
        for i, w in enumerate((wq, wk, wv)):
            wa[0, i * HD : (i + 1) * HD, lanes(k)] = w[rows, block(c, HD)].T
        wa[0, 3 * HD : 4 * HD, lanes(k)] = wo[block(c, HD), rows]
        if k == 1:
            z_first(a_piece, a_slot, za_send, za_recv)
            z_first(b_piece, b_slot, zb_send, zb_recv)
            rows_out(tok, x_own, row_send, row_recv)

    relay_a(1, 1, None)
    relay_a(2, 3, mid)
    for i, two in enumerate((prev_k, prev_v)):
        arrived(two, cache_recv.at[i], None)

    def pick(i, carry):
        m, h, b = i // 8, (i // 4) % 2, i % 4
        cols = block(h, HD)
        picks = knn[m, b, pl.ds(h, 1), :]
        rows = lax.broadcasted_iota(jnp.int32, (CACHE, TOPK), 0)
        hot_own = jnp.where(rows == picks, 1.0, 0.0).astype(BF)
        hot_prev = jnp.where(rows + CACHE == picks, 1.0, 0.0).astype(BF)
        for kv, own, prev in ((0, ck, prev_k), (1, cv, prev_v)):
            got = tn(hot_own, own[m, :, cols]) + tn(hot_prev, prev[m, :, cols])
            picked[m, h, pl.ds(pl.multiple_of(kv * 512 + b * TOPK, TOPK), TOPK), :] = got.astype(BF)
        return carry

    lax.fori_loop(0, 16, pick, 0)
    relay_b(1, 1, None)
    relay_b(2, 3, mid)
    relay_far(1, a_whole, xa_send, xa_recv)

    def send_mem():
        for m in range(MICRO):
            for h in range(2):
                kind = t ^ (2 * c + m)
                here = (c == h) & (kind == 0)
                sends.go(picked.at[m, h], mem.at[kind], mem_send.at[m, h], mem_recv.at[kind], at(q, h, 2 * c + m),
                         when=jnp.logical_not(here))
                pl.when(here)(pltpu.make_async_copy(picked.at[m, h], mem.at[kind], mem_recv.at[kind]).start)

    relay_far(1, b_whole, xb_send, xb_recv)
    rows_in(x_own, row_recv)
    gain = jnp.concatenate([gain_a[:, block(q ^ k, DP)] for k in range(NQ)], axis=1)
    for i in range(2):
        rows = slice(i * 256, (i + 1) * 256)
        x = x_own[rows, :].astype(F32)
        n_own[rows, :] = (x * scale_of(x) * gain).astype(BF)
    sends.go(n_own, n_oth, pair_send.at[0], pair_recv.at[0], partner)

    def project(j, who, n):
        acc = nt(n[...], wa[j, 0 : 3 * HD, :])
        rows = block(who, HALF)
        qkv[j, rows, 0:HD] = (acc[:, 0:HD] * (HD**-0.5)).astype(BF)
        qkv[j, rows, HD : 3 * HD] = acc[:, HD : 3 * HD].astype(BF)

    def attend(j):
        keep = causal()
        for b in range(LEN // BLK):
            rows = slice(b * BLK, (b + 1) * BLK)
            query = qkv[j, rows, 0:HD]
            diag = jnp.where(keep, nt(query, qkv[j, rows, HD : 2 * HD]), NEG)
            far = nt(query, mem[j, b * TOPK : (b + 1) * TOPK, :])
            top = jnp.maximum(jnp.max(diag, axis=1, keepdims=True), jnp.max(far, axis=1, keepdims=True))
            if b:
                past = nt(query, qkv[j, 0 : b * BLK, HD : 2 * HD])
                top = jnp.maximum(top, jnp.max(past, axis=1, keepdims=True))
            diag = jnp.exp(diag - top)
            far = jnp.exp(far - top)
            total = jnp.sum(diag, axis=1, keepdims=True) + jnp.sum(far, axis=1, keepdims=True)
            if b:
                past = jnp.exp(past - top)
                total = total + jnp.sum(past, axis=1, keepdims=True)
            inverse = 1.0 / total
            out = nn((diag * inverse).astype(BF), qkv[j, rows, 2 * HD : 3 * HD])
            out = out + nn((far * inverse).astype(BF), mem[j, 512 + b * TOPK : 512 + (b + 1) * TOPK, :])
            if b:
                out = out + nn((past * inverse).astype(BF), qkv[j, 0 : b * BLK, 2 * HD : 3 * HD])
            att[rows, block(j, HD)] = out.astype(BF)
            lse[j, rows, :] = jnp.broadcast_to(top + jnp.log(total), (BLK, HD))

    def got_mem(j):
        arrived(mem.at[j], mem_recv.at[j], None)

    relay_a(2, 2, ends)
    relay_a(3, 2, mid)
    relay_b(2, 2, ends)
    relay_b(3, 2, mid)
    send_mem()
    rows_out(cot, cot_own, cot_send, cot_recv)
    relay_far(2, a_whole, xa_send, xa_recv)
    arrived(n_oth, pair_recv.at[0], None)
    relay_far(2, b_whole, xb_send, xb_recv)
    relay_a(3, 3, ends)
    relay_b(3, 3, ends)

    def head(i, carry):
        j = jnp.where(i < 2, i, jnp.where(i == 2, second, third))
        for order in range(1, 4):
            pl.when(i == order)(functools.partial(in_place, order, a_whole, xa_recv))
        project(j, c, n_own)
        project(j, 1 - c, n_oth)
        got_mem(j)
        attend(j)
        return carry

    lax.fori_loop(0, 4, head, 0)
    weights = jnp.concatenate([wa[j, 3 * HD : 4 * HD, :] for j in range(4)], axis=0)
    o_send[...] = nn(att[block(1 - c, HALF), :], weights).astype(BF)
    sends.go(o_send, o_got, pair_send.at[1], pair_recv.at[1], partner)
    hidden[...] = nn(att[block(c, HALF), :], weights)
    rows_in(cot_own, cot_recv)
    sends.go(cot_own, cot_oth, pair_send.at[2], pair_recv.at[2], partner)
    arrived(o_got, pair_recv.at[1], None)
    gain = jnp.concatenate([gain_f[:, block(q ^ k, DP)] for k in range(NQ)], axis=1)
    for i in range(2):
        rows = slice(i * 256, (i + 1) * 256)
        h = x_own[rows, :].astype(F32) + (hidden[rows, :] + o_got[rows, :].astype(F32))
        hidden[rows, :] = h
        n2_own[rows, :] = (h * scale_of(h) * gain).astype(BF)
    sends.go(n2_own, n2_oth, pair_send.at[3], pair_recv.at[3], partner)
    for order in range(1, 4):
        in_place(order, b_whole, xb_recv)
    arrived(n2_oth, pair_recv.at[3], None)
    arrived(cot_oth, pair_recv.at[2], None)
    sends.drain()


def front(*args):
    hbm = pl.BlockSpec(memory_space=pl.ANY)
    outs = [
        ((4, RA, D), BF, VM), ((3, RB, D), BF, hbm), ((HALF, D), BF, VM), ((HALF, D), BF, VM), ((HALF, D), BF, VM),
        ((HALF, D), BF, hbm), ((HALF, D), BF, hbm), ((4, 1024, HD), BF, VM), ((4, LEN, 3 * HD), BF, VM),
        ((LEN, 4 * HD), BF, VM), ((4, LEN, HD), F32, VM), ((HALF, D), F32, VM), ((HALF, D), BF, VM), ((HALF, D), BF, VM),
    ]
    dma = pltpu.SemaphoreType.DMA
    return pl.pallas_call(
        front_body,
        out_shape=[jax.ShapeDtypeStruct(s, d) for s, d, _ in outs],
        in_specs=[hbm, hbm] + [VM] * 9 + [hbm] * 3,
        out_specs=[m for _, _, m in outs],
        scratch_shapes=[
            pltpu.VMEM((MICRO, CACHE, 256), BF), pltpu.VMEM((MICRO, CACHE, 256), BF),
            pltpu.VMEM((MICRO, 2, 1024, HD), BF), pltpu.VMEM((HALF, D), BF), pltpu.VMEM((HALF, D), BF),
            dma((2, 4)), dma((2, 4)), dma((2, 4)), dma((2, 4)), dma((2,)), dma((2,)), dma((2, 2)), dma((4,)),
            dma((5, 1)), dma((4, 1)), dma((4, 4)), dma((4, 4)), dma((5, 3)), dma((4, 3)), dma((4, 4)), dma((4, 4)),
            dma((4,)), dma((4,)),
        ],
        compiler_params=pltpu.CompilerParams(collective_id=0, has_side_effects=True, vmem_limit_bytes=60 << 20),
        name="front",
        cost_estimate=pl.CostEstimate(flops=int(2e10), bytes_accessed=int(5e7), transcendentals=0),
    )(*args)


def everyone(q, c, t):
    return (
        [at(q, c, t ^ j) for j in range(1, 4)] + [at(q, 1 - c, t ^ j) for j in range(4)]
        + [at(q ^ 1, c, t), at(q ^ 2, c, t)]
    )


def add_low(a, b):
    return (a.astype(F32) + b.astype(F32)).astype(BF)


def turn(i):
    return jnp.where(i < 2, 2 * i + 1, 6 - 2 * i)


def slot_of(p, k):
    return (0, (2, 1)[p], (1, 2)[p], 3)[k]


class Plane:
    def __init__(self, chunk, recv1, recv2, sems):
        self.chunk, self.recv1, self.recv2 = chunk, recv1, recv2
        self.s1, self.r1, self.s2, self.r2 = sems
        _, self.q, self.c, self.t = where_am_i()

    def copy1(self, j, p):
        return remote(self.chunk.at[j, p, pl.ds(2, 2)], self.recv1.at[j, p], self.s1.at[j, p], self.r1.at[j, p],
                      at(self.q ^ (1 + p), self.c, self.t))

    def copy2(self, j, p):
        return remote(self.chunk.at[j, p, 1], self.recv2.at[j, p], self.s2.at[j, p], self.r2.at[j, p],
                      at(self.q ^ (2 - p), self.c, self.t))

    def start(self, j):
        for p in range(2):
            self.copy1(j, p).start()

    def stage2(self, j):
        for p in range(2):
            arrived(self.recv1.at[j, p], self.r1.at[j, p], None)
            self.chunk[j, p, 1] = add_low(self.chunk[j, p, 1], self.recv1[j, p, 1])
        self.chunk[j, 0, 0] = add_low(self.chunk[j, 0, 0], self.recv1[j, 0, 0])
        for p in range(2):
            self.copy2(j, p).start()
        self.chunk[j, 1, 0] = add_low(self.chunk[j, 1, 0], self.recv1[j, 1, 0])

    def stage3(self, j, out):
        half = self.chunk.shape[3]
        for p in range(2):
            arrived(self.recv2.at[j, p], self.r2.at[j, p], None)
            out[p * half : (p + 1) * half, :] = add_low(self.chunk[j, p, 0], self.recv2[j, p])

    def drain(self):
        for j in range(4):
            for p in range(2):
                self.copy1(j, p).wait_send()
                self.copy2(j, p).wait_send()


def rows_back(sends, src, dst, send_sem, recv_sem, slots=(0, 1)):
    _, q, c, t = where_am_i()
    m = t & 1
    for s in slots:
        here = (c == (t >> 1)) & (s == m)
        for k in range(NQ):
            one = src.at[s * 256 : (s + 1) * 256, lanes(k)]
            two = dst.at[m, :, block(q ^ k, DP)]
            sends.go(one, two, send_sem.at[s, k], recv_sem.at[m, k], at(q, t >> 1, 2 * c + s),
                     when=jnp.logical_not(here))
            pl.when(here)(pltpu.make_async_copy(one, two, recv_sem.at[m, k]).start)


def rows_back_in(dst, recv_sem):
    _, q, _, _ = where_am_i()
    for m in range(2):
        for k in range(NQ):
            arrived(dst.at[m, :, block(q ^ k, DP)], recv_sem.at[m, k], None)


def put_gain(out, row, total):
    _, q, _, _ = where_am_i()
    for k in range(NQ):
        out[row : row + 1, block(q ^ k, DP)] = total[:, lanes(k)]


def local_gain(gain):
    _, q, _, _ = where_am_i()
    return jnp.concatenate([gain[:, block(q ^ k, DP)] for k in range(NQ)], axis=1)


DMA = pltpu.SemaphoreType.DMA
HBM = pl.BlockSpec(memory_space=pl.ANY)


def remote_call(body, name, number, args, places, outs, scratch, flops):
    return pl.pallas_call(
        body,
        out_shape=[jax.ShapeDtypeStruct(s, d) for s, d, _ in outs],
        in_specs=list(places),
        out_specs=[m for _, _, m in outs],
        scratch_shapes=list(scratch),
        compiler_params=pltpu.CompilerParams(collective_id=number, has_side_effects=True, vmem_limit_bytes=62 << 20),
        name=name,
        cost_estimate=pl.CostEstimate(flops=int(flops), bytes_accessed=int(5e7), transcendentals=0),
    )(*args)


def middle_body(n_own, n_oth, cot_own, cot_oth, hidden, gain_f, gate_t, up_t, down, wb,
                sums, grad_hidden, low_own, low_oth, out_rows, gain_two,
                wgu, wd, act, dgu, chunk, recv1, recv2, z_out, z_in, d_send, d_got, y_send, y_got, rows_buf,
                own_sem, got_sem, s1, r1, s2, r2, z_send, z_recv, pair_send, pair_recv, row_send, row_recv):
    _, q, c, t = where_am_i()
    partner = at(q, 1 - c, t)
    sends = Sends()

    def own_copies():
        rows = pl.ds(pl.multiple_of(c * HID, 32), HID)
        for k in range(NQ):
            for i, (w, two) in enumerate(((gate_t, wgu.at[0:HID, lanes(k)]), (up_t, wgu.at[HID : 2 * HID, lanes(k)]),
                                          (down, wd.at[0:HID, lanes(k)]))):
                yield pltpu.make_async_copy(w.at[rows, block(q ^ k, DP)], two, own_sem.at[i, k])

    def got_copies(j):
        gu = wgu.at[pl.ds(pl.multiple_of(j * (2 * HID), 32), 2 * HID)]
        d = wd.at[pl.ds(pl.multiple_of(j * HID, 32), HID)]
        yield pltpu.make_async_copy(wb.at[j - 1, pl.ds(0, 2 * HID)], gu, got_sem.at[j - 1, 0])
        yield pltpu.make_async_copy(wb.at[j - 1, pl.ds(2 * HID, HID)], d, got_sem.at[j - 1, 1])

    for j in range(1, 4):
        for copy in got_copies(j):
            copy.start()
    for copy in own_copies():
        copy.start()
    greet(everyone(q, c, t))
    plane = Plane(chunk, recv1, recv2, (s1, r1, s2, r2))

    def feed(i, carry):
        j = turn(i)

        @pl.when(j > 0)
        def _():
            for copy in got_copies(j):
                copy.wait()

        @pl.when(j == 0)
        def _():
            for copy in own_copies():
                copy.wait()

        gate_rows = pl.ds(pl.multiple_of(j * (2 * HID), 32), HID)
        up_rows = pl.ds(pl.multiple_of(j * (2 * HID) + HID, 32), HID)
        down_rows = pl.ds(pl.multiple_of(j * HID, 32), HID)
        for side, n, cot in ((0, n_own, cot_own), (1, n_oth, cot_oth)):
            for b in range(2):
                rows = slice(b * 256, (b + 1) * 256)
                cols = slice(side * HALF + b * 256, side * HALF + (b + 1) * 256)
                normed = n[rows, :]
                gate = nt(wgu[gate_rows, :], normed)
                up = nt(wgu[up_rows, :], normed)
                grad = nt(wd[down_rows, :], cot[rows, :])
                sig = 1.0 / (1.0 + jnp.exp(-gate))
                silu = gate * sig
                act[down_rows, cols] = (silu * up).astype(BF)
                dgu[gate_rows, cols] = (grad * up * sig * (1.0 + gate * (1.0 - sig))).astype(BF)
                dgu[up_rows, cols] = (grad * silu).astype(BF)
        both = pl.ds(pl.multiple_of(j * (2 * HID), 32), 2 * HID)
        half = RB // 2
        rest = 2 * HID - half
        for k in (3, 1, 2, 0):
            one, two = slot_of(0, k), slot_of(1, k)
            g = nn(dgu[both, 0:HALF], n_own[:, lanes(k)]) + nn(dgu[both, HALF:LEN], n_oth[:, lanes(k)])
            chunk[j, 0, one, :, :] = g[0:half].astype(BF)
            chunk[j, 1, two, 0:rest, :] = g[half:].astype(BF)
            if k == 0:
                plane.start(j)
            g = nn(act[down_rows, 0:HALF], cot_own[:, lanes(k)]) + nn(act[down_rows, HALF:LEN], cot_oth[:, lanes(k)])
            chunk[j, 1, two, rest:half, :] = g.astype(BF)

        @pl.when(i == 2)
        def _():
            plane.stage2(1)

        @pl.when(i == 3)
        def _():
            plane.stage2(3)

        return carry

    lax.fori_loop(0, 4, feed, 0)
    own, oth = slice(0, HALF), slice(HALF, LEN)
    d_send[...] = tn(dgu[:, oth], wgu[...]).astype(BF)
    sends.go(d_send, d_got, pair_send.at[0], pair_recv.at[0], partner)
    y_send[...] = tn(act[:, oth], wd[...]).astype(BF)
    sends.go(y_send, y_got, pair_send.at[1], pair_recv.at[1], partner)
    arrived(d_got, pair_recv.at[0], None)
    gain = local_gain(gain_f)
    total = jnp.zeros((1, D), F32)
    for b in range(2):
        rows = slice(b * 256, (b + 1) * 256)
        grad = tn(dgu[:, rows], wgu[...]) + d_got[rows, :].astype(F32)
        back, part = norm_back(grad, hidden[rows, :], gain)
        total = total + part
        g = cot_own[rows, :].astype(F32) + back
        grad_hidden[rows, :] = g
        low_own[rows, :] = g.astype(BF)
    put_gain(gain_two, 0, total)
    sends.go(low_own, low_oth, pair_send.at[2], pair_recv.at[2], partner)
    arrived(y_got, pair_recv.at[1], None)
    for b in range(2):
        rows = slice(b * 256, (b + 1) * 256)
        rows_buf[rows, :] = (hidden[rows, :] + (tn(act[:, rows], wd[...]) + y_got[rows, :].astype(F32))).astype(BF)
    rows_back(sends, rows_buf, out_rows, row_send, row_recv)
    plane.stage2(2)
    plane.stage3(1, z_out.at[0])
    plane.stage2(0)
    sends.go(z_out.at[0], z_in.at[0], z_send.at[0], z_recv.at[0], at(q, c, t ^ 1))
    plane.stage3(3, z_out.at[1])
    plane.stage3(2, sums.at[1])
    sends.go(z_out.at[1], z_in.at[1], z_send.at[1], z_recv.at[1], at(q, c, t ^ 1))
    plane.stage3(0, sums.at[0])
    for i in range(2):
        arrived(z_in.at[i], z_recv.at[i], None)
        sums[i] = add_low(sums[i], z_in[i])
    arrived(low_oth, pair_recv.at[2], None)
    rows_back_in(out_rows, row_recv)
    plane.drain()
    sends.drain()


def middle(*args):
    half16 = ((HALF, D), BF, VM)
    outs = [((2, RB, DP), BF, VM), ((HALF, D), F32, VM), half16, half16, ((MICRO, 256, D), BF, VM), ((1, D), F32, VM)]
    buf = pltpu.VMEM((HALF, D), BF)
    scratch = [
        pltpu.VMEM((4 * 2 * HID, D), BF), pltpu.VMEM((4 * HID, D), BF), pltpu.VMEM((4 * HID, LEN), BF),
        pltpu.VMEM((4 * 2 * HID, LEN), BF), pltpu.VMEM((4, 2, NQ, RB // 2, DP), BF), pltpu.VMEM((4, 2, 2, RB // 2, DP), BF),
        pltpu.VMEM((4, 2, RB // 2, DP), BF), pltpu.VMEM((2, RB, DP), BF), pltpu.VMEM((2, RB, DP), BF), buf, buf, buf, buf, buf,
        DMA((3, 4)), DMA((3, 2)), DMA((4, 2)), DMA((4, 2)), DMA((4, 2)), DMA((4, 2)), DMA((2,)), DMA((2,)), DMA((3,)), DMA((3,)),
        DMA((2, 4)), DMA((2, 4)),
    ]
    return remote_call(middle_body, "middle", 1, args, [VM] * 6 + [HBM] * 4, outs, scratch, 2.6e10)


class Spread:
    def __init__(self, piece, got, sends, send_sem, recv_sem):
        self.piece, self.got, self.sends, self.ss, self.rs = piece, got, sends, send_sem, recv_sem
        _, self.q, self.c, self.t = where_am_i()

    def place(self, k, half, p=None):
        size = self.got.shape[1] // 2
        rows = pl.ds(0, 2 * size) if p is None else pl.ds(p * size, size)
        return self.got.at[half, rows, block(self.q ^ k, DP)]

    def go(self, src, dst, number, device):
        self.sends.go(src, dst, self.ss.at[number], self.rs.at[number], device)

    def start(self):
        q, c, t = self.q, self.c, self.t
        for k in (1, 2):
            self.go(self.piece, self.place(0, c), k, at(q ^ k, c, t))
        self.go(self.piece, self.place(0, c), 4, at(q, 1 - c, t))
        pltpu.make_async_copy(self.piece, self.place(0, c), self.rs.at[0]).start()

    def relay(self):
        q, c, t = self.q, self.c, self.t
        for p, k, number in ((0, 1, 3), (1, 2, 8)):
            arrived(self.place(k, c), self.rs.at[k], None)
            self.go(self.place(k, c, p), self.place(k, c, p), number, at(q ^ (3 - k), c, t))
            self.go(self.place(k, c), self.place(k, c), 4 + k, at(q, 1 - c, t))

    def last(self):
        for p, number in ((0, 3), (1, 8)):
            arrived(self.place(3, self.c, p), self.rs.at[number], None)
        self.go(self.place(3, self.c), self.place(3, self.c), 7, at(self.q, 1 - self.c, self.t))

    def finish(self):
        arrived(self.place(0, self.c), self.rs.at[0], None)
        for k in range(NQ):
            arrived(self.place(k, 1 - self.c), self.rs.at[4 + k], None)


def tail_body(low_own, low_oth, gain_a, gain_two, sums_b, n_own_in, n_oth_in, x_in, wa_in, qkv_in, att_in, lse_in, mem_in, gh_in,
              grad_rows, got_b, got_a, gains,
              n_own, n_oth, x_own, wa, qkv_all, att_all, lse_all, mem_all, grad_hidden, load_sem, head_sem,
              da, dk, dv, dall, chunk, recv1, recv2, sums_a, zb, z1, z2, piece_b, piece_a, d_send, d_got, rows_buf, g_near, g_far,
              s1, r1, s2, r2, zb_send, zb_recv, z1_send, z1_recv, z2_send, z2_recv, pair_send, pair_recv, row_send, row_recv,
              bs, br, as_, ar, gs, gr, hs, hr):
    _, q, c, t = where_am_i()
    sends = Sends()

    def head_loads(j):
        for i, (one, two) in enumerate(((wa_in, wa), (qkv_in, qkv_all), (lse_in, lse_all), (mem_in, mem_all))):
            yield pltpu.make_async_copy(one.at[j], two.at[j], head_sem.at[j, i])

    shared = [
        pltpu.make_async_copy(one, two, load_sem.at[i])
        for i, (one, two) in enumerate(
            ((att_in, att_all), (n_own_in, n_own), (n_oth_in, n_oth), (x_in, x_own), (gh_in, grad_hidden))
        )
    ]
    for copy in shared[:3]:
        copy.start()
    for j in (1, 3, 2, 0):
        for copy in head_loads(j):
            copy.start()
    for copy in shared[3:]:
        copy.start()
    greet(everyone(q, c, t) + [at(q ^ 3, c, t)])
    plane = Plane(chunk, recv1, recv2, (s1, r1, s2, r2))
    sends.go(sums_b.at[1], zb, zb_send.at[0], zb_recv.at[0], at(q, c, t ^ 2))

    def z_first(i):
        sends.go(sums_a.at[2 * i + 1], z1.at[i], z1_send.at[i], z1_recv.at[i], at(q, c, t ^ 1))

    def attend_back(i, carry):
        j = turn(i)
        for copy in head_loads(j):
            copy.wait()
        wo = wa[j, 3 * HD : 4 * HD, :]
        qkv, lse, mem, head = qkv_all.at[j], lse_all.at[j], mem_all.at[j], block(j, HD)
        grad_o = jnp.zeros((HD, D), F32)
        for who, g in ((c, low_own), (1 - c, low_oth)):
            rows = block(who, HALF)
            grads = g[...]
            da[rows, :] = nt(grads, wo).astype(BF)
            grad_o = grad_o + tn(att_all[rows, head], grads)
        keep = causal()
        for b in range(LEN // BLK):
            rows = slice(b * BLK, (b + 1) * BLK)
            query = qkv[rows, 0:HD]
            grad = da[rows, :]
            level = lse[rows, 0:1]
            mem_k = mem[b * TOPK : (b + 1) * TOPK, :]
            mem_v = mem[512 + b * TOPK : 512 + (b + 1) * TOPK, :]
            p_d = jnp.exp(jnp.where(keep, nt(query, qkv[rows, HD : 2 * HD]), NEG) - level)
            p_f = jnp.exp(nt(query, mem_k) - level)
            g_d = nt(grad, qkv[rows, 2 * HD : 3 * HD])
            g_f = nt(grad, mem_v)
            delta = jnp.sum(p_d * g_d, axis=1, keepdims=True) + jnp.sum(p_f * g_f, axis=1, keepdims=True)
            if b:
                past = slice(0, b * BLK)
                p_p = jnp.exp(nt(query, qkv[past, HD : 2 * HD]) - level)
                g_p = nt(grad, qkv[past, 2 * HD : 3 * HD])
                delta = delta + jnp.sum(p_p * g_p, axis=1, keepdims=True)
            s_d = (p_d * (g_d - delta)).astype(BF)
            s_f = (p_f * (g_f - delta)).astype(BF)
            dq = nn(s_d, qkv[rows, HD : 2 * HD]) + nn(s_f, mem_k)
            if b:
                s_p = (p_p * (g_p - delta)).astype(BF)
                dq = dq + nn(s_p, qkv[past, HD : 2 * HD])
                dk[past, :] = dk[past, :] + tn(s_p, query)
                dv[past, :] = dv[past, :] + tn(p_p.astype(BF), grad)
            dk[rows, :] = tn(s_d, query)
            dv[rows, :] = tn(p_d.astype(BF), grad)
            dall[j, rows, 0:HD] = (dq * (HD**-0.5)).astype(BF)
        dall[j, :, HD : 2 * HD] = dk[...].astype(BF)
        dall[j, :, 2 * HD : 3 * HD] = dv[...].astype(BF)
        grad_w = tn(dall[j, block(c, HALF), :], n_own[...]) + tn(dall[j, block(1 - c, HALF), :], n_oth[...])
        for k in range(NQ):
            one, two = slot_of(0, k), slot_of(1, k)
            chunk[j, 0, one, :, :] = grad_w[0 : 2 * HD, lanes(k)].astype(BF)
            chunk[j, 1, two, 0:HD, :] = grad_w[2 * HD : 3 * HD, lanes(k)].astype(BF)
            chunk[j, 1, two, HD : 2 * HD, :] = grad_o[:, lanes(k)].astype(BF)

        @pl.when(i >= 1)
        def _():
            plane.stage2(turn(i - 1))

        plane.start(j)
        return carry

    for copy in shared[:3]:
        copy.wait()
    lax.fori_loop(0, 4, attend_back, 0)
    for copy in shared[3:]:
        copy.wait()
    weights = jnp.concatenate([wa[j, 0 : 3 * HD, :] for j in range(4)], axis=0)

    def into_rows(who, b):
        rows = pl.ds(pl.multiple_of(who * HALF + b * 256, 256), 256)
        d = jnp.concatenate([dall[j, rows, :] for j in range(4)], axis=1)
        return nn(d, weights)

    for b in range(2):
        d_send[b * 256 : (b + 1) * 256, :] = into_rows(1 - c, b).astype(BF)
    sends.go(d_send, d_got, pair_send.at[0], pair_recv.at[0], at(q, 1 - c, t))
    plane.stage3(1, sums_a.at[1])
    plane.stage3(3, sums_a.at[3])
    z_first(0)
    arrived(d_got, pair_recv.at[0], None)
    to_b = Spread(piece_b, got_b, sends, bs, br)
    to_a = Spread(piece_a, got_a, sends, as_, ar)
    gain = local_gain(gain_a)
    total = jnp.zeros((1, D), F32)
    for b in range(2):
        rows = slice(b * 256, (b + 1) * 256)
        grad = into_rows(c, b) + d_got[rows, :].astype(F32)
        back, part = norm_back(grad, x_own[rows, :].astype(F32), gain)
        total = total + part
        rows_buf[rows, :] = (grad_hidden[rows, :] + back).astype(BF)
        if b == 0:
            z_first(1)
            plane.stage2(0)
            arrived(zb, zb_recv.at[0], None)
            piece_b[...] = add_low(sums_b[0], zb[...])
            to_b.start()
    here = c * 4 + t
    put_gain(g_near.at[here], 0, total)
    g_near[here, 1:2, :] = gain_two[...]
    group = [(dc, dt) for dc in range(2) for dt in range(4) if dc + dt]
    for i, (dc, dt) in enumerate(group):
        sends.go(g_near.at[here], g_near.at[here], gs.at[i], gr.at[here], at(q, c ^ dc, t ^ dt))
    rows_back(sends, rows_buf, grad_rows, row_send, row_recv, (0,))
    plane.stage3(2, sums_a.at[2])
    arrived(z1.at[1], z1_recv.at[1], None)
    sums_a[2] = add_low(sums_a[2], z1[1])
    for dc, dt in group:
        there = (c ^ dc) * 4 + (t ^ dt)
        arrived(g_near.at[there], gr.at[there], None)
    sends.go(sums_a.at[2], z2, z2_send.at[0], z2_recv.at[0], at(q, c, t ^ 2))
    rows_back(sends, rows_buf, grad_rows, row_send, row_recv, (1,))
    part = g_near[0]
    for i in range(1, 8):
        part = part + g_near[i]
    g_far[q] = part
    for k in range(1, NQ):
        sends.go(g_far.at[q], g_far.at[q], hs.at[k], hr.at[q], at(q ^ k, c, t))
    plane.stage3(0, sums_a.at[0])
    to_b.relay()
    arrived(z1.at[0], z1_recv.at[0], None)
    arrived(z2, z2_recv.at[0], None)
    piece_a[...] = ((sums_a[0].astype(F32) + z1[0].astype(F32)) + z2[...].astype(F32)).astype(BF)
    to_a.start()
    to_b.last()
    for k in range(1, NQ):
        arrived(g_far.at[q ^ k], hr.at[q ^ k], None)
    gains[...] = ((g_far[0] + g_far[1]) + g_far[2]) + g_far[3]
    to_a.relay()
    to_a.last()
    to_b.finish()
    to_a.finish()
    rows_back_in(grad_rows, row_recv)
    plane.drain()
    sends.drain()


def tail(*args):
    outs = [((MICRO, 256, D), BF, VM), ((2, RB, D), BF, HBM), ((2, RA, D), BF, HBM), ((2, D), F32, VM)]
    buf = pltpu.VMEM((HALF, D), BF)
    scratch = [
        buf, buf, buf, pltpu.VMEM((4, RA, D), BF), pltpu.VMEM((4, LEN, 3 * HD), BF), pltpu.VMEM((LEN, 4 * HD), BF),
        pltpu.VMEM((4, LEN, HD), F32), pltpu.VMEM((4, 1024, HD), BF), pltpu.VMEM((HALF, D), F32), DMA((5,)), DMA((4, 4)),
        pltpu.VMEM((LEN, HD), BF), pltpu.VMEM((LEN, HD), F32), pltpu.VMEM((LEN, HD), F32), pltpu.VMEM((4, LEN, 3 * HD), BF),
        pltpu.VMEM((4, 2, NQ, RA // 2, DP), BF), pltpu.VMEM((4, 2, 2, RA // 2, DP), BF), pltpu.VMEM((4, 2, RA // 2, DP), BF),
        pltpu.VMEM((4, RA, DP), BF), pltpu.VMEM((RB, DP), BF), pltpu.VMEM((2, RA, DP), BF), pltpu.VMEM((RA, DP), BF),
        pltpu.VMEM((RB, DP), BF), pltpu.VMEM((RA, DP), BF), buf, buf, buf,
        pltpu.VMEM((8, 2, D), F32), pltpu.VMEM((NQ, 2, D), F32),
        DMA((4, 2)), DMA((4, 2)), DMA((4, 2)), DMA((4, 2)), DMA((1,)), DMA((1,)), DMA((2,)), DMA((2,)), DMA((1,)), DMA((1,)),
        DMA((1,)), DMA((1,)), DMA((2, 4)), DMA((2, 4)), DMA((9,)), DMA((9,)), DMA((9,)), DMA((9,)), DMA((7,)), DMA((8,)),
        DMA((4,)), DMA((4,)),
    ]
    return remote_call(tail_body, "tail", 2, args, [VM] * 5 + [HBM] * 9, outs, scratch, 1.5e10)


def per_device(tokens, attn_gain, ffn_gain, query_weight, key_weight, value_weight, out_weight, gate_weight,
               up_weight, down_weight, cache_keys, cache_values, knn_index, cotangent):
    gain_a, gain_f = attn_gain.reshape(1, D), ffn_gain.reshape(1, D)
    gate_t, up_t = gate_weight.T, up_weight.T
    wa, wb, x_own, n1_own, n1_oth, cot_own, cot_oth, mem, qkv, att, lse, hidden, n2_own, n2_oth = front(
        tokens, cotangent, gain_a, gain_f, cache_keys, cache_values, knn_index, query_weight, key_weight, value_weight,
        out_weight, gate_t, up_t, down_weight,
    )
    sums_b, grad_hidden, low_own, low_oth, output, gain_two = middle(
        n2_own, n2_oth, cot_own, cot_oth, hidden, gain_f, gate_t, up_t, down_weight, wb
    )
    grad_tokens, got_b, got_a, gains = tail(
        low_own, low_oth, gain_a, gain_two, sums_b, n1_own, n1_oth, x_own, wa, qkv, att, lse, mem, grad_hidden
    )
    if lax.axis_size("r") > 1:
        got_b = lax.psum(got_b.astype(F32), "r")
        got_a = lax.psum(got_a.astype(F32), "r")
        gains = lax.psum(gains, "r")
    gg, gu, gd = place(place_b_body, got_b, ("tall", "tall", "tall"), "place_b")
    gq, gk, gv, go = place(place_a_body, got_a, ("col", "col", "col", "row"), "place_a")
    return output, grad_tokens, gq, gk, gv, go, gg.T, gu.T, gd, gains[0], gains[1]


def solution(mesh):
    n_dp, n_t = mesh.shape["dp"], mesh.shape["tensor"]
    fine = Mesh(mesh.devices.reshape(n_dp // 8, NQ, 2, n_t), ("r", "q", "c", "t"))
    dp = ("r", "q", "c")
    rows = P(None, dp + ("t",), None)
    placed = (
        rows, P(), P(), P(None, "t"), P(None, "t"), P(None, "t"), P("t", None), P(None, "t"), P(None, "t"),
        P("t", None), P(None, dp, "t"), P(None, dp, "t"), P(None, dp, "t", None), rows,
    )
    return jax.shard_map(
        per_device,
        mesh=fine,
        in_specs=placed,
        out_specs=(
            rows, rows, P(None, "t"), P(None, "t"), P(None, "t"), P("t", None), P(None, "t"), P(None, "t"),
            P("t", None), P(), P(),
        ),
        check_vma=False,
    )
```

```python
import functools

import jax
import jax.numpy as jnp
from jax import lax
from jax.experimental import pallas as pl
from jax.experimental.pallas import tpu as pltpu
from jax.sharding import Mesh
from jax.sharding import PartitionSpec as P

HEADS = 8
HD = 128
MICRO = 2
BLK = 256
TOPK = 128
CACHE = 256
D = 1024
NQ = 4
DP = D // NQ
HALF = 512
LEN = 1024
HID = 352
RA = 4 * HD
RB = 3 * HID

EPS = 1e-06
NEG = -1e30
BF = jnp.bfloat16
F32 = jnp.float32


def nn(a, b):
    return lax.dot_general(a, b, (((1,), (0,)), ((), ())), preferred_element_type=F32)


def nt(a, b):
    return lax.dot_general(a, b, (((1,), (1,)), ((), ())), preferred_element_type=F32)


def tn(a, b):
    return lax.dot_general(a, b, (((0,), (0,)), ((), ())), preferred_element_type=F32)


VM = pl.BlockSpec(memory_space=pltpu.VMEM)


def block(index, size):
    return pl.ds(pl.multiple_of(index * size, size), size)


def lanes(k):
    return slice(k * DP, (k + 1) * DP)


def scale_of(x):
    return lax.rsqrt(jnp.mean(x * x, axis=-1, keepdims=True) + EPS)


def norm_back(grad, x, gain):
    scale = scale_of(x)
    scaled = grad * gain
    gain_part = jnp.sum(grad * x * scale, axis=0, keepdims=True)
    back = scale * scaled - x * (scale * scale * scale) * jnp.mean(scaled * x, axis=-1, keepdims=True)
    return back, gain_part


def causal():
    return lax.broadcasted_iota(jnp.int32, (BLK, BLK), 1) <= lax.broadcasted_iota(jnp.int32, (BLK, BLK), 0)


def place_a_body(got, gq, gk, gv, go):
    for half in range(2):
        rows = slice(half * HD, (half + 1) * HD)
        for i, out in enumerate((gq, gk, gv)):
            out[:, rows] = got[half, i * HD : (i + 1) * HD, :].astype(F32).T
        go[rows, :] = got[half, 3 * HD : 4 * HD, :].astype(F32)


def place_b_body(got, *outs):
    for half in range(2):
        for i, out in enumerate(outs):
            out[half * HID : (half + 1) * HID, :] = got[half, i * HID : (i + 1) * HID, :].astype(F32)


def place(body, got, kinds, name):
    shapes = {"tall": (2 * HID, D), "col": (D, 2 * HD), "row": (2 * HD, D)}
    specs = {
        "tall": pl.BlockSpec((2 * HID, DP), lambda i: (0, i)),
        "col": pl.BlockSpec((DP, 2 * HD), lambda i: (i, 0)),
        "row": pl.BlockSpec((2 * HD, DP), lambda i: (0, i)),
    }
    return pl.pallas_call(
        body,
        grid=(NQ,),
        out_shape=[jax.ShapeDtypeStruct(shapes[k], F32) for k in kinds],
        in_specs=[pl.BlockSpec((*got.shape[:2], DP), lambda i: (0, 0, i))],
        out_specs=[specs[k] for k in kinds],
        name=name,
        cost_estimate=pl.CostEstimate(flops=0, bytes_accessed=int(got.size * 6), transcendentals=0),
    )(got)


def where_am_i():
    return lax.axis_index("r"), lax.axis_index("q"), lax.axis_index("c"), lax.axis_index("t")


def at(q, c, t):
    return {"q": q, "c": c, "t": t}


def dp_at(index):
    return {"r": index // (2 * NQ), "q": lax.rem(index // 2, NQ), "c": lax.rem(index, 2)}


def remote(src, dst, send_sem, recv_sem, device):
    return pltpu.make_async_remote_copy(
        src_ref=src, dst_ref=dst, send_sem=send_sem, recv_sem=recv_sem, device_id=device,
        device_id_type=pl.DeviceIdType.MESH,
    )


def arrived(dst, recv_sem, spare):
    pltpu.make_async_copy(dst, dst, recv_sem).wait()


def greet(devices):
    barrier = pltpu.get_barrier_semaphore()
    for device in devices:
        pl.semaphore_signal(barrier, inc=1, device_id=device, device_id_type=pl.DeviceIdType.MESH)
    pl.semaphore_wait(barrier, len(devices))


class Sends:
    def __init__(self):
        self.open = []

    def go(self, src, dst, send_sem, recv_sem, device, when=None):
        copy = remote(src, dst, send_sem, recv_sem, device)
        self.open.append((copy, when))
        if when is None:
            copy.start()
        else:
            pl.when(when)(copy.start)

    def drain(self):
        for copy, when in self.open:
            if when is None:
                copy.wait_send()
            else:
                pl.when(when)(copy.wait_send)
        self.open = []


def front_body(tok, cot, gain_a, gain_f, ck, cv, knn, wq, wk, wv, wo, gate_t, up_t, down,
               wa, wb, x_own, n_own, n_oth, cot_own, cot_oth, mem, qkv, att, lse, hidden, n2_own, n2_oth,
               prev_k, prev_v, picked, o_send, o_got,
               row_send, row_recv, cot_send, cot_recv, cache_send, cache_recv, mem_send, mem_recv,
               za_send, za_recv, xa_send, xa_recv, zb_send, zb_recv, xb_send, xb_recv, pair_send, pair_recv):
    r, q, c, t = where_am_i()
    count = lax.axis_size("r") * 2 * NQ
    me = (r * NQ + q) * 2 + c
    after = dp_at(lax.rem(me + 1, count))
    across = dp_at(lax.rem(me + jnp.where(c == 0, count - 1, 1), count))
    mid = (t == 1) | (t == 2)
    second, third = jnp.where(mid, 3, 2), jnp.where(mid, 2, 3)
    partner = at(q, 1 - c, t)
    sends = Sends()
    greet(
        [at(q, c, t ^ j) for j in range(1, 4)] + [at(q, 1 - c, t ^ j) for j in range(4)]
        + [at(q ^ 1, c, t), at(q ^ 2, c, t), at(q ^ 3, c, t), across]
    )

    def rows_out(src, dst, send_sem, recv_sem):
        slot = t & 1
        for m in range(MICRO):
            here = (c == (t >> 1)) & (m == slot)
            for k in range(NQ):
                one = src.at[m, :, block(q ^ k, DP)]
                two = dst.at[block(slot, 256), lanes(k)]
                sends.go(one, two, send_sem.at[m, k], recv_sem.at[slot, k], at(q, t >> 1, 2 * c + m),
                         when=jnp.logical_not(here))
                pl.when(here)(pltpu.make_async_copy(one, two, recv_sem.at[slot, k]).start)

    def rows_in(dst, recv_sem):
        for slot in range(2):
            for k in range(NQ):
                arrived(dst.at[slot * 256 : (slot + 1) * 256, lanes(k)], recv_sem.at[slot, k], None)

    near, far_mid = at(q, c, t ^ 1), at(q, c, t ^ 3)
    ends = jnp.logical_not(mid)
    a_piece = [wa.at[0, :, lanes(0)]]
    b_piece = [w.at[pl.ds(pl.multiple_of(c * HID, 32), HID), block(q, DP)] for w in (gate_t, up_t, down)]

    def a_slot(s):
        return [wa.at[s, :, lanes(0)]]

    def b_slot(s):
        return [wb.at[s - 1, i * HID : (i + 1) * HID, lanes(0)] for i in range(3)]

    def z_first(piece, slot, send_sem, recv_sem):
        for i, (one, two) in enumerate(zip(piece, slot(1))):
            sends.go(one, two, send_sem.at[0, i], recv_sem.at[1, i], near)
        for i, (one, two) in enumerate(zip(piece, slot(3))):
            sends.go(one, two, send_sem.at[1, i], recv_sem.at[3, i], far_mid, when=mid)

    def relay_some(order, s, when, slot, whole, z_send, z_recv, x_send, x_recv):
        for i, two in enumerate(slot(s)):
            if when is None:
                arrived(two, z_recv.at[s, i], None)
            else:
                pl.when(when)(functools.partial(arrived, two, z_recv.at[s, i], None))
        if order == 1:
            for i, (one, two) in enumerate(zip(slot(1), slot(2))):
                sends.go(one, two, z_send.at[2, i], z_recv.at[2, i], far_mid, when=mid)
        elif when is mid:
            back = 2 if order == 2 else 3
            for i, (one, two) in enumerate(zip(slot(s), slot(back))):
                sends.go(one, two, z_send.at[order + 1, i], z_recv.at[back, i], near, when=mid)
        for k in (1, 2, 3) if order == 3 else (1, 2):
            sends.go(whole(s, 0), whole(s, k), x_send.at[s, k], x_recv.at[s, k], at(q ^ k, c, t), when=when)

    def relay_far(order, whole, x_send, x_recv):
        s = (None, 1, second)[order]
        arrived(whole(s, order), x_recv.at[s, order], None)
        sends.go(whole(s, order), whole(s, 3), x_send.at[s, 3], x_recv.at[s, 3], at(q ^ (3 - order), c, t))

    def in_place(order, whole, x_recv):
        s = (None, 1, second, third)[order]
        for k in range(1, NQ):
            if k != order or order == 3:
                arrived(whole(s, k), x_recv.at[s, k], None)

    def a_whole(s, k):
        return wa.at[s, :, lanes(k)]

    def b_whole(s, k):
        return wb.at[s - 1, :, lanes(k)]

    relay_a = functools.partial(relay_some, slot=a_slot, whole=a_whole, z_send=za_send, z_recv=za_recv, x_send=xa_send, x_recv=xa_recv)
    relay_b = functools.partial(relay_some, slot=b_slot, whole=b_whole, z_send=zb_send, z_recv=zb_recv, x_send=xb_send, x_recv=xb_recv)

    for i, (one, two) in enumerate(((ck, prev_k), (cv, prev_v))):
        sends.go(one, two, cache_send.at[i], cache_recv.at[i], after)
    for k in range(NQ):
        rows = block(q ^ k, DP)
        for i, w in enumerate((wq, wk, wv)):
            wa[0, i * HD : (i + 1) * HD, lanes(k)] = w[rows, block(c, HD)].T
        wa[0, 3 * HD : 4 * HD, lanes(k)] = wo[block(c, HD), rows]
        if k == 1:
            z_first(a_piece, a_slot, za_send, za_recv)
            z_first(b_piece, b_slot, zb_send, zb_recv)
            rows_out(tok, x_own, row_send, row_recv)

    relay_a(1, 1, None)
    relay_a(2, 3, mid)
    for i, two in enumerate((prev_k, prev_v)):
        arrived(two, cache_recv.at[i], None)

    def pick(i, carry):
        m, h, b = i // 8, (i // 4) % 2, i % 4
        cols = block(h, HD)
        picks = knn[m, b, pl.ds(h, 1), :]
        rows = lax.broadcasted_iota(jnp.int32, (CACHE, TOPK), 0)
        hot_own = jnp.where(rows == picks, 1.0, 0.0).astype(BF)
        hot_prev = jnp.where(rows + CACHE == picks, 1.0, 0.0).astype(BF)
        for kv, own, prev in ((0, ck, prev_k), (1, cv, prev_v)):
            got = tn(hot_own, own[m, :, cols]) + tn(hot_prev, prev[m, :, cols])
            picked[m, h, pl.ds(pl.multiple_of(kv * 512 + b * TOPK, TOPK), TOPK), :] = got.astype(BF)
        return carry

    lax.fori_loop(0, 16, pick, 0)
    relay_b(1, 1, None)
    relay_b(2, 3, mid)
    relay_far(1, a_whole, xa_send, xa_recv)

    def send_mem():
        for m in range(MICRO):
            for h in range(2):
                kind = t ^ (2 * c + m)
                here = (c == h) & (kind == 0)
                sends.go(picked.at[m, h], mem.at[kind], mem_send.at[m, h], mem_recv.at[kind], at(q, h, 2 * c + m),
                         when=jnp.logical_not(here))
                pl.when(here)(pltpu.make_async_copy(picked.at[m, h], mem.at[kind], mem_recv.at[kind]).start)

    relay_far(1, b_whole, xb_send, xb_recv)
    rows_in(x_own, row_recv)
    gain = jnp.concatenate([gain_a[:, block(q ^ k, DP)] for k in range(NQ)], axis=1)
    for i in range(2):
        rows = slice(i * 256, (i + 1) * 256)
        x = x_own[rows, :].astype(F32)
        n_own[rows, :] = (x * scale_of(x) * gain).astype(BF)
    sends.go(n_own, n_oth, pair_send.at[0], pair_recv.at[0], partner)

    def project(j, who, n):
        acc = nt(n[...], wa[j, 0 : 3 * HD, :])
        rows = block(who, HALF)
        qkv[j, rows, 0:HD] = (acc[:, 0:HD] * (HD**-0.5)).astype(BF)
        qkv[j, rows, HD : 3 * HD] = acc[:, HD : 3 * HD].astype(BF)

    def attend(j):
        keep = causal()
        for b in range(LEN // BLK):
            rows = slice(b * BLK, (b + 1) * BLK)
            query = qkv[j, rows, 0:HD]
            diag = jnp.where(keep, nt(query, qkv[j, rows, HD : 2 * HD]), NEG)
            far = nt(query, mem[j, b * TOPK : (b + 1) * TOPK, :])
            top = jnp.maximum(jnp.max(diag, axis=1, keepdims=True), jnp.max(far, axis=1, keepdims=True))
            if b:
                past = nt(query, qkv[j, 0 : b * BLK, HD : 2 * HD])
                top = jnp.maximum(top, jnp.max(past, axis=1, keepdims=True))
            diag = jnp.exp(diag - top)
            far = jnp.exp(far - top)
            total = jnp.sum(diag, axis=1, keepdims=True) + jnp.sum(far, axis=1, keepdims=True)
            if b:
                past = jnp.exp(past - top)
                total = total + jnp.sum(past, axis=1, keepdims=True)
            inverse = 1.0 / total
            out = nn((diag * inverse).astype(BF), qkv[j, rows, 2 * HD : 3 * HD])
            out = out + nn((far * inverse).astype(BF), mem[j, 512 + b * TOPK : 512 + (b + 1) * TOPK, :])
            if b:
                out = out + nn((past * inverse).astype(BF), qkv[j, 0 : b * BLK, 2 * HD : 3 * HD])
            att[rows, block(j, HD)] = out.astype(BF)
            lse[j, rows, :] = jnp.broadcast_to(top + jnp.log(total), (BLK, HD))

    def got_mem(j):
        arrived(mem.at[j], mem_recv.at[j], None)

    relay_a(2, 2, ends)
    relay_a(3, 2, mid)
    relay_b(2, 2, ends)
    relay_b(3, 2, mid)
    send_mem()
    rows_out(cot, cot_own, cot_send, cot_recv)
    relay_far(2, a_whole, xa_send, xa_recv)
    arrived(n_oth, pair_recv.at[0], None)
    relay_far(2, b_whole, xb_send, xb_recv)
    relay_a(3, 3, ends)
    relay_b(3, 3, ends)

    def head(i, carry):
        j = jnp.where(i < 2, i, jnp.where(i == 2, second, third))
        for order in range(1, 4):
            pl.when(i == order)(functools.partial(in_place, order, a_whole, xa_recv))
        project(j, c, n_own)
        project(j, 1 - c, n_oth)
        got_mem(j)
        attend(j)
        return carry

    lax.fori_loop(0, 4, head, 0)
    weights = jnp.concatenate([wa[j, 3 * HD : 4 * HD, :] for j in range(4)], axis=0)
    for b in range(2):
        rows = slice(b * 256, (b + 1) * 256)
        o_send[rows, :] = nn(att[block(2 * (1 - c) + b, 256), :], weights).astype(BF)
        sends.go(o_send.at[rows], o_got.at[rows], pair_send.at[1 + b], pair_recv.at[1 + b], partner)
    hidden[...] = nn(att[block(c, HALF), :], weights)
    gain = jnp.concatenate([gain_f[:, block(q ^ k, DP)] for k in range(NQ)], axis=1)
    for b in range(2):
        rows = slice(b * 256, (b + 1) * 256)
        arrived(o_got.at[rows], pair_recv.at[1 + b], None)
        h = x_own[rows, :].astype(F32) + (hidden[rows, :] + o_got[rows, :].astype(F32))
        hidden[rows, :] = h
        n2_own[rows, :] = (h * scale_of(h) * gain).astype(BF)
        sends.go(n2_own.at[rows], n2_oth.at[rows], pair_send.at[3 + b], pair_recv.at[3 + b], partner)
    for b in range(2):
        rows = slice(b * 256, (b + 1) * 256)
        for k in range(NQ):
            arrived(cot_own.at[rows, lanes(k)], cot_recv.at[b, k], None)
        sends.go(cot_own.at[rows], cot_oth.at[rows], pair_send.at[5 + b], pair_recv.at[5 + b], partner)
    for order in range(1, 4):
        in_place(order, b_whole, xb_recv)
    for b in range(2):
        rows = slice(b * 256, (b + 1) * 256)
        arrived(n2_oth.at[rows], pair_recv.at[3 + b], None)
        arrived(cot_oth.at[rows], pair_recv.at[5 + b], None)
    sends.drain()


def front(*args):
    hbm = pl.BlockSpec(memory_space=pl.ANY)
    outs = [
        ((4, RA, D), BF, VM), ((3, RB, D), BF, hbm), ((HALF, D), BF, VM), ((HALF, D), BF, VM), ((HALF, D), BF, VM),
        ((HALF, D), BF, hbm), ((HALF, D), BF, hbm), ((4, 1024, HD), BF, VM), ((4, LEN, 3 * HD), BF, VM),
        ((LEN, 4 * HD), BF, VM), ((4, LEN, HD), F32, VM), ((HALF, D), F32, VM), ((HALF, D), BF, VM), ((HALF, D), BF, VM),
    ]
    dma = pltpu.SemaphoreType.DMA
    return pl.pallas_call(
        front_body,
        out_shape=[jax.ShapeDtypeStruct(s, d) for s, d, _ in outs],
        in_specs=[hbm, hbm] + [VM] * 9 + [hbm] * 3,
        out_specs=[m for _, _, m in outs],
        scratch_shapes=[
            pltpu.VMEM((MICRO, CACHE, 256), BF), pltpu.VMEM((MICRO, CACHE, 256), BF),
            pltpu.VMEM((MICRO, 2, 1024, HD), BF), pltpu.VMEM((HALF, D), BF), pltpu.VMEM((HALF, D), BF),
            dma((2, 4)), dma((2, 4)), dma((2, 4)), dma((2, 4)), dma((2,)), dma((2,)), dma((2, 2)), dma((4,)),
            dma((5, 1)), dma((4, 1)), dma((4, 4)), dma((4, 4)), dma((5, 3)), dma((4, 3)), dma((4, 4)), dma((4, 4)),
            dma((7,)), dma((7,)),
        ],
        compiler_params=pltpu.CompilerParams(collective_id=0, has_side_effects=True, vmem_limit_bytes=60 << 20),
        name="front",
        cost_estimate=pl.CostEstimate(flops=int(2e10), bytes_accessed=int(5e7), transcendentals=0),
    )(*args)


def everyone(q, c, t):
    return (
        [at(q, c, t ^ j) for j in range(1, 4)] + [at(q, 1 - c, t ^ j) for j in range(4)]
        + [at(q ^ 1, c, t), at(q ^ 2, c, t)]
    )


def add_low(a, b):
    return (a.astype(F32) + b.astype(F32)).astype(BF)


def turn(i):
    return jnp.where(i < 2, 2 * i + 1, 6 - 2 * i)


def slot_of(p, k):
    return (0, (2, 1)[p], (1, 2)[p], 3)[k]


class Plane:
    def __init__(self, chunk, recv1, recv2, sems):
        self.chunk, self.recv1, self.recv2 = chunk, recv1, recv2
        self.s1, self.r1, self.s2, self.r2 = sems
        _, self.q, self.c, self.t = where_am_i()

    def copy1(self, j, p):
        return remote(self.chunk.at[j, p, pl.ds(2, 2)], self.recv1.at[j, p], self.s1.at[j, p], self.r1.at[j, p],
                      at(self.q ^ (1 + p), self.c, self.t))

    def copy2(self, j, p):
        return remote(self.chunk.at[j, p, 1], self.recv2.at[j, p], self.s2.at[j, p], self.r2.at[j, p],
                      at(self.q ^ (2 - p), self.c, self.t))

    def start(self, j):
        for p in range(2):
            self.copy1(j, p).start()

    def stage2(self, j):
        for p in range(2):
            arrived(self.recv1.at[j, p], self.r1.at[j, p], None)
            self.chunk[j, p, 1] = add_low(self.chunk[j, p, 1], self.recv1[j, p, 1])
        self.chunk[j, 0, 0] = add_low(self.chunk[j, 0, 0], self.recv1[j, 0, 0])
        for p in range(2):
            self.copy2(j, p).start()
        self.chunk[j, 1, 0] = add_low(self.chunk[j, 1, 0], self.recv1[j, 1, 0])

    def stage3(self, j, out):
        half = self.chunk.shape[3]
        for p in range(2):
            arrived(self.recv2.at[j, p], self.r2.at[j, p], None)
            out[p * half : (p + 1) * half, :] = add_low(self.chunk[j, p, 0], self.recv2[j, p])

    def drain(self):
        for j in range(4):
            for p in range(2):
                self.copy1(j, p).wait_send()
                self.copy2(j, p).wait_send()


def rows_back(sends, src, dst, send_sem, recv_sem, slots=(0, 1)):
    _, q, c, t = where_am_i()
    m = t & 1
    for s in slots:
        here = (c == (t >> 1)) & (s == m)
        for k in range(NQ):
            one = src.at[s * 256 : (s + 1) * 256, lanes(k)]
            two = dst.at[m, :, block(q ^ k, DP)]
            sends.go(one, two, send_sem.at[s, k], recv_sem.at[m, k], at(q, t >> 1, 2 * c + s),
                     when=jnp.logical_not(here))
            pl.when(here)(pltpu.make_async_copy(one, two, recv_sem.at[m, k]).start)


def rows_back_in(dst, recv_sem):
    _, q, _, _ = where_am_i()
    for m in range(2):
        for k in range(NQ):
            arrived(dst.at[m, :, block(q ^ k, DP)], recv_sem.at[m, k], None)


def put_gain(out, row, total):
    _, q, _, _ = where_am_i()
    for k in range(NQ):
        out[row : row + 1, block(q ^ k, DP)] = total[:, lanes(k)]


def local_gain(gain):
    _, q, _, _ = where_am_i()
    return jnp.concatenate([gain[:, block(q ^ k, DP)] for k in range(NQ)], axis=1)


DMA = pltpu.SemaphoreType.DMA
HBM = pl.BlockSpec(memory_space=pl.ANY)


def remote_call(body, name, number, args, places, outs, scratch, flops):
    return pl.pallas_call(
        body,
        out_shape=[jax.ShapeDtypeStruct(s, d) for s, d, _ in outs],
        in_specs=list(places),
        out_specs=[m for _, _, m in outs],
        scratch_shapes=list(scratch),
        compiler_params=pltpu.CompilerParams(collective_id=number, has_side_effects=True, vmem_limit_bytes=62 << 20),
        name=name,
        cost_estimate=pl.CostEstimate(flops=int(flops), bytes_accessed=int(5e7), transcendentals=0),
    )(*args)


def middle_body(n_own, n_oth, cot_own, cot_oth, hidden, gain_f, gate_t, up_t, down, wb,
                sums, grad_hidden, low_own, low_oth, out_rows, gain_two,
                wgu, wd, act, dgu, chunk, recv1, recv2, z_out, z_in, d_send, d_got, y_send, y_got, rows_buf,
                own_sem, got_sem, s1, r1, s2, r2, z_send, z_recv, pair_send, pair_recv, row_send, row_recv):
    _, q, c, t = where_am_i()
    partner = at(q, 1 - c, t)
    sends = Sends()

    def own_copies():
        rows = pl.ds(pl.multiple_of(c * HID, 32), HID)
        for k in range(NQ):
            for i, (w, two) in enumerate(((gate_t, wgu.at[0:HID, lanes(k)]), (up_t, wgu.at[HID : 2 * HID, lanes(k)]),
                                          (down, wd.at[0:HID, lanes(k)]))):
                yield pltpu.make_async_copy(w.at[rows, block(q ^ k, DP)], two, own_sem.at[i, k])

    def got_copies(j):
        gu = wgu.at[pl.ds(pl.multiple_of(j * (2 * HID), 32), 2 * HID)]
        d = wd.at[pl.ds(pl.multiple_of(j * HID, 32), HID)]
        yield pltpu.make_async_copy(wb.at[j - 1, pl.ds(0, 2 * HID)], gu, got_sem.at[j - 1, 0])
        yield pltpu.make_async_copy(wb.at[j - 1, pl.ds(2 * HID, HID)], d, got_sem.at[j - 1, 1])

    for j in range(1, 4):
        for copy in got_copies(j):
            copy.start()
    for copy in own_copies():
        copy.start()
    greet(everyone(q, c, t))
    plane = Plane(chunk, recv1, recv2, (s1, r1, s2, r2))

    def feed(i, carry):
        j = turn(i)

        @pl.when(j > 0)
        def _():
            for copy in got_copies(j):
                copy.wait()

        @pl.when(j == 0)
        def _():
            for copy in own_copies():
                copy.wait()

        gate_rows = pl.ds(pl.multiple_of(j * (2 * HID), 32), HID)
        up_rows = pl.ds(pl.multiple_of(j * (2 * HID) + HID, 32), HID)
        down_rows = pl.ds(pl.multiple_of(j * HID, 32), HID)
        for side, n, cot in ((0, n_own, cot_own), (1, n_oth, cot_oth)):
            for b in range(2):
                rows = slice(b * 256, (b + 1) * 256)
                cols = slice(side * HALF + b * 256, side * HALF + (b + 1) * 256)
                normed = n[rows, :]
                gate = nt(wgu[gate_rows, :], normed)
                up = nt(wgu[up_rows, :], normed)
                grad = nt(wd[down_rows, :], cot[rows, :])
                sig = 1.0 / (1.0 + jnp.exp(-gate))
                silu = gate * sig
                act[down_rows, cols] = (silu * up).astype(BF)
                dgu[gate_rows, cols] = (grad * up * sig * (1.0 + gate * (1.0 - sig))).astype(BF)
                dgu[up_rows, cols] = (grad * silu).astype(BF)
        both = pl.ds(pl.multiple_of(j * (2 * HID), 32), 2 * HID)
        half = RB // 2
        rest = 2 * HID - half
        for k in (3, 1, 2, 0):
            one, two = slot_of(0, k), slot_of(1, k)
            g = nn(dgu[both, 0:HALF], n_own[:, lanes(k)]) + nn(dgu[both, HALF:LEN], n_oth[:, lanes(k)])
            chunk[j, 0, one, :, :] = g[0:half].astype(BF)
            chunk[j, 1, two, 0:rest, :] = g[half:].astype(BF)
            if k == 0:
                plane.start(j)
            g = nn(act[down_rows, 0:HALF], cot_own[:, lanes(k)]) + nn(act[down_rows, HALF:LEN], cot_oth[:, lanes(k)])
            chunk[j, 1, two, rest:half, :] = g.astype(BF)

        @pl.when(i == 2)
        def _():
            plane.stage2(1)

        @pl.when(i == 3)
        def _():
            plane.stage2(3)

        return carry

    lax.fori_loop(0, 4, feed, 0)
    own, oth = slice(0, HALF), slice(HALF, LEN)
    d_send[...] = tn(dgu[:, oth], wgu[...]).astype(BF)
    sends.go(d_send, d_got, pair_send.at[0], pair_recv.at[0], partner)
    y_send[...] = tn(act[:, oth], wd[...]).astype(BF)
    sends.go(y_send, y_got, pair_send.at[1], pair_recv.at[1], partner)
    arrived(d_got, pair_recv.at[0], None)
    gain = local_gain(gain_f)
    total = jnp.zeros((1, D), F32)
    for b in range(2):
        rows = slice(b * 256, (b + 1) * 256)
        grad = tn(dgu[:, rows], wgu[...]) + d_got[rows, :].astype(F32)
        back, part = norm_back(grad, hidden[rows, :], gain)
        total = total + part
        g = cot_own[rows, :].astype(F32) + back
        grad_hidden[rows, :] = g
        low_own[rows, :] = g.astype(BF)
    put_gain(gain_two, 0, total)
    sends.go(low_own, low_oth, pair_send.at[2], pair_recv.at[2], partner)
    arrived(y_got, pair_recv.at[1], None)
    for b in range(2):
        rows = slice(b * 256, (b + 1) * 256)
        rows_buf[rows, :] = (hidden[rows, :] + (tn(act[:, rows], wd[...]) + y_got[rows, :].astype(F32))).astype(BF)
    rows_back(sends, rows_buf, out_rows, row_send, row_recv)
    plane.stage2(2)
    plane.stage3(1, z_out.at[0])
    plane.stage2(0)
    sends.go(z_out.at[0], z_in.at[0], z_send.at[0], z_recv.at[0], at(q, c, t ^ 1))
    plane.stage3(3, z_out.at[1])
    plane.stage3(2, sums.at[1])
    sends.go(z_out.at[1], z_in.at[1], z_send.at[1], z_recv.at[1], at(q, c, t ^ 1))
    plane.stage3(0, sums.at[0])
    for i in range(2):
        arrived(z_in.at[i], z_recv.at[i], None)
        sums[i] = add_low(sums[i], z_in[i])
    arrived(low_oth, pair_recv.at[2], None)
    rows_back_in(out_rows, row_recv)
    plane.drain()
    sends.drain()


def middle(*args):
    half16 = ((HALF, D), BF, VM)
    outs = [((2, RB, DP), BF, VM), ((HALF, D), F32, VM), half16, half16, ((MICRO, 256, D), BF, VM), ((1, D), F32, VM)]
    buf = pltpu.VMEM((HALF, D), BF)
    scratch = [
        pltpu.VMEM((4 * 2 * HID, D), BF), pltpu.VMEM((4 * HID, D), BF), pltpu.VMEM((4 * HID, LEN), BF),
        pltpu.VMEM((4 * 2 * HID, LEN), BF), pltpu.VMEM((4, 2, NQ, RB // 2, DP), BF), pltpu.VMEM((4, 2, 2, RB // 2, DP), BF),
        pltpu.VMEM((4, 2, RB // 2, DP), BF), pltpu.VMEM((2, RB, DP), BF), pltpu.VMEM((2, RB, DP), BF), buf, buf, buf, buf, buf,
        DMA((3, 4)), DMA((3, 2)), DMA((4, 2)), DMA((4, 2)), DMA((4, 2)), DMA((4, 2)), DMA((2,)), DMA((2,)), DMA((3,)), DMA((3,)),
        DMA((2, 4)), DMA((2, 4)),
    ]
    return remote_call(middle_body, "middle", 1, args, [VM] * 6 + [HBM] * 4, outs, scratch, 2.6e10)


class Spread:
    def __init__(self, piece, got, sends, send_sem, recv_sem):
        self.piece, self.got, self.sends, self.ss, self.rs = piece, got, sends, send_sem, recv_sem
        _, self.q, self.c, self.t = where_am_i()

    def place(self, k, half, p=None):
        size = self.got.shape[1] // 2
        rows = pl.ds(0, 2 * size) if p is None else pl.ds(p * size, size)
        return self.got.at[half, rows, block(self.q ^ k, DP)]

    def go(self, src, dst, number, device):
        self.sends.go(src, dst, self.ss.at[number], self.rs.at[number], device)

    def start(self):
        q, c, t = self.q, self.c, self.t
        for k in (1, 2):
            self.go(self.piece, self.place(0, c), k, at(q ^ k, c, t))
        self.go(self.piece, self.place(0, c), 4, at(q, 1 - c, t))
        pltpu.make_async_copy(self.piece, self.place(0, c), self.rs.at[0]).start()

    def relay(self):
        q, c, t = self.q, self.c, self.t
        for p, k, number in ((0, 1, 3), (1, 2, 8)):
            arrived(self.place(k, c), self.rs.at[k], None)
            self.go(self.place(k, c, p), self.place(k, c, p), number, at(q ^ (3 - k), c, t))
            self.go(self.place(k, c), self.place(k, c), 4 + k, at(q, 1 - c, t))

    def last(self):
        for p, number in ((0, 3), (1, 8)):
            arrived(self.place(3, self.c, p), self.rs.at[number], None)
        self.go(self.place(3, self.c), self.place(3, self.c), 7, at(self.q, 1 - self.c, self.t))

    def finish(self):
        arrived(self.place(0, self.c), self.rs.at[0], None)
        for k in range(NQ):
            arrived(self.place(k, 1 - self.c), self.rs.at[4 + k], None)


def tail_body(low_own, low_oth, gain_a, gain_two, sums_b, n_own_in, n_oth_in, x_in, wa_in, qkv_in, att_in, lse_in, mem_in, gh_in,
              grad_rows, got_b, got_a, gains,
              n_own, n_oth, x_own, wa, qkv_all, att_all, lse_all, mem_all, grad_hidden, load_sem, head_sem,
              da, dk, dv, dall, chunk, recv1, recv2, sums_a, zb, z1, z2, piece_b, piece_a, d_send, d_got, rows_buf, g_near, g_far,
              s1, r1, s2, r2, zb_send, zb_recv, z1_send, z1_recv, z2_send, z2_recv, pair_send, pair_recv, row_send, row_recv,
              bs, br, as_, ar, gs, gr, hs, hr):
    _, q, c, t = where_am_i()
    sends = Sends()

    def head_loads(j):
        for i, (one, two) in enumerate(((wa_in, wa), (qkv_in, qkv_all), (lse_in, lse_all), (mem_in, mem_all))):
            yield pltpu.make_async_copy(one.at[j], two.at[j], head_sem.at[j, i])

    shared = [
        pltpu.make_async_copy(one, two, load_sem.at[i])
        for i, (one, two) in enumerate(
            ((att_in, att_all), (n_own_in, n_own), (n_oth_in, n_oth), (x_in, x_own), (gh_in, grad_hidden))
        )
    ]
    for copy in shared[:3]:
        copy.start()
    for j in (1, 3, 2, 0):
        for copy in head_loads(j):
            copy.start()
    for copy in shared[3:]:
        copy.start()
    greet(everyone(q, c, t) + [at(q ^ 3, c, t)])
    plane = Plane(chunk, recv1, recv2, (s1, r1, s2, r2))
    sends.go(sums_b.at[1], zb, zb_send.at[0], zb_recv.at[0], at(q, c, t ^ 2))

    def z_first(i):
        sends.go(sums_a.at[2 * i + 1], z1.at[i], z1_send.at[i], z1_recv.at[i], at(q, c, t ^ 1))

    def attend_back(i, carry):
        j = turn(i)
        for copy in head_loads(j):
            copy.wait()
        wo = wa[j, 3 * HD : 4 * HD, :]
        qkv, lse, mem, head = qkv_all.at[j], lse_all.at[j], mem_all.at[j], block(j, HD)
        grad_o = jnp.zeros((HD, D), F32)
        for who, g in ((c, low_own), (1 - c, low_oth)):
            rows = block(who, HALF)
            grads = g[...]
            da[rows, :] = nt(grads, wo).astype(BF)
            grad_o = grad_o + tn(att_all[rows, head], grads)
        keep = causal()
        for b in range(LEN // BLK):
            rows = slice(b * BLK, (b + 1) * BLK)
            query = qkv[rows, 0:HD]
            grad = da[rows, :]
            level = lse[rows, 0:1]
            mem_k = mem[b * TOPK : (b + 1) * TOPK, :]
            mem_v = mem[512 + b * TOPK : 512 + (b + 1) * TOPK, :]
            p_d = jnp.exp(jnp.where(keep, nt(query, qkv[rows, HD : 2 * HD]), NEG) - level)
            p_f = jnp.exp(nt(query, mem_k) - level)
            g_d = nt(grad, qkv[rows, 2 * HD : 3 * HD])
            g_f = nt(grad, mem_v)
            delta = jnp.sum(p_d * g_d, axis=1, keepdims=True) + jnp.sum(p_f * g_f, axis=1, keepdims=True)
            if b:
                past = slice(0, b * BLK)
                p_p = jnp.exp(nt(query, qkv[past, HD : 2 * HD]) - level)
                g_p = nt(grad, qkv[past, 2 * HD : 3 * HD])
                delta = delta + jnp.sum(p_p * g_p, axis=1, keepdims=True)
            s_d = (p_d * (g_d - delta)).astype(BF)
            s_f = (p_f * (g_f - delta)).astype(BF)
            dq = nn(s_d, qkv[rows, HD : 2 * HD]) + nn(s_f, mem_k)
            if b:
                s_p = (p_p * (g_p - delta)).astype(BF)
                dq = dq + nn(s_p, qkv[past, HD : 2 * HD])
                dk[past, :] = dk[past, :] + tn(s_p, query)
                dv[past, :] = dv[past, :] + tn(p_p.astype(BF), grad)
            dk[rows, :] = tn(s_d, query)
            dv[rows, :] = tn(p_d.astype(BF), grad)
            dall[j, rows, 0:HD] = (dq * (HD**-0.5)).astype(BF)
        dall[j, :, HD : 2 * HD] = dk[...].astype(BF)
        dall[j, :, 2 * HD : 3 * HD] = dv[...].astype(BF)
        grad_w = tn(dall[j, block(c, HALF), :], n_own[...]) + tn(dall[j, block(1 - c, HALF), :], n_oth[...])
        for k in range(NQ):
            one, two = slot_of(0, k), slot_of(1, k)
            chunk[j, 0, one, :, :] = grad_w[0 : 2 * HD, lanes(k)].astype(BF)
            chunk[j, 1, two, 0:HD, :] = grad_w[2 * HD : 3 * HD, lanes(k)].astype(BF)
            chunk[j, 1, two, HD : 2 * HD, :] = grad_o[:, lanes(k)].astype(BF)

        @pl.when(i >= 1)
        def _():
            plane.stage2(turn(i - 1))

        plane.start(j)
        return carry

    for copy in shared[:3]:
        copy.wait()
    lax.fori_loop(0, 4, attend_back, 0)
    for copy in shared[3:]:
        copy.wait()
    weights = jnp.concatenate([wa[j, 0 : 3 * HD, :] for j in range(4)], axis=0)

    def into_rows(who, b):
        rows = pl.ds(pl.multiple_of(who * HALF + b * 256, 256), 256)
        d = jnp.concatenate([dall[j, rows, :] for j in range(4)], axis=1)
        return nn(d, weights)

    for b in range(2):
        d_send[b * 256 : (b + 1) * 256, :] = into_rows(1 - c, b).astype(BF)
    sends.go(d_send, d_got, pair_send.at[0], pair_recv.at[0], at(q, 1 - c, t))
    plane.stage3(1, sums_a.at[1])
    plane.stage3(3, sums_a.at[3])
    z_first(0)
    arrived(d_got, pair_recv.at[0], None)
    to_b = Spread(piece_b, got_b, sends, bs, br)
    to_a = Spread(piece_a, got_a, sends, as_, ar)
    gain = local_gain(gain_a)
    total = jnp.zeros((1, D), F32)
    for b in range(2):
        rows = slice(b * 256, (b + 1) * 256)
        grad = into_rows(c, b) + d_got[rows, :].astype(F32)
        back, part = norm_back(grad, x_own[rows, :].astype(F32), gain)
        total = total + part
        rows_buf[rows, :] = (grad_hidden[rows, :] + back).astype(BF)
        if b == 0:
            z_first(1)
            plane.stage2(0)
            arrived(zb, zb_recv.at[0], None)
            piece_b[...] = add_low(sums_b[0], zb[...])
            to_b.start()
    here = c * 4 + t
    put_gain(g_near.at[here], 0, total)
    g_near[here, 1:2, :] = gain_two[...]
    group = [(dc, dt) for dc in range(2) for dt in range(4) if dc + dt]
    for i, (dc, dt) in enumerate(group):
        sends.go(g_near.at[here], g_near.at[here], gs.at[i], gr.at[here], at(q, c ^ dc, t ^ dt))
    rows_back(sends, rows_buf, grad_rows, row_send, row_recv, (0,))
    plane.stage3(2, sums_a.at[2])
    arrived(z1.at[1], z1_recv.at[1], None)
    sums_a[2] = add_low(sums_a[2], z1[1])
    for dc, dt in group:
        there = (c ^ dc) * 4 + (t ^ dt)
        arrived(g_near.at[there], gr.at[there], None)
    sends.go(sums_a.at[2], z2, z2_send.at[0], z2_recv.at[0], at(q, c, t ^ 2))
    rows_back(sends, rows_buf, grad_rows, row_send, row_recv, (1,))
    part = g_near[0]
    for i in range(1, 8):
        part = part + g_near[i]
    g_far[q] = part
    for k in range(1, NQ):
        sends.go(g_far.at[q], g_far.at[q], hs.at[k], hr.at[q], at(q ^ k, c, t))
    plane.stage3(0, sums_a.at[0])
    to_b.relay()
    arrived(z1.at[0], z1_recv.at[0], None)
    arrived(z2, z2_recv.at[0], None)
    piece_a[...] = ((sums_a[0].astype(F32) + z1[0].astype(F32)) + z2[...].astype(F32)).astype(BF)
    to_a.start()
    to_b.last()
    for k in range(1, NQ):
        arrived(g_far.at[q ^ k], hr.at[q ^ k], None)
    gains[...] = ((g_far[0] + g_far[1]) + g_far[2]) + g_far[3]
    to_a.relay()
    to_a.last()
    to_b.finish()
    to_a.finish()
    rows_back_in(grad_rows, row_recv)
    plane.drain()
    sends.drain()


def tail(*args):
    outs = [((MICRO, 256, D), BF, VM), ((2, RB, D), BF, HBM), ((2, RA, D), BF, HBM), ((2, D), F32, VM)]
    buf = pltpu.VMEM((HALF, D), BF)
    scratch = [
        buf, buf, buf, pltpu.VMEM((4, RA, D), BF), pltpu.VMEM((4, LEN, 3 * HD), BF), pltpu.VMEM((LEN, 4 * HD), BF),
        pltpu.VMEM((4, LEN, HD), F32), pltpu.VMEM((4, 1024, HD), BF), pltpu.VMEM((HALF, D), F32), DMA((5,)), DMA((4, 4)),
        pltpu.VMEM((LEN, HD), BF), pltpu.VMEM((LEN, HD), F32), pltpu.VMEM((LEN, HD), F32), pltpu.VMEM((4, LEN, 3 * HD), BF),
        pltpu.VMEM((4, 2, NQ, RA // 2, DP), BF), pltpu.VMEM((4, 2, 2, RA // 2, DP), BF), pltpu.VMEM((4, 2, RA // 2, DP), BF),
        pltpu.VMEM((4, RA, DP), BF), pltpu.VMEM((RB, DP), BF), pltpu.VMEM((2, RA, DP), BF), pltpu.VMEM((RA, DP), BF),
        pltpu.VMEM((RB, DP), BF), pltpu.VMEM((RA, DP), BF), buf, buf, buf,
        pltpu.VMEM((8, 2, D), F32), pltpu.VMEM((NQ, 2, D), F32),
        DMA((4, 2)), DMA((4, 2)), DMA((4, 2)), DMA((4, 2)), DMA((1,)), DMA((1,)), DMA((2,)), DMA((2,)), DMA((1,)), DMA((1,)),
        DMA((1,)), DMA((1,)), DMA((2, 4)), DMA((2, 4)), DMA((9,)), DMA((9,)), DMA((9,)), DMA((9,)), DMA((7,)), DMA((8,)),
        DMA((4,)), DMA((4,)),
    ]
    return remote_call(tail_body, "tail", 2, args, [VM] * 5 + [HBM] * 9, outs, scratch, 1.5e10)


def per_device(tokens, attn_gain, ffn_gain, query_weight, key_weight, value_weight, out_weight, gate_weight,
               up_weight, down_weight, cache_keys, cache_values, knn_index, cotangent):
    gain_a, gain_f = attn_gain.reshape(1, D), ffn_gain.reshape(1, D)
    gate_t, up_t = gate_weight.T, up_weight.T
    wa, wb, x_own, n1_own, n1_oth, cot_own, cot_oth, mem, qkv, att, lse, hidden, n2_own, n2_oth = front(
        tokens, cotangent, gain_a, gain_f, cache_keys, cache_values, knn_index, query_weight, key_weight, value_weight,
        out_weight, gate_t, up_t, down_weight,
    )
    sums_b, grad_hidden, low_own, low_oth, output, gain_two = middle(
        n2_own, n2_oth, cot_own, cot_oth, hidden, gain_f, gate_t, up_t, down_weight, wb
    )
    grad_tokens, got_b, got_a, gains = tail(
        low_own, low_oth, gain_a, gain_two, sums_b, n1_own, n1_oth, x_own, wa, qkv, att, lse, mem, grad_hidden
    )
    if lax.axis_size("r") > 1:
        got_b = lax.psum(got_b.astype(F32), "r")
        got_a = lax.psum(got_a.astype(F32), "r")
        gains = lax.psum(gains, "r")
    gg, gu, gd = place(place_b_body, got_b, ("tall", "tall", "tall"), "place_b")
    gq, gk, gv, go = place(place_a_body, got_a, ("col", "col", "col", "row"), "place_a")
    return output, grad_tokens, gq, gk, gv, go, gg.T, gu.T, gd, gains[0], gains[1]


def solution(mesh):
    n_dp, n_t = mesh.shape["dp"], mesh.shape["tensor"]
    fine = Mesh(mesh.devices.reshape(n_dp // 8, NQ, 2, n_t), ("r", "q", "c", "t"))
    dp = ("r", "q", "c")
    rows = P(None, dp + ("t",), None)
    placed = (
        rows, P(), P(), P(None, "t"), P(None, "t"), P(None, "t"), P("t", None), P(None, "t"), P(None, "t"),
        P("t", None), P(None, dp, "t"), P(None, dp, "t"), P(None, dp, "t", None), rows,
    )
    return jax.shard_map(
        per_device,
        mesh=fine,
        in_specs=placed,
        out_specs=(
            rows, rows, P(None, "t"), P(None, "t"), P(None, "t"), P("t", None), P(None, "t"), P(None, "t"),
            P("t", None), P(), P(),
        ),
        check_vma=False,
    )
```

```python
import functools

import jax
import jax.numpy as jnp
from jax import lax
from jax.experimental import pallas as pl
from jax.experimental.pallas import tpu as pltpu
from jax.sharding import Mesh
from jax.sharding import PartitionSpec as P

HEADS = 8
HD = 128
MICRO = 2
BLK = 256
TOPK = 128
CACHE = 256
D = 1024
NQ = 4
DP = D // NQ
HALF = 512
LEN = 1024
HID = 352
RA = 4 * HD
RB = 3 * HID

EPS = 1e-06
NEG = -1e30
BF = jnp.bfloat16
F32 = jnp.float32


def nn(a, b):
    return lax.dot_general(a, b, (((1,), (0,)), ((), ())), preferred_element_type=F32)


def nt(a, b):
    return lax.dot_general(a, b, (((1,), (1,)), ((), ())), preferred_element_type=F32)


def tn(a, b):
    return lax.dot_general(a, b, (((0,), (0,)), ((), ())), preferred_element_type=F32)


VM = pl.BlockSpec(memory_space=pltpu.VMEM)


def block(index, size):
    return pl.ds(pl.multiple_of(index * size, size), size)


def lanes(k):
    return slice(k * DP, (k + 1) * DP)


def scale_of(x):
    return lax.rsqrt(jnp.mean(x * x, axis=-1, keepdims=True) + EPS)


def norm_back(grad, x, gain):
    scale = scale_of(x)
    scaled = grad * gain
    gain_part = jnp.sum(grad * x * scale, axis=0, keepdims=True)
    back = scale * scaled - x * (scale * scale * scale) * jnp.mean(scaled * x, axis=-1, keepdims=True)
    return back, gain_part


def causal():
    return lax.broadcasted_iota(jnp.int32, (BLK, BLK), 1) <= lax.broadcasted_iota(jnp.int32, (BLK, BLK), 0)


def place_a_body(got, gq, gk, gv, go):
    for half in range(2):
        rows = slice(half * HD, (half + 1) * HD)
        for i, out in enumerate((gq, gk, gv)):
            out[:, rows] = got[half, i * HD : (i + 1) * HD, :].astype(F32).T
        go[rows, :] = got[half, 3 * HD : 4 * HD, :].astype(F32)


def place_b_body(got, *outs):
    for half in range(2):
        for i, out in enumerate(outs):
            out[half * HID : (half + 1) * HID, :] = got[half, i * HID : (i + 1) * HID, :].astype(F32)


def place(body, got, kinds, name):
    shapes = {"tall": (2 * HID, D), "col": (D, 2 * HD), "row": (2 * HD, D)}
    specs = {
        "tall": pl.BlockSpec((2 * HID, DP), lambda i: (0, i)),
        "col": pl.BlockSpec((DP, 2 * HD), lambda i: (i, 0)),
        "row": pl.BlockSpec((2 * HD, DP), lambda i: (0, i)),
    }
    return pl.pallas_call(
        body,
        grid=(NQ,),
        out_shape=[jax.ShapeDtypeStruct(shapes[k], F32) for k in kinds],
        in_specs=[pl.BlockSpec((*got.shape[:2], DP), lambda i: (0, 0, i))],
        out_specs=[specs[k] for k in kinds],
        name=name,
        cost_estimate=pl.CostEstimate(flops=0, bytes_accessed=int(got.size * 6), transcendentals=0),
    )(got)


def where_am_i():
    return lax.axis_index("r"), lax.axis_index("q"), lax.axis_index("c"), lax.axis_index("t")


def at(q, c, t):
    return {"q": q, "c": c, "t": t}


def dp_at(index):
    return {"r": index // (2 * NQ), "q": lax.rem(index // 2, NQ), "c": lax.rem(index, 2)}


def remote(src, dst, send_sem, recv_sem, device):
    return pltpu.make_async_remote_copy(
        src_ref=src, dst_ref=dst, send_sem=send_sem, recv_sem=recv_sem, device_id=device,
        device_id_type=pl.DeviceIdType.MESH,
    )


def arrived(dst, recv_sem, spare):
    pltpu.make_async_copy(dst, dst, recv_sem).wait()


def greet(devices):
    barrier = pltpu.get_barrier_semaphore()
    for device in devices:
        pl.semaphore_signal(barrier, inc=1, device_id=device, device_id_type=pl.DeviceIdType.MESH)
    pl.semaphore_wait(barrier, len(devices))


class Sends:
    def __init__(self):
        self.open = []

    def go(self, src, dst, send_sem, recv_sem, device, when=None):
        copy = remote(src, dst, send_sem, recv_sem, device)
        self.open.append((copy, when))
        if when is None:
            copy.start()
        else:
            pl.when(when)(copy.start)

    def drain(self):
        for copy, when in self.open:
            if when is None:
                copy.wait_send()
            else:
                pl.when(when)(copy.wait_send)
        self.open = []


def front_body(tok, cot, gain_a, gain_f, ck, cv, knn, wq, wk, wv, wo, gate_t, up_t, down,
               wa, wb, x_own, n_own, n_oth, cot_own, cot_oth, mem, qkv, att, lse, hidden, n2_own, n2_oth,
               prev_k, prev_v, picked, o_send, o_got,
               row_send, row_recv, cot_send, cot_recv, cache_send, cache_recv, mem_send, mem_recv,
               za_send, za_recv, xa_send, xa_recv, zb_send, zb_recv, xb_send, xb_recv, pair_send, pair_recv):
    r, q, c, t = where_am_i()
    count = lax.axis_size("r") * 2 * NQ
    me = (r * NQ + q) * 2 + c
    after = dp_at(lax.rem(me + 1, count))
    across = dp_at(lax.rem(me + jnp.where(c == 0, count - 1, 1), count))
    mid = (t == 1) | (t == 2)
    second, third = jnp.where(mid, 3, 2), jnp.where(mid, 2, 3)
    partner = at(q, 1 - c, t)
    sends = Sends()
    greet(
        [at(q, c, t ^ j) for j in range(1, 4)] + [at(q, 1 - c, t ^ j) for j in range(4)]
        + [at(q ^ 1, c, t), at(q ^ 2, c, t), at(q ^ 3, c, t), across]
    )

    def rows_out(src, dst, send_sem, recv_sem):
        slot = t & 1
        for m in range(MICRO):
            here = (c == (t >> 1)) & (m == slot)
            for k in range(NQ):
                one = src.at[m, :, block(q ^ k, DP)]
                two = dst.at[block(slot, 256), lanes(k)]
                sends.go(one, two, send_sem.at[m, k], recv_sem.at[slot, k], at(q, t >> 1, 2 * c + m),
                         when=jnp.logical_not(here))
                pl.when(here)(pltpu.make_async_copy(one, two, recv_sem.at[slot, k]).start)

    def rows_in(dst, recv_sem):
        for slot in range(2):
            for k in range(NQ):
                arrived(dst.at[slot * 256 : (slot + 1) * 256, lanes(k)], recv_sem.at[slot, k], None)

    near, far_mid = at(q, c, t ^ 1), at(q, c, t ^ 3)
    ends = jnp.logical_not(mid)
    a_piece = [wa.at[0, :, lanes(0)]]
    b_piece = [w.at[pl.ds(pl.multiple_of(c * HID, 32), HID), block(q, DP)] for w in (gate_t, up_t, down)]

    def a_slot(s):
        return [wa.at[s, :, lanes(0)]]

    def b_slot(s):
        return [wb.at[s - 1, i * HID : (i + 1) * HID, lanes(0)] for i in range(3)]

    def z_first(piece, slot, send_sem, recv_sem):
        for i, (one, two) in enumerate(zip(piece, slot(1))):
            sends.go(one, two, send_sem.at[0, i], recv_sem.at[1, i], near)
        for i, (one, two) in enumerate(zip(piece, slot(3))):
            sends.go(one, two, send_sem.at[1, i], recv_sem.at[3, i], far_mid, when=mid)

    def relay_some(order, s, when, slot, whole, z_send, z_recv, x_send, x_recv):
        for i, two in enumerate(slot(s)):
            if when is None:
                arrived(two, z_recv.at[s, i], None)
            else:
                pl.when(when)(functools.partial(arrived, two, z_recv.at[s, i], None))
        if order == 1:
            for i, (one, two) in enumerate(zip(slot(1), slot(2))):
                sends.go(one, two, z_send.at[2, i], z_recv.at[2, i], far_mid, when=mid)
        elif when is mid:
            back = 2 if order == 2 else 3
            for i, (one, two) in enumerate(zip(slot(s), slot(back))):
                sends.go(one, two, z_send.at[order + 1, i], z_recv.at[back, i], near, when=mid)
        for k in (1, 2, 3) if order == 3 else (1, 2):
            sends.go(whole(s, 0), whole(s, k), x_send.at[s, k], x_recv.at[s, k], at(q ^ k, c, t), when=when)

    def relay_far(order, whole, x_send, x_recv):
        s = (None, 1, second)[order]
        arrived(whole(s, order), x_recv.at[s, order], None)
        sends.go(whole(s, order), whole(s, 3), x_send.at[s, 3], x_recv.at[s, 3], at(q ^ (3 - order), c, t))

    def in_place(order, whole, x_recv):
        s = (None, 1, second, third)[order]
        for k in range(1, NQ):
            if k != order or order == 3:
                arrived(whole(s, k), x_recv.at[s, k], None)

    def a_whole(s, k):
        return wa.at[s, :, lanes(k)]

    def b_whole(s, k):
        return wb.at[s - 1, :, lanes(k)]

    relay_a = functools.partial(relay_some, slot=a_slot, whole=a_whole, z_send=za_send, z_recv=za_recv, x_send=xa_send, x_recv=xa_recv)
    relay_b = functools.partial(relay_some, slot=b_slot, whole=b_whole, z_send=zb_send, z_recv=zb_recv, x_send=xb_send, x_recv=xb_recv)

    for i, (one, two) in enumerate(((ck, prev_k), (cv, prev_v))):
        sends.go(one, two, cache_send.at[i], cache_recv.at[i], after)
    for k in range(NQ):
        rows = block(q ^ k, DP)
        for i, w in enumerate((wq, wk, wv)):
            wa[0, i * HD : (i + 1) * HD, lanes(k)] = w[rows, block(c, HD)].T
        wa[0, 3 * HD : 4 * HD, lanes(k)] = wo[block(c, HD), rows]
        if k == 1:
            z_first(a_piece, a_slot, za_send, za_recv)
            z_first(b_piece, b_slot, zb_send, zb_recv)
            rows_out(tok, x_own, row_send, row_recv)

    relay_a(1, 1, None)
    relay_a(2, 3, mid)
    for i, two in enumerate((prev_k, prev_v)):
        arrived(two, cache_recv.at[i], None)

    def pick(i, carry):
        m, h, b = i // 8, (i // 4) % 2, i % 4
        cols = block(h, HD)
        picks = knn[m, b, pl.ds(h, 1), :]
        rows = lax.broadcasted_iota(jnp.int32, (CACHE, TOPK), 0)
        hot_own = jnp.where(rows == picks, 1.0, 0.0).astype(BF)
        hot_prev = jnp.where(rows + CACHE == picks, 1.0, 0.0).astype(BF)
        for kv, own, prev in ((0, ck, prev_k), (1, cv, prev_v)):
            got = tn(hot_own, own[m, :, cols]) + tn(hot_prev, prev[m, :, cols])
            picked[m, h, pl.ds(pl.multiple_of(kv * 512 + b * TOPK, TOPK), TOPK), :] = got.astype(BF)
        return carry

    lax.fori_loop(0, 16, pick, 0)
    relay_b(1, 1, None)
    relay_b(2, 3, mid)
    relay_far(1, a_whole, xa_send, xa_recv)

    def send_mem():
        for m in range(MICRO):
            for h in range(2):
                kind = t ^ (2 * c + m)
                here = (c == h) & (kind == 0)
                sends.go(picked.at[m, h], mem.at[kind], mem_send.at[m, h], mem_recv.at[kind], at(q, h, 2 * c + m),
                         when=jnp.logical_not(here))
                pl.when(here)(pltpu.make_async_copy(picked.at[m, h], mem.at[kind], mem_recv.at[kind]).start)

    relay_far(1, b_whole, xb_send, xb_recv)
    rows_in(x_own, row_recv)
    gain = jnp.concatenate([gain_a[:, block(q ^ k, DP)] for k in range(NQ)], axis=1)
    for i in range(2):
        rows = slice(i * 256, (i + 1) * 256)
        x = x_own[rows, :].astype(F32)
        n_own[rows, :] = (x * scale_of(x) * gain).astype(BF)
    sends.go(n_own, n_oth, pair_send.at[0], pair_recv.at[0], partner)

    def project(j, who, n):
        acc = nt(n[...], wa[j, 0 : 3 * HD, :])
        rows = block(who, HALF)
        qkv[j, rows, 0:HD] = (acc[:, 0:HD] * (HD**-0.5)).astype(BF)
        qkv[j, rows, HD : 3 * HD] = acc[:, HD : 3 * HD].astype(BF)

    def attend(j):
        keep = causal()
        for b in range(LEN // BLK):
            rows = slice(b * BLK, (b + 1) * BLK)
            query = qkv[j, rows, 0:HD]
            diag = jnp.where(keep, nt(query, qkv[j, rows, HD : 2 * HD]), NEG)
            far = nt(query, mem[j, b * TOPK : (b + 1) * TOPK, :])
            top = jnp.maximum(jnp.max(diag, axis=1, keepdims=True), jnp.max(far, axis=1, keepdims=True))
            if b:
                past = nt(query, qkv[j, 0 : b * BLK, HD : 2 * HD])
                top = jnp.maximum(top, jnp.max(past, axis=1, keepdims=True))
            diag = jnp.exp(diag - top)
            far = jnp.exp(far - top)
            total = jnp.sum(diag, axis=1, keepdims=True) + jnp.sum(far, axis=1, keepdims=True)
            if b:
                past = jnp.exp(past - top)
                total = total + jnp.sum(past, axis=1, keepdims=True)
            inverse = 1.0 / total
            out = nn((diag * inverse).astype(BF), qkv[j, rows, 2 * HD : 3 * HD])
            out = out + nn((far * inverse).astype(BF), mem[j, 512 + b * TOPK : 512 + (b + 1) * TOPK, :])
            if b:
                out = out + nn((past * inverse).astype(BF), qkv[j, 0 : b * BLK, 2 * HD : 3 * HD])
            att[rows, block(j, HD)] = out.astype(BF)
            lse[j, rows, :] = jnp.broadcast_to(top + jnp.log(total), (BLK, HD))

    def got_mem(j):
        arrived(mem.at[j], mem_recv.at[j], None)

    relay_a(2, 2, ends)
    relay_a(3, 2, mid)
    relay_b(2, 2, ends)
    send_mem()
    relay_b(3, 2, mid)
    rows_out(cot, cot_own, cot_send, cot_recv)
    relay_far(2, a_whole, xa_send, xa_recv)
    arrived(n_oth, pair_recv.at[0], None)
    relay_far(2, b_whole, xb_send, xb_recv)
    relay_a(3, 3, ends)
    relay_b(3, 3, ends)

    def head(i, carry):
        j = jnp.where(i < 2, i, jnp.where(i == 2, second, third))
        for order in range(1, 4):
            pl.when(i == order)(functools.partial(in_place, order, a_whole, xa_recv))
        project(j, c, n_own)
        project(j, 1 - c, n_oth)
        got_mem(j)
        attend(j)
        return carry

    lax.fori_loop(0, 4, head, 0)
    weights = jnp.concatenate([wa[j, 3 * HD : 4 * HD, :] for j in range(4)], axis=0)
    for b in range(2):
        rows = slice(b * 256, (b + 1) * 256)
        o_send[rows, :] = nn(att[block(2 * (1 - c) + b, 256), :], weights).astype(BF)
        sends.go(o_send.at[rows], o_got.at[rows], pair_send.at[1 + b], pair_recv.at[1 + b], partner)
    hidden[...] = nn(att[block(c, HALF), :], weights)
    gain = jnp.concatenate([gain_f[:, block(q ^ k, DP)] for k in range(NQ)], axis=1)
    for b in range(2):
        rows = slice(b * 256, (b + 1) * 256)
        arrived(o_got.at[rows], pair_recv.at[1 + b], None)
        h = x_own[rows, :].astype(F32) + (hidden[rows, :] + o_got[rows, :].astype(F32))
        hidden[rows, :] = h
        n2_own[rows, :] = (h * scale_of(h) * gain).astype(BF)
        sends.go(n2_own.at[rows], n2_oth.at[rows], pair_send.at[3 + b], pair_recv.at[3 + b], partner)
    for b in range(2):
        rows = slice(b * 256, (b + 1) * 256)
        for k in range(NQ):
            arrived(cot_own.at[rows, lanes(k)], cot_recv.at[b, k], None)
        sends.go(cot_own.at[rows], cot_oth.at[rows], pair_send.at[5 + b], pair_recv.at[5 + b], partner)
    for order in range(1, 4):
        in_place(order, b_whole, xb_recv)
    for b in range(2):
        rows = slice(b * 256, (b + 1) * 256)
        arrived(n2_oth.at[rows], pair_recv.at[3 + b], None)
        arrived(cot_oth.at[rows], pair_recv.at[5 + b], None)
    sends.drain()


def front(*args):
    hbm = pl.BlockSpec(memory_space=pl.ANY)
    outs = [
        ((4, RA, D), BF, VM), ((3, RB, D), BF, hbm), ((HALF, D), BF, VM), ((HALF, D), BF, VM), ((HALF, D), BF, VM),
        ((HALF, D), BF, hbm), ((HALF, D), BF, hbm), ((4, 1024, HD), BF, VM), ((4, LEN, 3 * HD), BF, VM),
        ((LEN, 4 * HD), BF, VM), ((4, LEN, HD), F32, VM), ((HALF, D), F32, VM), ((HALF, D), BF, VM), ((HALF, D), BF, VM),
    ]
    dma = pltpu.SemaphoreType.DMA
    return pl.pallas_call(
        front_body,
        out_shape=[jax.ShapeDtypeStruct(s, d) for s, d, _ in outs],
        in_specs=[hbm, hbm] + [VM] * 9 + [hbm] * 3,
        out_specs=[m for _, _, m in outs],
        scratch_shapes=[
            pltpu.VMEM((MICRO, CACHE, 256), BF), pltpu.VMEM((MICRO, CACHE, 256), BF),
            pltpu.VMEM((MICRO, 2, 1024, HD), BF), pltpu.VMEM((HALF, D), BF), pltpu.VMEM((HALF, D), BF),
            dma((2, 4)), dma((2, 4)), dma((2, 4)), dma((2, 4)), dma((2,)), dma((2,)), dma((2, 2)), dma((4,)),
            dma((5, 1)), dma((4, 1)), dma((4, 4)), dma((4, 4)), dma((5, 3)), dma((4, 3)), dma((4, 4)), dma((4, 4)),
            dma((7,)), dma((7,)),
        ],
        compiler_params=pltpu.CompilerParams(collective_id=0, has_side_effects=True, vmem_limit_bytes=60 << 20),
        name="front",
        cost_estimate=pl.CostEstimate(flops=int(2e10), bytes_accessed=int(5e7), transcendentals=0),
    )(*args)


def everyone(q, c, t):
    return (
        [at(q, c, t ^ j) for j in range(1, 4)] + [at(q, 1 - c, t ^ j) for j in range(4)]
        + [at(q ^ 1, c, t), at(q ^ 2, c, t)]
    )


def add_low(a, b):
    return (a.astype(F32) + b.astype(F32)).astype(BF)


def turn(i):
    return jnp.where(i < 2, 2 * i + 1, 6 - 2 * i)


def slot_of(p, k):
    return (0, (2, 1)[p], (1, 2)[p], 3)[k]


class Plane:
    def __init__(self, chunk, recv1, recv2, sems):
        self.chunk, self.recv1, self.recv2 = chunk, recv1, recv2
        self.s1, self.r1, self.s2, self.r2 = sems
        _, self.q, self.c, self.t = where_am_i()

    def copy1(self, j, p):
        return remote(self.chunk.at[j, p, pl.ds(2, 2)], self.recv1.at[j, p], self.s1.at[j, p], self.r1.at[j, p],
                      at(self.q ^ (1 + p), self.c, self.t))

    def copy2(self, j, p):
        return remote(self.chunk.at[j, p, 1], self.recv2.at[j, p], self.s2.at[j, p], self.r2.at[j, p],
                      at(self.q ^ (2 - p), self.c, self.t))

    def start(self, j):
        for p in range(2):
            self.copy1(j, p).start()

    def stage2(self, j):
        for p in range(2):
            arrived(self.recv1.at[j, p], self.r1.at[j, p], None)
            self.chunk[j, p, 1] = add_low(self.chunk[j, p, 1], self.recv1[j, p, 1])
        self.chunk[j, 0, 0] = add_low(self.chunk[j, 0, 0], self.recv1[j, 0, 0])
        for p in range(2):
            self.copy2(j, p).start()
        self.chunk[j, 1, 0] = add_low(self.chunk[j, 1, 0], self.recv1[j, 1, 0])

    def stage3(self, j, out):
        half = self.chunk.shape[3]
        for p in range(2):
            arrived(self.recv2.at[j, p], self.r2.at[j, p], None)
            out[p * half : (p + 1) * half, :] = add_low(self.chunk[j, p, 0], self.recv2[j, p])

    def drain(self):
        for j in range(4):
            for p in range(2):
                self.copy1(j, p).wait_send()
                self.copy2(j, p).wait_send()


def rows_back(sends, src, dst, send_sem, recv_sem, slots=(0, 1)):
    _, q, c, t = where_am_i()
    m = t & 1
    for s in slots:
        here = (c == (t >> 1)) & (s == m)
        for k in range(NQ):
            one = src.at[s * 256 : (s + 1) * 256, lanes(k)]
            two = dst.at[m, :, block(q ^ k, DP)]
            sends.go(one, two, send_sem.at[s, k], recv_sem.at[m, k], at(q, t >> 1, 2 * c + s),
                     when=jnp.logical_not(here))
            pl.when(here)(pltpu.make_async_copy(one, two, recv_sem.at[m, k]).start)


def rows_back_in(dst, recv_sem):
    _, q, _, _ = where_am_i()
    for m in range(2):
        for k in range(NQ):
            arrived(dst.at[m, :, block(q ^ k, DP)], recv_sem.at[m, k], None)


def put_gain(out, row, total):
    _, q, _, _ = where_am_i()
    for k in range(NQ):
        out[row : row + 1, block(q ^ k, DP)] = total[:, lanes(k)]


def local_gain(gain):
    _, q, _, _ = where_am_i()
    return jnp.concatenate([gain[:, block(q ^ k, DP)] for k in range(NQ)], axis=1)


DMA = pltpu.SemaphoreType.DMA
HBM = pl.BlockSpec(memory_space=pl.ANY)


def remote_call(body, name, number, args, places, outs, scratch, flops):
    return pl.pallas_call(
        body,
        out_shape=[jax.ShapeDtypeStruct(s, d) for s, d, _ in outs],
        in_specs=list(places),
        out_specs=[m for _, _, m in outs],
        scratch_shapes=list(scratch),
        compiler_params=pltpu.CompilerParams(collective_id=number, has_side_effects=True, vmem_limit_bytes=62 << 20),
        name=name,
        cost_estimate=pl.CostEstimate(flops=int(flops), bytes_accessed=int(5e7), transcendentals=0),
    )(*args)


def middle_body(n_own, n_oth, cot_own, cot_oth, hidden, gain_f, gate_t, up_t, down, wb,
                sums, grad_hidden, low_own, low_oth, out_rows, gain_two,
                wgu, wd, act, dgu, chunk, recv1, recv2, z_out, z_in, d_send, d_got, y_send, y_got, rows_buf,
                own_sem, got_sem, s1, r1, s2, r2, z_send, z_recv, pair_send, pair_recv, row_send, row_recv):
    _, q, c, t = where_am_i()
    partner = at(q, 1 - c, t)
    sends = Sends()

    def own_copies():
        rows = pl.ds(pl.multiple_of(c * HID, 32), HID)
        for k in range(NQ):
            for i, (w, two) in enumerate(((gate_t, wgu.at[0:HID, lanes(k)]), (up_t, wgu.at[HID : 2 * HID, lanes(k)]),
                                          (down, wd.at[0:HID, lanes(k)]))):
                yield pltpu.make_async_copy(w.at[rows, block(q ^ k, DP)], two, own_sem.at[i, k])

    def got_copies(j):
        gu = wgu.at[pl.ds(pl.multiple_of(j * (2 * HID), 32), 2 * HID)]
        d = wd.at[pl.ds(pl.multiple_of(j * HID, 32), HID)]
        yield pltpu.make_async_copy(wb.at[j - 1, pl.ds(0, 2 * HID)], gu, got_sem.at[j - 1, 0])
        yield pltpu.make_async_copy(wb.at[j - 1, pl.ds(2 * HID, HID)], d, got_sem.at[j - 1, 1])

    for j in range(1, 4):
        for copy in got_copies(j):
            copy.start()
    for copy in own_copies():
        copy.start()
    greet(everyone(q, c, t))
    plane = Plane(chunk, recv1, recv2, (s1, r1, s2, r2))

    def feed(i, carry):
        j = turn(i)

        @pl.when(j > 0)
        def _():
            for copy in got_copies(j):
                copy.wait()

        @pl.when(j == 0)
        def _():
            for copy in own_copies():
                copy.wait()

        gate_rows = pl.ds(pl.multiple_of(j * (2 * HID), 32), HID)
        up_rows = pl.ds(pl.multiple_of(j * (2 * HID) + HID, 32), HID)
        down_rows = pl.ds(pl.multiple_of(j * HID, 32), HID)
        for side, n, cot in ((0, n_own, cot_own), (1, n_oth, cot_oth)):
            for b in range(2):
                rows = slice(b * 256, (b + 1) * 256)
                cols = slice(side * HALF + b * 256, side * HALF + (b + 1) * 256)
                normed = n[rows, :]
                gate = nt(wgu[gate_rows, :], normed)
                up = nt(wgu[up_rows, :], normed)
                grad = nt(wd[down_rows, :], cot[rows, :])
                sig = 1.0 / (1.0 + jnp.exp(-gate))
                silu = gate * sig
                act[down_rows, cols] = (silu * up).astype(BF)
                dgu[gate_rows, cols] = (grad * up * sig * (1.0 + gate * (1.0 - sig))).astype(BF)
                dgu[up_rows, cols] = (grad * silu).astype(BF)
        both = pl.ds(pl.multiple_of(j * (2 * HID), 32), 2 * HID)
        half = RB // 2
        rest = 2 * HID - half
        for k in (3, 1, 2, 0):
            one, two = slot_of(0, k), slot_of(1, k)
            g = nn(dgu[both, 0:HALF], n_own[:, lanes(k)]) + nn(dgu[both, HALF:LEN], n_oth[:, lanes(k)])
            chunk[j, 0, one, :, :] = g[0:half].astype(BF)
            chunk[j, 1, two, 0:rest, :] = g[half:].astype(BF)
            if k == 0:
                plane.start(j)
            g = nn(act[down_rows, 0:HALF], cot_own[:, lanes(k)]) + nn(act[down_rows, HALF:LEN], cot_oth[:, lanes(k)])
            chunk[j, 1, two, rest:half, :] = g.astype(BF)

        @pl.when(i == 2)
        def _():
            plane.stage2(1)

        @pl.when(i == 3)
        def _():
            plane.stage2(3)

        return carry

    lax.fori_loop(0, 4, feed, 0)
    own, oth = slice(0, HALF), slice(HALF, LEN)
    d_send[...] = tn(dgu[:, oth], wgu[...]).astype(BF)
    sends.go(d_send, d_got, pair_send.at[0], pair_recv.at[0], partner)
    y_send[...] = tn(act[:, oth], wd[...]).astype(BF)
    sends.go(y_send, y_got, pair_send.at[1], pair_recv.at[1], partner)
    arrived(d_got, pair_recv.at[0], None)
    gain = local_gain(gain_f)
    total = jnp.zeros((1, D), F32)
    for b in range(2):
        rows = slice(b * 256, (b + 1) * 256)
        grad = tn(dgu[:, rows], wgu[...]) + d_got[rows, :].astype(F32)
        back, part = norm_back(grad, hidden[rows, :], gain)
        total = total + part
        g = cot_own[rows, :].astype(F32) + back
        grad_hidden[rows, :] = g
        low_own[rows, :] = g.astype(BF)
    put_gain(gain_two, 0, total)
    sends.go(low_own, low_oth, pair_send.at[2], pair_recv.at[2], partner)
    arrived(y_got, pair_recv.at[1], None)
    for b in range(2):
        rows = slice(b * 256, (b + 1) * 256)
        rows_buf[rows, :] = (hidden[rows, :] + (tn(act[:, rows], wd[...]) + y_got[rows, :].astype(F32))).astype(BF)
    rows_back(sends, rows_buf, out_rows, row_send, row_recv)
    plane.stage2(2)
    plane.stage3(1, z_out.at[0])
    plane.stage2(0)
    sends.go(z_out.at[0], z_in.at[0], z_send.at[0], z_recv.at[0], at(q, c, t ^ 1))
    plane.stage3(3, z_out.at[1])
    plane.stage3(2, sums.at[1])
    sends.go(z_out.at[1], z_in.at[1], z_send.at[1], z_recv.at[1], at(q, c, t ^ 1))
    plane.stage3(0, sums.at[0])
    for i in range(2):
        arrived(z_in.at[i], z_recv.at[i], None)
        sums[i] = add_low(sums[i], z_in[i])
    arrived(low_oth, pair_recv.at[2], None)
    rows_back_in(out_rows, row_recv)
    plane.drain()
    sends.drain()


def middle(*args):
    half16 = ((HALF, D), BF, VM)
    outs = [((2, RB, DP), BF, VM), ((HALF, D), F32, VM), half16, half16, ((MICRO, 256, D), BF, VM), ((1, D), F32, VM)]
    buf = pltpu.VMEM((HALF, D), BF)
    scratch = [
        pltpu.VMEM((4 * 2 * HID, D), BF), pltpu.VMEM((4 * HID, D), BF), pltpu.VMEM((4 * HID, LEN), BF),
        pltpu.VMEM((4 * 2 * HID, LEN), BF), pltpu.VMEM((4, 2, NQ, RB // 2, DP), BF), pltpu.VMEM((4, 2, 2, RB // 2, DP), BF),
        pltpu.VMEM((4, 2, RB // 2, DP), BF), pltpu.VMEM((2, RB, DP), BF), pltpu.VMEM((2, RB, DP), BF), buf, buf, buf, buf, buf,
        DMA((3, 4)), DMA((3, 2)), DMA((4, 2)), DMA((4, 2)), DMA((4, 2)), DMA((4, 2)), DMA((2,)), DMA((2,)), DMA((3,)), DMA((3,)),
        DMA((2, 4)), DMA((2, 4)),
    ]
    return remote_call(middle_body, "middle", 1, args, [VM] * 6 + [HBM] * 4, outs, scratch, 2.6e10)


class Spread:
    def __init__(self, piece, got, sends, send_sem, recv_sem):
        self.piece, self.got, self.sends, self.ss, self.rs = piece, got, sends, send_sem, recv_sem
        _, self.q, self.c, self.t = where_am_i()

    def place(self, k, half, p=None):
        size = self.got.shape[1] // 2
        rows = pl.ds(0, 2 * size) if p is None else pl.ds(p * size, size)
        return self.got.at[half, rows, block(self.q ^ k, DP)]

    def go(self, src, dst, number, device):
        self.sends.go(src, dst, self.ss.at[number], self.rs.at[number], device)

    def start(self):
        q, c, t = self.q, self.c, self.t
        for k in (1, 2):
            self.go(self.piece, self.place(0, c), k, at(q ^ k, c, t))
        self.go(self.piece, self.place(0, c), 4, at(q, 1 - c, t))
        pltpu.make_async_copy(self.piece, self.place(0, c), self.rs.at[0]).start()

    def relay(self):
        q, c, t = self.q, self.c, self.t
        for p, k, number in ((0, 1, 3), (1, 2, 8)):
            arrived(self.place(k, c), self.rs.at[k], None)
            self.go(self.place(k, c, p), self.place(k, c, p), number, at(q ^ (3 - k), c, t))
            self.go(self.place(k, c), self.place(k, c), 4 + k, at(q, 1 - c, t))

    def last(self):
        for p, number in ((0, 3), (1, 8)):
            arrived(self.place(3, self.c, p), self.rs.at[number], None)
        self.go(self.place(3, self.c), self.place(3, self.c), 7, at(self.q, 1 - self.c, self.t))

    def finish(self):
        arrived(self.place(0, self.c), self.rs.at[0], None)
        for k in range(NQ):
            arrived(self.place(k, 1 - self.c), self.rs.at[4 + k], None)


def tail_body(low_own, low_oth, gain_a, gain_two, sums_b, n_own_in, n_oth_in, x_in, wa_in, qkv_in, att_in, lse_in, mem_in, gh_in,
              grad_rows, got_b, got_a, gains,
              n_own, n_oth, x_own, wa, qkv_all, att_all, lse_all, mem_all, grad_hidden, load_sem, head_sem,
              da, dk, dv, dall, chunk, recv1, recv2, sums_a, zb, z1, z2, piece_b, piece_a, d_send, d_got, rows_buf, g_near, g_far,
              s1, r1, s2, r2, zb_send, zb_recv, z1_send, z1_recv, z2_send, z2_recv, pair_send, pair_recv, row_send, row_recv,
              bs, br, as_, ar, gs, gr, hs, hr):
    _, q, c, t = where_am_i()
    sends = Sends()

    def head_loads(j):
        for i, (one, two) in enumerate(((wa_in, wa), (qkv_in, qkv_all), (lse_in, lse_all), (mem_in, mem_all))):
            yield pltpu.make_async_copy(one.at[j], two.at[j], head_sem.at[j, i])

    shared = [
        pltpu.make_async_copy(one, two, load_sem.at[i])
        for i, (one, two) in enumerate(
            ((att_in, att_all), (n_own_in, n_own), (n_oth_in, n_oth), (x_in, x_own), (gh_in, grad_hidden))
        )
    ]
    for copy in shared[:3]:
        copy.start()
    for j in (1, 3, 2, 0):
        for copy in head_loads(j):
            copy.start()
    for copy in shared[3:]:
        copy.start()
    greet(everyone(q, c, t) + [at(q ^ 3, c, t)])
    plane = Plane(chunk, recv1, recv2, (s1, r1, s2, r2))
    sends.go(sums_b.at[1], zb, zb_send.at[0], zb_recv.at[0], at(q, c, t ^ 2))

    def z_first(i):
        sends.go(sums_a.at[2 * i + 1], z1.at[i], z1_send.at[i], z1_recv.at[i], at(q, c, t ^ 1))

    def attend_back(i, carry):
        j = turn(i)
        for copy in head_loads(j):
            copy.wait()
        wo = wa[j, 3 * HD : 4 * HD, :]
        qkv, lse, mem, head = qkv_all.at[j], lse_all.at[j], mem_all.at[j], block(j, HD)
        grad_o = jnp.zeros((HD, D), F32)
        for who, g in ((c, low_own), (1 - c, low_oth)):
            rows = block(who, HALF)
            grads = g[...]
            da[rows, :] = nt(grads, wo).astype(BF)
            grad_o = grad_o + tn(att_all[rows, head], grads)
        keep = causal()
        for b in range(LEN // BLK):
            rows = slice(b * BLK, (b + 1) * BLK)
            query = qkv[rows, 0:HD]
            grad = da[rows, :]
            level = lse[rows, 0:1]
            mem_k = mem[b * TOPK : (b + 1) * TOPK, :]
            mem_v = mem[512 + b * TOPK : 512 + (b + 1) * TOPK, :]
            p_d = jnp.exp(jnp.where(keep, nt(query, qkv[rows, HD : 2 * HD]), NEG) - level)
            p_f = jnp.exp(nt(query, mem_k) - level)
            g_d = nt(grad, qkv[rows, 2 * HD : 3 * HD])
            g_f = nt(grad, mem_v)
            delta = jnp.sum(p_d * g_d, axis=1, keepdims=True) + jnp.sum(p_f * g_f, axis=1, keepdims=True)
            if b:
                past = slice(0, b * BLK)
                p_p = jnp.exp(nt(query, qkv[past, HD : 2 * HD]) - level)
                g_p = nt(grad, qkv[past, 2 * HD : 3 * HD])
                delta = delta + jnp.sum(p_p * g_p, axis=1, keepdims=True)
            s_d = (p_d * (g_d - delta)).astype(BF)
            s_f = (p_f * (g_f - delta)).astype(BF)
            dq = nn(s_d, qkv[rows, HD : 2 * HD]) + nn(s_f, mem_k)
            if b:
                s_p = (p_p * (g_p - delta)).astype(BF)
                dq = dq + nn(s_p, qkv[past, HD : 2 * HD])
                dk[past, :] = dk[past, :] + tn(s_p, query)
                dv[past, :] = dv[past, :] + tn(p_p.astype(BF), grad)
            dk[rows, :] = tn(s_d, query)
            dv[rows, :] = tn(p_d.astype(BF), grad)
            dall[j, rows, 0:HD] = (dq * (HD**-0.5)).astype(BF)
        dall[j, :, HD : 2 * HD] = dk[...].astype(BF)
        dall[j, :, 2 * HD : 3 * HD] = dv[...].astype(BF)
        grad_w = tn(dall[j, block(c, HALF), :], n_own[...]) + tn(dall[j, block(1 - c, HALF), :], n_oth[...])
        for k in range(NQ):
            one, two = slot_of(0, k), slot_of(1, k)
            chunk[j, 0, one, :, :] = grad_w[0 : 2 * HD, lanes(k)].astype(BF)
            chunk[j, 1, two, 0:HD, :] = grad_w[2 * HD : 3 * HD, lanes(k)].astype(BF)
            chunk[j, 1, two, HD : 2 * HD, :] = grad_o[:, lanes(k)].astype(BF)

        @pl.when(i >= 1)
        def _():
            plane.stage2(turn(i - 1))

        plane.start(j)
        return carry

    for copy in shared[:3]:
        copy.wait()
    lax.fori_loop(0, 4, attend_back, 0)
    for copy in shared[3:]:
        copy.wait()
    weights = jnp.concatenate([wa[j, 0 : 3 * HD, :] for j in range(4)], axis=0)

    def into_rows(who, b):
        rows = pl.ds(pl.multiple_of(who * HALF + b * 256, 256), 256)
        d = jnp.concatenate([dall[j, rows, :] for j in range(4)], axis=1)
        return nn(d, weights)

    for b in range(2):
        d_send[b * 256 : (b + 1) * 256, :] = into_rows(1 - c, b).astype(BF)
    sends.go(d_send, d_got, pair_send.at[0], pair_recv.at[0], at(q, 1 - c, t))
    plane.stage3(1, sums_a.at[1])
    plane.stage3(3, sums_a.at[3])
    z_first(0)
    arrived(d_got, pair_recv.at[0], None)
    to_b = Spread(piece_b, got_b, sends, bs, br)
    to_a = Spread(piece_a, got_a, sends, as_, ar)
    gain = local_gain(gain_a)
    total = jnp.zeros((1, D), F32)
    for b in range(2):
        rows = slice(b * 256, (b + 1) * 256)
        grad = into_rows(c, b) + d_got[rows, :].astype(F32)
        back, part = norm_back(grad, x_own[rows, :].astype(F32), gain)
        total = total + part
        rows_buf[rows, :] = (grad_hidden[rows, :] + back).astype(BF)
        if b == 0:
            z_first(1)
            plane.stage2(0)
            arrived(zb, zb_recv.at[0], None)
            piece_b[...] = add_low(sums_b[0], zb[...])
            to_b.start()
    here = c * 4 + t
    put_gain(g_near.at[here], 0, total)
    g_near[here, 1:2, :] = gain_two[...]
    group = [(dc, dt) for dc in range(2) for dt in range(4) if dc + dt]
    for i, (dc, dt) in enumerate(group):
        sends.go(g_near.at[here], g_near.at[here], gs.at[i], gr.at[here], at(q, c ^ dc, t ^ dt))
    rows_back(sends, rows_buf, grad_rows, row_send, row_recv, (0,))
    plane.stage3(2, sums_a.at[2])
    arrived(z1.at[1], z1_recv.at[1], None)
    sums_a[2] = add_low(sums_a[2], z1[1])
    for dc, dt in group:
        there = (c ^ dc) * 4 + (t ^ dt)
        arrived(g_near.at[there], gr.at[there], None)
    sends.go(sums_a.at[2], z2, z2_send.at[0], z2_recv.at[0], at(q, c, t ^ 2))
    rows_back(sends, rows_buf, grad_rows, row_send, row_recv, (1,))
    part = g_near[0]
    for i in range(1, 8):
        part = part + g_near[i]
    g_far[q] = part
    for k in range(1, NQ):
        sends.go(g_far.at[q], g_far.at[q], hs.at[k], hr.at[q], at(q ^ k, c, t))
    plane.stage3(0, sums_a.at[0])
    to_b.relay()
    arrived(z1.at[0], z1_recv.at[0], None)
    arrived(z2, z2_recv.at[0], None)
    piece_a[...] = ((sums_a[0].astype(F32) + z1[0].astype(F32)) + z2[...].astype(F32)).astype(BF)
    to_a.start()
    to_b.last()
    for k in range(1, NQ):
        arrived(g_far.at[q ^ k], hr.at[q ^ k], None)
    gains[...] = ((g_far[0] + g_far[1]) + g_far[2]) + g_far[3]
    to_a.relay()
    to_a.last()
    to_b.finish()
    to_a.finish()
    rows_back_in(grad_rows, row_recv)
    plane.drain()
    sends.drain()


def tail(*args):
    outs = [((MICRO, 256, D), BF, VM), ((2, RB, D), BF, HBM), ((2, RA, D), BF, HBM), ((2, D), F32, VM)]
    buf = pltpu.VMEM((HALF, D), BF)
    scratch = [
        buf, buf, buf, pltpu.VMEM((4, RA, D), BF), pltpu.VMEM((4, LEN, 3 * HD), BF), pltpu.VMEM((LEN, 4 * HD), BF),
        pltpu.VMEM((4, LEN, HD), F32), pltpu.VMEM((4, 1024, HD), BF), pltpu.VMEM((HALF, D), F32), DMA((5,)), DMA((4, 4)),
        pltpu.VMEM((LEN, HD), BF), pltpu.VMEM((LEN, HD), F32), pltpu.VMEM((LEN, HD), F32), pltpu.VMEM((4, LEN, 3 * HD), BF),
        pltpu.VMEM((4, 2, NQ, RA // 2, DP), BF), pltpu.VMEM((4, 2, 2, RA // 2, DP), BF), pltpu.VMEM((4, 2, RA // 2, DP), BF),
        pltpu.VMEM((4, RA, DP), BF), pltpu.VMEM((RB, DP), BF), pltpu.VMEM((2, RA, DP), BF), pltpu.VMEM((RA, DP), BF),
        pltpu.VMEM((RB, DP), BF), pltpu.VMEM((RA, DP), BF), buf, buf, buf,
        pltpu.VMEM((8, 2, D), F32), pltpu.VMEM((NQ, 2, D), F32),
        DMA((4, 2)), DMA((4, 2)), DMA((4, 2)), DMA((4, 2)), DMA((1,)), DMA((1,)), DMA((2,)), DMA((2,)), DMA((1,)), DMA((1,)),
        DMA((1,)), DMA((1,)), DMA((2, 4)), DMA((2, 4)), DMA((9,)), DMA((9,)), DMA((9,)), DMA((9,)), DMA((7,)), DMA((8,)),
        DMA((4,)), DMA((4,)),
    ]
    return remote_call(tail_body, "tail", 2, args, [VM] * 5 + [HBM] * 9, outs, scratch, 1.5e10)


def per_device(tokens, attn_gain, ffn_gain, query_weight, key_weight, value_weight, out_weight, gate_weight,
               up_weight, down_weight, cache_keys, cache_values, knn_index, cotangent):
    gain_a, gain_f = attn_gain.reshape(1, D), ffn_gain.reshape(1, D)
    gate_t, up_t = gate_weight.T, up_weight.T
    wa, wb, x_own, n1_own, n1_oth, cot_own, cot_oth, mem, qkv, att, lse, hidden, n2_own, n2_oth = front(
        tokens, cotangent, gain_a, gain_f, cache_keys, cache_values, knn_index, query_weight, key_weight, value_weight,
        out_weight, gate_t, up_t, down_weight,
    )
    sums_b, grad_hidden, low_own, low_oth, output, gain_two = middle(
        n2_own, n2_oth, cot_own, cot_oth, hidden, gain_f, gate_t, up_t, down_weight, wb
    )
    grad_tokens, got_b, got_a, gains = tail(
        low_own, low_oth, gain_a, gain_two, sums_b, n1_own, n1_oth, x_own, wa, qkv, att, lse, mem, grad_hidden
    )
    if lax.axis_size("r") > 1:
        got_b = lax.psum(got_b.astype(F32), "r")
        got_a = lax.psum(got_a.astype(F32), "r")
        gains = lax.psum(gains, "r")
    gg, gu, gd = place(place_b_body, got_b, ("tall", "tall", "tall"), "place_b")
    gq, gk, gv, go = place(place_a_body, got_a, ("col", "col", "col", "row"), "place_a")
    return output, grad_tokens, gq, gk, gv, go, gg.T, gu.T, gd, gains[0], gains[1]


def solution(mesh):
    n_dp, n_t = mesh.shape["dp"], mesh.shape["tensor"]
    fine = Mesh(mesh.devices.reshape(n_dp // 8, NQ, 2, n_t), ("r", "q", "c", "t"))
    dp = ("r", "q", "c")
    rows = P(None, dp + ("t",), None)
    placed = (
        rows, P(), P(), P(None, "t"), P(None, "t"), P(None, "t"), P("t", None), P(None, "t"), P(None, "t"),
        P("t", None), P(None, dp, "t"), P(None, dp, "t"), P(None, dp, "t", None), rows,
    )
    return jax.shard_map(
        per_device,
        mesh=fine,
        in_specs=placed,
        out_specs=(
            rows, rows, P(None, "t"), P(None, "t"), P(None, "t"), P("t", None), P(None, "t"), P(None, "t"),
            P("t", None), P(), P(),
        ),
        check_vma=False,
    )
```
